32 devices in a mesh: seq: 2 (over x), fsdp: 16 (over z, y, core).
Axes of the slice: x: 2, y: 2, z: 4, core: 2. Of those that a mesh axis runs over, the one named last changes fastest.
Arguments:
- tokens: bfloat16 [16, 1024, 1024], P('fsdp', 'seq'), may hold values from -6 to 6
- cotangent: bfloat16 [16, 1024, 1024], P('fsdp', 'seq'), may hold values from -6 to 6
- ffn1_up: float32 [1024, 4096], P('fsdp'), may hold values from -0.1875 to 0.1875
- ffn1_down: float32 [4096, 1024], P('fsdp'), may hold values from -0.09375 to 0.09375
- qkv_weight: float32 [1024, 3072], P('fsdp'), may hold values from -0.1875 to 0.1875
- out_weight: float32 [1024, 1024], P('fsdp'), may hold values from -3 to 3
- conv_in: float32 [1024, 2048], P('fsdp'), may hold values from -0.1875 to 0.1875
- conv_out: float32 [1024, 1024], P('fsdp'), may hold values from -0.1875 to 0.1875
- ffn2_up: float32 [1024, 4096], P('fsdp'), may hold values from -0.1875 to 0.1875
- ffn2_down: float32 [4096, 1024], P('fsdp'), may hold values from -0.09375 to 0.09375
- norm_gains: float32 [6, 1024], replicated, may hold values from 0.5 to 1.5
- norm_biases: float32 [6, 1024], replicated, may hold values from -1 to 1
- hidden_biases: float32 [2, 4096], replicated, may hold values from -1.5 to 1.5
- model_biases: float32 [5, 1024], replicated, may hold values from -1.5 to 1.5
- dw_kernel: float32 [31, 1024], replicated, may hold values from -1 to 1
- rel_table: float32 [73, 64], replicated, may hold values from -6 to 6
Outputs:
- output: bfloat16 [16, 1024, 1024], P('fsdp', 'seq')
- input_grad: bfloat16 [16, 1024, 1024], P('fsdp', 'seq')
- ffn1_up_grad: float32 [1024, 4096], P('fsdp', 'seq')
- ffn1_down_grad: float32 [4096, 1024], P('fsdp', 'seq')
- qkv_grad: float32 [1024, 3072], P('fsdp', 'seq')
- out_grad: float32 [1024, 1024], P('fsdp', 'seq')
- conv_in_grad: float32 [1024, 2048], P('fsdp', 'seq')
- conv_out_grad: float32 [1024, 1024], P('fsdp', 'seq')
- ffn2_up_grad: float32 [1024, 4096], P('fsdp', 'seq')
- ffn2_down_grad: float32 [4096, 1024], P('fsdp', 'seq')
- gains_grad: float32 [6, 1024], replicated
- norm_biases_grad: float32 [3, 1024], replicated
- later_biases_grad: float32 [3, 1024], replicated
- hidden_biases_grad: float32 [2, 4096], replicated
- model_biases_grad: float32 [3, 1024], replicated
- output_biases_grad: float32 [2, 1024], replicated
- kernel_grad: float32 [31, 1024], replicated
- table_grad: float32 [73, 64], replicated
The draws below stay inside these ranges and needn't reach their ends.
All inputs are finite; a program needn't handle non-finite values.
Results may differ from the reference program's by a relative error of at most 0.02.
Values may be sent and summed in bfloat16 or wider, within the bound.
A program may use at most 256 MiB of HBM per device.

```python
import jax
import jax.numpy as jnp
from jax import lax

D = 1024
FF = 4096
HEADS = 16
HEAD = 64
KERNEL = 31
LEFT = 64
RIGHT = 8
BUCKETS = 73
LEN = 1024
CLIPS = 16


def shard_levels(own_key, shape, shards, low, high):
    def one(dim, parts):
        heights = jax.random.uniform(jax.random.fold_in(jax.random.fold_in(own_key, 6), dim), (parts,), jnp.float32, low / len(shards), high / len(shards))
        return jnp.repeat(jnp.exp(heights), shape[dim] // parts).reshape((-1,) + (1,) * (len(shape) - dim - 1))

    level = one(*shards[0])
    for cut in shards[1:]:
        level = level * one(*cut)
    return level


def noise(own_key, dims, deviation, most, split=(), held_as=jnp.bfloat16):
    values = deviation * jax.random.normal(own_key, dims, jnp.float32)
    if split:
        values = values * shard_levels(own_key, dims, split, -0.22, 0.18)
    return jnp.clip(values, -most, most).astype(held_as)


def setup_inputs(seed: int = 0) -> dict:
    keys = jax.random.split(jax.random.key(seed), 17)
    tokens = noise(keys[0], (CLIPS, LEN, D), 1.0, 6.0, ((0, 16), (1, 2)))
    cotangent = noise(keys[1], (CLIPS, LEN, D), 1.0, 6.0, ((0, 16), (1, 2)))
    ffn1_up = noise(keys[2], (D, FF), D ** -0.5, 0.1875, ((0, 16),), jnp.float32)
    ffn1_down = noise(keys[3], (FF, D), FF ** -0.5, 0.09375, ((0, 16),), jnp.float32)
    qkv_weight = noise(keys[4], (D, 3 * D), D ** -0.5, 0.1875, ((0, 16),), jnp.float32)
    out_weight = noise(keys[5], (D, D), (max(1, D // 256)) ** -0.5, 3.0, ((0, 16),), jnp.float32)
    conv_in = noise(keys[6], (D, 2 * D), D ** -0.5, 0.1875, ((0, 16),), jnp.float32)
    conv_out = noise(keys[7], (D, D), D ** -0.5, 0.1875, ((0, 16),), jnp.float32)
    ffn2_up = noise(keys[8], (D, FF), D ** -0.5, 0.1875, ((0, 16),), jnp.float32)
    ffn2_down = noise(keys[9], (FF, D), FF ** -0.5, 0.09375, ((0, 16),), jnp.float32)
    norm_gains = jnp.clip(1.0 + 0.1 * jax.random.normal(keys[10], (6, D), jnp.float32), 0.5, 1.5)
    norm_biases = noise(keys[11], (6, D), 0.2, 1.0, (), jnp.float32)
    hidden_biases = noise(keys[12], (2, FF), 0.3, 1.5, (), jnp.float32)
    model_biases = noise(keys[13], (5, D), 0.3, 1.5, (), jnp.float32)
    dw_kernel = noise(keys[14], (KERNEL, D), KERNEL ** -0.5, 1.0, (), jnp.float32)
    rel_table = noise(keys[15], (BUCKETS, HEAD), 1.0, 6.0, (), jnp.float32)
    return dict(tokens=tokens, cotangent=cotangent, ffn1_up=ffn1_up, ffn1_down=ffn1_down, qkv_weight=qkv_weight, out_weight=out_weight, conv_in=conv_in, conv_out=conv_out, ffn2_up=ffn2_up, ffn2_down=ffn2_down, norm_gains=norm_gains, norm_biases=norm_biases, hidden_biases=hidden_biases, model_biases=model_biases, dw_kernel=dw_kernel, rel_table=rel_table)


EPSILON = 1e-05

@jax.custom_vjp
def low(v):
    return lax.optimization_barrier(v.astype(jnp.bfloat16)).astype(jnp.float32)

@jax.custom_vjp
def low_back(v):
    return v

def low_keep(v):
    return (low(v), None)

def low_pass(kept, grad):
    return (grad,)

def back_keep(v):
    return (v, None)

def back_low(kept, grad):
    return (low(grad),)
low.defvjp(low_keep, low_pass)
low_back.defvjp(back_keep, back_low)

def matmul(former, latter):
    return jnp.dot(former, latter, precision=lax.Precision.HIGHEST)

def layer_norm(values, norm_gain, norm_shift):
    center = values - lax.optimization_barrier(jnp.mean(values, axis=-1, keepdims=True))
    spread = lax.optimization_barrier(jnp.mean(center * center, axis=-1, keepdims=True))
    return center * lax.rsqrt(spread + EPSILON) * norm_gain + norm_shift

def both_round(values):
    return low(low_back(values))

def feed_forward(values, norm_gain, norm_shift, weight_up, bias_up, weight_down, bias_down):
    normed = low(layer_norm(values, norm_gain, norm_shift))
    hidden = low_back(matmul(normed, low(weight_up)) + bias_up)
    active = low(jax.nn.silu(hidden))
    return low_back(matmul(active, low(weight_down)) + bias_down)

def bucket_index(length):
    places = jnp.arange(length, dtype=jnp.int32)
    return (jnp.clip(places[None, :] - places[:, None], -LEFT, RIGHT) + LEFT).astype(jnp.int32)

def attention(values, norm_gain, norm_shift, qkv_weight, out_weight, query_bias, value_bias, out_bias, rel_table):
    length = values.shape[0]
    model_width = values.shape[1]
    normed = low(layer_norm(values, norm_gain, norm_shift))
    projected = matmul(normed, low(qkv_weight))
    queries = both_round(projected[:, :model_width] + query_bias)
    keys_all = both_round(projected[:, model_width:2 * model_width])
    values_all = both_round(projected[:, 2 * model_width:] + value_bias)

    def to_heads(array):
        return array.reshape(length, HEADS, HEAD).transpose(1, 0, 2)
    rel_low = low(rel_table)
    buckets = bucket_index(length)
    score_scale = HEAD ** (-0.5)

    def one_head(operands):
        query_head, key_head, value_head = operands
        direct = matmul(query_head, key_head.T)
        position = matmul(query_head, rel_low.T)
        scores = low_back((direct + jnp.take_along_axis(position, buckets, axis=1)) * score_scale)
        highest = lax.optimization_barrier(jnp.max(scores, axis=-1, keepdims=True))
        weights_exp = jnp.exp(scores - highest)
        weights_soft = weights_exp / lax.optimization_barrier(jnp.sum(weights_exp, axis=-1, keepdims=True))
        return both_round(matmul(low(weights_soft), value_head))
    head_outputs = lax.map(jax.checkpoint(one_head), (to_heads(queries), to_heads(keys_all), to_heads(values_all)))
    merged = head_outputs.transpose(1, 0, 2).reshape(length, model_width)
    return low_back(matmul(merged, low(out_weight)) + out_bias)

def convolution(values, gain_first, shift_first, gain_second, shift_second, conv_in, conv_out, kernel_weights):
    length = values.shape[0]
    model_width = values.shape[1]
    normed = low(layer_norm(values, gain_first, shift_first))
    gate_input = low_back(matmul(normed, low(conv_in)))
    glu_out = low(gate_input[:, :model_width] * jax.nn.sigmoid(gate_input[:, model_width:]))
    padded = jnp.pad(glu_out, ((KERNEL - 1, 0), (0, 0)))
    mixed_rows = padded[0:length] * kernel_weights[0]
    for offset in range(1, KERNEL):
        mixed_rows = mixed_rows + padded[offset:offset + length] * kernel_weights[offset]
    mixed_rows = low_back(mixed_rows)
    swished = low(jax.nn.silu(layer_norm(mixed_rows, gain_second, shift_second)))
    return low_back(matmul(swished, low(conv_out)))

def forward(values, params):
    ffn1_up, ffn1_down, qkv_weight, out_weight, conv_in, conv_out, ffn2_up, ffn2_down, norm_gains, norm_biases, hidden_biases, model_biases, dw_kernel, rel_table = params
    after_one = values + 0.5 * feed_forward(values, norm_gains[0], norm_biases[0], ffn1_up, hidden_biases[0], ffn1_down, model_biases[0])
    after_two = after_one + attention(after_one, norm_gains[1], norm_biases[1], qkv_weight, out_weight, model_biases[1], model_biases[2], model_biases[3], rel_table)
    after_three = after_two + convolution(after_two, norm_gains[2], norm_biases[2], norm_gains[3], norm_biases[3], conv_in, conv_out, dw_kernel)
    after_four = after_three + 0.5 * feed_forward(after_three, norm_gains[4], norm_biases[4], ffn2_up, hidden_biases[1], ffn2_down, model_biases[4])
    return layer_norm(after_four, norm_gains[5], norm_biases[5])

def reference(tokens, cotangent, ffn1_up, ffn1_down, qkv_weight, out_weight, conv_in, conv_out, ffn2_up, ffn2_down, norm_gains, norm_biases, hidden_biases, model_biases, dw_kernel, rel_table):
    params = (ffn1_up, ffn1_down, qkv_weight, out_weight, conv_in, conv_out, ffn2_up, ffn2_down, norm_gains, norm_biases, hidden_biases, model_biases, dw_kernel, rel_table)

    def per_clip(totals, operands):
        clip_tokens, clip_cotangent = operands
        result, pullback = jax.vjp(forward, clip_tokens.astype(jnp.float32), params)
        input_part, param_parts = pullback(clip_cotangent.astype(jnp.float32))
        totals = jax.tree.map(lambda former, latter: former + latter, totals, param_parts)
        return (totals, (result.astype(jnp.bfloat16), input_part.astype(jnp.bfloat16)))
    initial = jax.tree.map(jnp.zeros_like, params)
    totals, (outputs, input_grads) = lax.scan(per_clip, initial, (tokens, cotangent))
    return (outputs, input_grads, totals[0], totals[1], totals[2], totals[3], totals[4], totals[5], totals[6], totals[7], totals[8], totals[9][0:3], totals[9][3:6], totals[10], totals[11][0:3], totals[11][3:5], totals[12], totals[13])
```

```python
from functools import partial

import jax
import jax.numpy as jnp
from jax import lax
from jax.experimental import pallas as pl
from jax.experimental.pallas import tpu as pltpu
from jax.sharding import PartitionSpec as P

HEAD = 64
KERNEL = 31
LEFT = 64
RIGHT = 8
BUCKETS = 73


EPSILON = 1e-05


def passed_along(value, axis, by):
    length = lax.axis_size(axis)
    pairs = [(i, i + by) for i in range(length) if 0 <= i + by < length]
    return lax.ppermute(value, axis, pairs)


def layer_norm(values, norm_gain, norm_shift):
    center = values - jnp.mean(values, axis=-1, keepdims=True)
    spread = jnp.mean(center * center, axis=-1, keepdims=True)
    return center * lax.rsqrt(spread + EPSILON) * norm_gain + norm_shift


def product(former, latter):
    return jnp.dot(former, latter, preferred_element_type=jnp.float32)


def contract_rows(former, latter):
    return lax.dot_general(
        former, latter, (((0,), (0,)), ((), ())), preferred_element_type=jnp.float32
    )


def times_transposed(former, latter):
    return lax.dot_general(
        former, latter, (((1,), (1,)), ((), ())), preferred_element_type=jnp.float32
    )


def glu_function(gate_input):
    half_width = gate_input.shape[1] // 2
    return gate_input[:, :half_width] * jax.nn.sigmoid(gate_input[:, half_width:])


def conv_tail(mixed_rows, norm_gain, norm_shift):
    return jax.nn.silu(layer_norm(mixed_rows, norm_gain, norm_shift))


def depthwise(wide_rows, kernel_now):
    return lax.conv_general_dilated(
        wide_rows,
        kernel_now[:, None, :],
        (1,),
        "VALID",
        dimension_numbers=("NWC", "WIO", "NWC"),
        feature_group_count=wide_rows.shape[2],
        precision=lax.Precision.HIGHEST,
    )


PAIR = 2
LANES = 128
FWD_ROWS = 256
BACK_ROWS = 256


def nt(former, latter):
    return lax.dot_general(former, latter, (((1,), (1,)), ((), ())), preferred_element_type=jnp.float32)


def nn(former, latter):
    return lax.dot_general(former, latter, (((1,), (0,)), ((), ())), preferred_element_type=jnp.float32)


def window_of(start, rows, length):
    low, high = start - LANES, start + rows + LANES
    return max(low, 0), min(high, length), max(low, 0) - low


def window_buckets(rows):
    width = rows + 2 * LANES
    places = lax.broadcasted_iota(jnp.int32, (rows, width), 1)
    lines = lax.broadcasted_iota(jnp.int32, (rows, width), 0)
    return places - lines - (LANES - LEFT)


def biased_scores(scores, position, start, rows, length):
    width = rows + 2 * LANES
    low, high, skip = window_of(start, rows, length)
    wide = jnp.concatenate([position, jnp.zeros((rows, width - LANES), jnp.float32)], axis=1)
    band = pltpu.roll(wide, LANES - LEFT, 1, stride=1, stride_axis=0)
    first, last = position[:, 0:1], position[:, BUCKETS - 1 : BUCKETS]
    bucket = window_buckets(rows)
    band = jnp.where(bucket <= 0, first, jnp.where(bucket >= BUCKETS - 1, last, band))
    pieces = []
    if low > 0:
        pieces.append(scores[:, :low] + first)
    pieces.append(scores[:, low:high] + band[:, skip : skip + high - low])
    if high < length:
        pieces.append(scores[:, high:] + last)
    return pieces[0] if len(pieces) == 1 else jnp.concatenate(pieces, axis=1)


def bucket_sums(score_grad, mirror, start, rows, length):
    width = rows + 2 * LANES
    low, high, skip = window_of(start, rows, length)
    inner = score_grad[:, low:high]
    pieces = []
    if skip > 0:
        pieces.append(jnp.zeros((rows, skip), jnp.float32))
    pieces.append(inner)
    if skip + high - low < width:
        pieces.append(jnp.zeros((rows, width - skip - high + low), jnp.float32))
    wide = pieces[0] if len(pieces) == 1 else jnp.concatenate(pieces, axis=1)
    bucket = window_buckets(rows)
    first = jnp.sum(jnp.where(bucket <= 0, wide, 0.0), axis=1, keepdims=True)
    last = jnp.sum(jnp.where(bucket >= BUCKETS - 1, wide, 0.0), axis=1, keepdims=True)
    if low > 0:
        first = first + jnp.sum(score_grad[:, :low], axis=1, keepdims=True)
    if high < length:
        last = last + jnp.sum(score_grad[:, high:], axis=1, keepdims=True)
    turned = nn(wide.astype(jnp.bfloat16), mirror)
    band = pltpu.roll(turned, (LANES + LANES - LEFT) % width, 1, stride=1, stride_axis=0)[:, :LANES]
    bucket = LANES - 1 - lax.broadcasted_iota(jnp.int32, (rows, LANES), 1)
    return jnp.where(bucket == 0, first, jnp.where(bucket == BUCKETS - 1, last, jnp.where(bucket < BUCKETS, band, 0.0)))


def mirror_of(width):
    lines = lax.broadcasted_iota(jnp.int32, (width, width), 0)
    places = lax.broadcasted_iota(jnp.int32, (width, width), 1)
    return jnp.where(lines + places == width - 1, 1.0, 0.0).astype(jnp.bfloat16)


def attend_kernel(q_ref, k_ref, v_ref, rel_ref, out_ref, log_ref):
    length = q_ref.shape[1]
    rows = min(FWD_ROWS, length)
    scale = HEAD ** (-0.5)
    rel = rel_ref[...]
    for start in range(0, length, rows):
        outs, logs = [], []
        for h in range(PAIR):
            lanes = slice(h * HEAD, (h + 1) * HEAD)
            query = q_ref[0, start : start + rows, lanes] * scale
            scores = nt(query, k_ref[0, :, lanes])
            scores = biased_scores(scores, nt(query, rel), start, rows, length)
            highest = jnp.max(scores, axis=1, keepdims=True)
            weights = jnp.exp(scores - highest)
            total = jnp.sum(weights, axis=1, keepdims=True)
            outs.append(nn(weights.astype(jnp.bfloat16), v_ref[0, :, lanes]) / total)
            logs.append(highest + jnp.log(total))
        out_ref[0, start : start + rows, :] = jnp.concatenate(outs, axis=1).astype(jnp.bfloat16)
        log_ref[0, 0, start : start + rows, :] = jnp.concatenate(logs, axis=1)


def attend_back_kernel(q_ref, k_ref, v_ref, do_ref, log_ref, rel_ref, back_ref, mirror_ref, dq_ref, dk_ref, dv_ref, table_ref, dkt, dvt):
    length = q_ref.shape[1]
    rows = min(BACK_ROWS, length)
    scale = HEAD ** (-0.5)
    rel = rel_ref[...]
    q_turned = (jnp.transpose(q_ref[0].astype(jnp.float32)) * scale).astype(jnp.bfloat16)
    do_turned = jnp.transpose(do_ref[0].astype(jnp.float32)).astype(jnp.bfloat16)
    back = back_ref[...]
    table = jnp.zeros((HEAD, LANES), jnp.float32)
    for start in range(0, length, rows):
        span = slice(start, start + rows)
        parts = []
        for h in range(PAIR):
            lanes = slice(h * HEAD, (h + 1) * HEAD)
            query = q_ref[0, span, lanes] * scale
            scores = nt(query, k_ref[0, :, lanes])
            scores = biased_scores(scores, nt(query, rel), start, rows, length)
            weights = jnp.exp(scores - log_ref[0, 0, span, h : h + 1])
            low_weights = weights.astype(jnp.bfloat16)
            grads = nt(do_ref[0, span, lanes], v_ref[0, :, lanes])
            both = weights * grads
            delta = jnp.sum(both, axis=1, keepdims=True)
            score_grad = (both - weights * delta).astype(jnp.bfloat16)
            value_part = nn(do_turned[lanes, span], low_weights)
            key_part = nn(q_turned[lanes, span], score_grad)
            if start == 0:
                dvt[lanes, :] = value_part
                dkt[lanes, :] = key_part
            else:
                dvt[lanes, :] += value_part
                dkt[lanes, :] += key_part
            bucket = bucket_sums(score_grad.astype(jnp.float32), mirror_ref[...], start, rows, length)
            high = bucket.astype(jnp.bfloat16)
            rest = (bucket - high.astype(jnp.float32)).astype(jnp.bfloat16)
            parts.append((nn(score_grad, k_ref[0, :, lanes]) + nn(high, back) + nn(rest, back)) * scale)
            table = table + nn(q_turned[lanes, span], high) + nn(q_turned[lanes, span], rest)
        dq_ref[0, span, :] = jnp.concatenate(parts, axis=1).astype(jnp.bfloat16)
    dk_ref[0] = jnp.transpose(dkt[...]).astype(jnp.bfloat16)
    dv_ref[0] = jnp.transpose(dvt[...]).astype(jnp.bfloat16)
    table_ref[0, 0] = table


def width_of(length):
    return min(BACK_ROWS, length) + 2 * LANES


def head_block(length):
    return pl.BlockSpec((1, length, PAIR * HEAD), lambda i, j: (i, 0, j))


def padded_table(rel_table):
    return jnp.pad(rel_table.astype(jnp.bfloat16), ((0, LANES - BUCKETS), (0, 0)))


def attend(query, key, value, rel_low):
    clips, length, width = query.shape
    pairs = width // (PAIR * HEAD)
    block = head_block(length)
    return pl.pallas_call(
        attend_kernel,
        grid=(clips, pairs),
        in_specs=[block, block, block, pl.BlockSpec((LANES, HEAD), lambda i, j: (0, 0))],
        out_specs=[block, pl.BlockSpec((1, 1, length, PAIR), lambda i, j: (i, j, 0, 0))],
        out_shape=[
            jax.ShapeDtypeStruct(query.shape, jnp.bfloat16),
            jax.ShapeDtypeStruct((clips, pairs, length, PAIR), jnp.float32),
        ],
        compiler_params=pltpu.CompilerParams(vmem_limit_bytes=48 << 20),
        cost_estimate=pl.CostEstimate(flops=4 * clips * width * length * length * 4, bytes_accessed=8 * query.size, transcendentals=clips * pairs * PAIR * length * length),
        name="attend",
    )(query, key, value, rel_low)


def attend_back(query, key, value, out_grad, logs, rel_low):
    clips, length, width = query.shape
    pairs = width // (PAIR * HEAD)
    block = head_block(length)
    shape = jax.ShapeDtypeStruct(query.shape, jnp.bfloat16)
    return pl.pallas_call(
        attend_back_kernel,
        grid=(clips, pairs),
        in_specs=[
            block, block, block, block,
            pl.BlockSpec((1, 1, length, PAIR), lambda i, j: (i, j, 0, 0)),
            pl.BlockSpec((LANES, HEAD), lambda i, j: (0, 0)),
            pl.BlockSpec((LANES, HEAD), lambda i, j: (0, 0)),
            pl.BlockSpec((width_of(length),) * 2, lambda i, j: (0, 0)),
        ],
        out_specs=[block, block, block, pl.BlockSpec((1, 1, HEAD, LANES), lambda i, j: (i, j, 0, 0))],
        out_shape=[shape, shape, shape, jax.ShapeDtypeStruct((clips, pairs, HEAD, LANES), jnp.float32)],
        scratch_shapes=[pltpu.VMEM((PAIR * HEAD, length), jnp.float32)] * 2,
        compiler_params=pltpu.CompilerParams(vmem_limit_bytes=48 << 20),
        cost_estimate=pl.CostEstimate(flops=10 * clips * width * length * length * 4, bytes_accessed=14 * query.size, transcendentals=clips * pairs * PAIR * length * length),
        name="attend_back",
    )(query, key, value, out_grad, logs, rel_low, rel_low[::-1], mirror_of(width_of(length)))


def feed_forward(values, norm_gain, norm_shift, weight_up, bias_up, weight_down, bias_down):
    normed = layer_norm(values, norm_gain, norm_shift).astype(jnp.bfloat16)
    hidden = product(normed, weight_up) + bias_up
    active = jax.nn.silu(hidden).astype(jnp.bfloat16)
    branch = product(active, weight_down) + bias_down
    return (branch, (normed, hidden, active))


def feed_backward(residual_grad, values, kept_parts, norm_gain, norm_shift, weight_up, weight_down):
    normed, hidden, active = kept_parts
    branch_grad = (0.5 * residual_grad).astype(jnp.bfloat16)
    down_grad = contract_rows(active, branch_grad)
    down_bias_grad = jnp.sum(branch_grad.astype(jnp.float32), axis=0)
    active_grad = times_transposed(branch_grad, weight_down)
    silu_pull = jax.vjp(jax.nn.silu, hidden)[1]
    hidden_grad = silu_pull(active_grad)[0].astype(jnp.bfloat16)
    up_grad = contract_rows(normed, hidden_grad)
    up_bias_grad = jnp.sum(hidden_grad.astype(jnp.float32), axis=0)
    normed_grad = times_transposed(hidden_grad, weight_up)
    norm_pull = jax.vjp(layer_norm, values, norm_gain, norm_shift)[1]
    values_grad, gain_grad, shift_grad = norm_pull(normed_grad)
    return (
        residual_grad + values_grad,
        up_grad,
        up_bias_grad,
        down_grad,
        down_bias_grad,
        gain_grad,
        shift_grad,
    )


def body(
    tokens,
    cotangent,
    ffn1_up,
    ffn1_down,
    qkv_weight,
    out_weight,
    conv_in,
    conv_out,
    ffn2_up,
    ffn2_down,
    norm_gains,
    norm_biases,
    hidden_biases,
    model_biases,
    dw_kernel,
    rel_table,
):
    clip_count, segment, model_width = tokens.shape
    row_count = clip_count * segment
    rim_width = KERNEL - 1
    up_one, down_one, qkv_full, out_full, conv_first, conv_second, up_two, down_two = (
        lax.all_gather(ffn1_up.astype(jnp.bfloat16), "fsdp", axis=0, tiled=True),
        lax.all_gather(ffn1_down.astype(jnp.bfloat16), "fsdp", axis=0, tiled=True),
        lax.all_gather(qkv_weight.astype(jnp.bfloat16), "fsdp", axis=0, tiled=True),
        lax.all_gather(out_weight.astype(jnp.bfloat16), "fsdp", axis=0, tiled=True),
        lax.all_gather(conv_in.astype(jnp.bfloat16), "fsdp", axis=0, tiled=True),
        lax.all_gather(conv_out.astype(jnp.bfloat16), "fsdp", axis=0, tiled=True),
        lax.all_gather(ffn2_up.astype(jnp.bfloat16), "fsdp", axis=0, tiled=True),
        lax.all_gather(ffn2_down.astype(jnp.bfloat16), "fsdp", axis=0, tiled=True),
    )
    input_rows = tokens.reshape(row_count, model_width).astype(jnp.float32)
    branch_one, kept_one = feed_forward(
        input_rows,
        norm_gains[0],
        norm_biases[0],
        up_one,
        hidden_biases[0],
        down_one,
        model_biases[0],
    )
    after_one = input_rows + 0.5 * branch_one
    normed_attn = layer_norm(after_one, norm_gains[1], norm_biases[1]).astype(jnp.bfloat16)
    projected = product(normed_attn, qkv_full)
    queries = (
        (projected[:, :model_width] + model_biases[1])
        .astype(jnp.bfloat16)
        .reshape(clip_count, segment, model_width)
    )
    keys_seq = (
        projected[:, model_width : 2 * model_width]
        .astype(jnp.bfloat16)
        .reshape(clip_count, segment, model_width)
    )
    values_seq = (
        (projected[:, 2 * model_width :] + model_biases[2])
        .astype(jnp.bfloat16)
        .reshape(clip_count, segment, model_width)
    )
    query_heads, key_heads, value_heads = (
        lax.all_to_all(queries, "seq", split_axis=2, concat_axis=1, tiled=True),
        lax.all_to_all(keys_seq, "seq", split_axis=2, concat_axis=1, tiled=True),
        lax.all_to_all(values_seq, "seq", split_axis=2, concat_axis=1, tiled=True),
    )
    rel_low = padded_table(rel_table)
    merged, log_totals = attend(query_heads, key_heads, value_heads, rel_low)
    attn_seq = lax.all_to_all(merged, "seq", split_axis=1, concat_axis=2, tiled=True)
    attn_rows = attn_seq.reshape(row_count, model_width)
    after_two = after_one + product(attn_rows, out_full) + model_biases[3]
    normed_conv = layer_norm(after_two, norm_gains[2], norm_biases[2]).astype(jnp.bfloat16)
    gate_input = product(normed_conv, conv_first)
    glu_out = (
        glu_function(gate_input).astype(jnp.bfloat16).reshape(clip_count, segment, model_width)
    )
    glu_before = passed_along(glu_out[:, segment - rim_width :], "seq", 1)
    glu_wide = jnp.concatenate([glu_before, glu_out], axis=1).astype(jnp.float32)
    mixed_rows, kernel_pull = jax.vjp(partial(depthwise, glu_wide), dw_kernel)
    mixed_flat = mixed_rows.reshape(row_count, model_width)
    swished = conv_tail(mixed_flat, norm_gains[3], norm_biases[3]).astype(jnp.bfloat16)
    after_three = after_two + product(swished, conv_second)
    branch_two, kept_two = feed_forward(
        after_three,
        norm_gains[4],
        norm_biases[4],
        up_two,
        hidden_biases[1],
        down_two,
        model_biases[4],
    )
    after_four = after_three + 0.5 * branch_two
    final_rows, final_pull = jax.vjp(layer_norm, after_four, norm_gains[5], norm_biases[5])
    output = final_rows.astype(jnp.bfloat16).reshape(clip_count, segment, model_width)
    grad_four, gain_five, shift_five = final_pull(
        cotangent.reshape(row_count, model_width).astype(jnp.float32)
    )
    grad_three, up_two_grad, up_two_bias, down_two_grad, down_two_bias, gain_four, shift_four = (
        feed_backward(
            grad_four, after_three, kept_two, norm_gains[4], norm_biases[4], up_two, down_two
        )
    )
    conv_grad = grad_three.astype(jnp.bfloat16)
    conv_second_grad = contract_rows(swished, conv_grad)
    swished_grad = times_transposed(conv_grad, conv_second)
    tail_pull = jax.vjp(conv_tail, mixed_flat, norm_gains[3], norm_biases[3])[1]
    mixed_grad, gain_three, shift_three = tail_pull(swished_grad)
    mixed_low = mixed_grad.astype(jnp.bfloat16).reshape(clip_count, segment, model_width)
    mixed_after = passed_along(mixed_low[:, 0:rim_width], "seq", -1)
    mixed_wide = jnp.concatenate([mixed_low, mixed_after], axis=1).astype(jnp.float32)
    glu_grad = depthwise(mixed_wide, dw_kernel[::-1])
    kernel_grad = kernel_pull(mixed_low.astype(jnp.float32))[0]
    glu_pull = jax.vjp(glu_function, gate_input)[1]
    gate_grad = glu_pull(glu_grad.reshape(row_count, model_width))[0].astype(jnp.bfloat16)
    conv_first_grad = contract_rows(normed_conv, gate_grad)
    conv_norm_pull = jax.vjp(layer_norm, after_two, norm_gains[2], norm_biases[2])[1]
    values_grad, gain_two, shift_two = conv_norm_pull(times_transposed(gate_grad, conv_first))
    grad_two = grad_three + values_grad
    attn_grad = grad_two.astype(jnp.bfloat16)
    out_grad = contract_rows(attn_rows, attn_grad)
    out_bias_grad = jnp.sum(attn_grad.astype(jnp.float32), axis=0)
    merged_grad = (
        times_transposed(attn_grad, out_full)
        .astype(jnp.bfloat16)
        .reshape(clip_count, segment, model_width)
    )
    merged_heads = lax.all_to_all(merged_grad, "seq", split_axis=2, concat_axis=1, tiled=True)
    query_back, key_back, value_back, table_parts = attend_back(
        query_heads, key_heads, value_heads, merged_heads, log_totals, rel_low
    )
    table_grad = jnp.sum(table_parts, axis=(0, 1)).T[::-1][:BUCKETS]
    query_seq_grad, key_seq_grad, value_seq_grad = (
        lax.all_to_all(
            query_back,
            "seq",
            split_axis=1,
            concat_axis=2,
            tiled=True,
        ),
        lax.all_to_all(
            key_back,
            "seq",
            split_axis=1,
            concat_axis=2,
            tiled=True,
        ),
        lax.all_to_all(
            value_back,
            "seq",
            split_axis=1,
            concat_axis=2,
            tiled=True,
        ),
    )
    projected_grad = jnp.concatenate(
        [query_seq_grad, key_seq_grad, value_seq_grad], axis=-1
    ).reshape(row_count, 3 * model_width)
    qkv_grad = contract_rows(normed_attn, projected_grad)
    query_bias_grad = jnp.sum(query_seq_grad.astype(jnp.float32), axis=(0, 1))
    value_bias_grad = jnp.sum(value_seq_grad.astype(jnp.float32), axis=(0, 1))
    attn_norm_pull = jax.vjp(layer_norm, after_one, norm_gains[1], norm_biases[1])[1]
    values_grad, gain_one, shift_one = attn_norm_pull(times_transposed(projected_grad, qkv_full))
    grad_one = grad_two + values_grad
    grad_zero, up_one_grad, up_one_bias, down_one_grad, down_one_bias, gain_zero, shift_zero = (
        feed_backward(
            grad_one, input_rows, kept_one, norm_gains[0], norm_biases[0], up_one, down_one
        )
    )
    input_grad = grad_zero.astype(jnp.bfloat16).reshape(clip_count, segment, model_width)
    partial_sums = (
        lax.psum_scatter(
            up_one_grad.astype(jnp.bfloat16), "seq", scatter_dimension=1, tiled=True
        ).astype(jnp.float32),
        lax.psum_scatter(
            down_one_grad.astype(jnp.bfloat16), "seq", scatter_dimension=1, tiled=True
        ).astype(jnp.float32),
        lax.psum_scatter(
            qkv_grad.astype(jnp.bfloat16), "seq", scatter_dimension=1, tiled=True
        ).astype(jnp.float32),
        lax.psum_scatter(
            out_grad.astype(jnp.bfloat16), "seq", scatter_dimension=1, tiled=True
        ).astype(jnp.float32),
        lax.psum_scatter(
            conv_first_grad.astype(jnp.bfloat16), "seq", scatter_dimension=1, tiled=True
        ).astype(jnp.float32),
        lax.psum_scatter(
            conv_second_grad.astype(jnp.bfloat16), "seq", scatter_dimension=1, tiled=True
        ).astype(jnp.float32),
        lax.psum_scatter(
            up_two_grad.astype(jnp.bfloat16), "seq", scatter_dimension=1, tiled=True
        ).astype(jnp.float32),
        lax.psum_scatter(
            down_two_grad.astype(jnp.bfloat16), "seq", scatter_dimension=1, tiled=True
        ).astype(jnp.float32),
    )
    reduced = (
        lax.psum_scatter(
            partial_sums[0].astype(jnp.bfloat16), "fsdp", scatter_dimension=0, tiled=True
        ).astype(jnp.float32),
        lax.psum_scatter(
            partial_sums[1].astype(jnp.bfloat16), "fsdp", scatter_dimension=0, tiled=True
        ).astype(jnp.float32),
        lax.psum_scatter(
            partial_sums[2].astype(jnp.bfloat16), "fsdp", scatter_dimension=0, tiled=True
        ).astype(jnp.float32),
        lax.psum_scatter(
            partial_sums[3].astype(jnp.bfloat16), "fsdp", scatter_dimension=0, tiled=True
        ).astype(jnp.float32),
        lax.psum_scatter(
            partial_sums[4].astype(jnp.bfloat16), "fsdp", scatter_dimension=0, tiled=True
        ).astype(jnp.float32),
        lax.psum_scatter(
            partial_sums[5].astype(jnp.bfloat16), "fsdp", scatter_dimension=0, tiled=True
        ).astype(jnp.float32),
        lax.psum_scatter(
            partial_sums[6].astype(jnp.bfloat16), "fsdp", scatter_dimension=0, tiled=True
        ).astype(jnp.float32),
        lax.psum_scatter(
            partial_sums[7].astype(jnp.bfloat16), "fsdp", scatter_dimension=0, tiled=True
        ).astype(jnp.float32),
    )
    gains_stack = jnp.stack([gain_zero, gain_one, gain_two, gain_three, gain_four, gain_five])
    shifts_stack = jnp.stack(
        [shift_zero, shift_one, shift_two, shift_three, shift_four, shift_five]
    )
    hidden_stack = jnp.stack([up_one_bias, up_two_bias])
    model_stack = jnp.stack(
        [down_one_bias, query_bias_grad, value_bias_grad, out_bias_grad, down_two_bias]
    )
    gains_sum, shifts_sum, hidden_sum, model_sum, kernel_sum, table_sum = lax.psum(
        (gains_stack, shifts_stack, hidden_stack, model_stack, kernel_grad, table_grad),
        ("seq", "fsdp"),
    )
    return (
        output,
        input_grad,
        reduced[0],
        reduced[1],
        reduced[2],
        reduced[3],
        reduced[4],
        reduced[5],
        reduced[6],
        reduced[7],
        gains_sum,
        shifts_sum[0:3],
        shifts_sum[3:6],
        hidden_sum,
        model_sum[0:3],
        model_sum[3:5],
        kernel_sum,
        table_sum,
    )


def solution(mesh):
    in_specs = (
        P("fsdp", "seq", None),
        P("fsdp", "seq", None),
        P("fsdp", None),
        P("fsdp", None),
        P("fsdp", None),
        P("fsdp", None),
        P("fsdp", None),
        P("fsdp", None),
        P("fsdp", None),
        P("fsdp", None),
        P(),
        P(),
        P(),
        P(),
        P(),
        P(),
    )
    out_specs = (
        P("fsdp", "seq", None),
        P("fsdp", "seq", None),
        P("fsdp", "seq"),
        P("fsdp", "seq"),
        P("fsdp", "seq"),
        P("fsdp", "seq"),
        P("fsdp", "seq"),
        P("fsdp", "seq"),
        P("fsdp", "seq"),
        P("fsdp", "seq"),
        P(),
        P(),
        P(),
        P(),
        P(),
        P(),
        P(),
        P(),
    )
    return jax.shard_map(body, mesh=mesh, in_specs=in_specs, out_specs=out_specs, check_vma=False)
```

```python
import functools
from functools import partial

import jax
import jax.numpy as jnp
from jax import lax
from jax.experimental import pallas as pl
from jax.experimental.pallas import tpu as pltpu
from jax.sharding import PartitionSpec as P

HEAD = 64
KERNEL = 31
LEFT = 64
RIGHT = 8
BUCKETS = 73


EPSILON = 1e-05


def passed_along(value, axis, by):
    length = lax.axis_size(axis)
    pairs = [(i, i + by) for i in range(length) if 0 <= i + by < length]
    return lax.ppermute(value, axis, pairs)


def layer_norm(values, norm_gain, norm_shift):
    center = values - jnp.mean(values, axis=-1, keepdims=True)
    spread = jnp.mean(center * center, axis=-1, keepdims=True)
    return center * lax.rsqrt(spread + EPSILON) * norm_gain + norm_shift


def product(former, latter):
    return jnp.dot(former, latter, preferred_element_type=jnp.float32)


def contract_rows(former, latter):
    return lax.dot_general(
        former, latter, (((0,), (0,)), ((), ())), preferred_element_type=jnp.float32
    )


def times_transposed(former, latter):
    return lax.dot_general(
        former, latter, (((1,), (1,)), ((), ())), preferred_element_type=jnp.float32
    )


def glu_function(gate_input):
    half_width = gate_input.shape[1] // 2
    return gate_input[:, :half_width] * jax.nn.sigmoid(gate_input[:, half_width:])


def conv_tail(mixed_rows, norm_gain, norm_shift):
    return jax.nn.silu(layer_norm(mixed_rows, norm_gain, norm_shift))


def depthwise(wide_rows, kernel_now):
    return lax.conv_general_dilated(
        wide_rows,
        kernel_now[:, None, :],
        (1,),
        "VALID",
        dimension_numbers=("NWC", "WIO", "NWC"),
        feature_group_count=wide_rows.shape[2],
        precision=lax.Precision.HIGHEST,
    )


MESH = pl.DeviceIdType.MESH
PIECE = 512


class Place:
    def __init__(self):
        self.x = lax.axis_index("seq")
        self.f = lax.axis_index("fsdp")
        self.c = lax.rem(self.f, 2)
        self.y = lax.rem(lax.div(self.f, 2), 2)
        self.z = lax.div(self.f, 4)

    def across(self):
        return (1 - self.x, self.f)

    def twin(self):
        return (self.x, self.f + 1 - 2 * self.c)

    def beside(self):
        return (self.x, self.f + 2 - 4 * self.y)

    def along(self, step):
        return (self.x, lax.rem(self.z + step, 4) * 4 + self.y * 2 + self.c)

    def greet(self):
        barrier = pltpu.get_barrier_semaphore()
        peers = [self.across(), self.twin(), self.beside()] + [self.along(s) for s in (1, 2, 3)]
        for peer in peers:
            pl.semaphore_signal(barrier, inc=1, device_id=peer, device_id_type=MESH)
        pl.semaphore_wait(barrier, len(peers))


def chunks_of(shapes, lines):
    found = []
    for index, (rows, width) in enumerate(shapes):
        for line in range(0, rows, lines):
            for column in range(0, width // 2, PIECE):
                found.append((index, line, column, len(found) % 3 != 2))
    return found


class Sent:
    def __init__(self, source, target, send_sem, recv_sem, device):
        self.parts = dict(src_ref=source, dst_ref=target, send_sem=send_sem, recv_sem=recv_sem, device_id=device, device_id_type=MESH)

    def start(self):
        pltpu.make_async_remote_copy(**self.parts).start()

    def wait_recv(self):
        pltpu.make_async_remote_copy(**self.parts).wait_recv()

    def wait_send(self):
        pltpu.make_async_remote_copy(**self.parts).wait_send()


def send(source, target, send_sem, recv_sem, device):
    copy = Sent(source, target, send_sem, recv_sem, device)
    copy.start()
    return copy


def gather_kernel(count, chunks, lines, *refs):
    shards, wholes = refs[:count], refs[count : 2 * count]
    own_sem, z_send, z_recv, y_send, y_recv, x_send, x_recv, c_send, c_recv = refs[2 * count :]
    me = Place()
    me.greet()
    live = {}

    def halves(chunk):
        index, line, column, early = chunk
        half = shards[index].shape[1] // 2
        if early:
            return [pl.ds(pl.multiple_of(me.x * half + column, PIECE), PIECE)]
        return [pl.ds(column, PIECE), pl.ds(half + column, PIECE)]

    def both(chunk):
        half = shards[chunk[0]].shape[1] // 2
        return [pl.ds(chunk[2], PIECE), pl.ds(half + chunk[2], PIECE)]

    def first(t):
        index, line, column, early = chunks[t]
        shard, whole = shards[index], wholes[index]
        rows = pl.ds(line, lines)
        live[t, "own"] = []
        for j, cols in enumerate(halves(chunks[t])):
            copy = pltpu.make_async_copy(shard.at[rows, cols], whole.at[me.z, me.y, me.c, rows, cols], own_sem.at[t, j])
            copy.start()
            live[t, "own"].append(copy)
        live[t, "z"] = [
            send(shard.at[rows, cols], whole.at[me.z, me.y, me.c, rows, cols], z_send.at[t, j, s - 1], z_recv.at[t, j, s - 1], me.along(s))
            for j, cols in enumerate(halves(chunks[t]))
            for s in (1, 2, 3)
        ]

    def second(t):
        index, line, column, early = chunks[t]
        whole, rows = wholes[index], pl.ds(line, lines)
        for copy in live[t, "own"]:
            copy.wait()
        for copy in live[t, "z"]:
            copy.wait_recv()
        live[t, "y"] = [
            send(whole.at[:, me.y, me.c, rows, cols], whole.at[:, me.y, me.c, rows, cols], y_send.at[t, j], y_recv.at[t, j], me.beside())
            for j, cols in enumerate(halves(chunks[t]))
        ]

    def third(t):
        index, line, column, early = chunks[t]
        whole, rows = wholes[index], pl.ds(line, lines)
        for copy in live[t, "y"]:
            copy.wait_recv()
        if early:
            (cols,) = halves(chunks[t])
            view = whole.at[:, :, me.c, rows, cols]
            live[t, "x"] = [send(view, view, x_send.at[t], x_recv.at[t], me.across())]
        else:
            live[t, "x"] = []

    def fourth(t):
        index, line, column, early = chunks[t]
        whole, rows = wholes[index], pl.ds(line, lines)
        for copy in live[t, "x"]:
            copy.wait_recv()
        live[t, "c"] = [
            send(whole.at[:, :, me.c, rows, cols], whole.at[:, :, me.c, rows, cols], c_send.at[t, j], c_recv.at[t, j], me.twin())
            for j, cols in enumerate(both(chunks[t]))
        ]

    total = len(chunks)
    for step in range(total + 3):
        for lag, phase in enumerate((first, second, third, fourth)):
            if 0 <= step - lag < total:
                phase(step - lag)
    for t in range(total):
        for copy in live[t, "c"]:
            copy.wait_recv()
        for kind in "zyxc":
            for copy in live[t, kind]:
                copy.wait_send()


def gather_whole(shards, identity):
    shapes = [shard.shape for shard in shards]
    lines = min(rows for rows, _ in shapes)
    chunks = chunks_of(shapes, lines)
    count, total = len(shards), len(chunks)
    dma = pltpu.SemaphoreType.DMA
    anywhere = pl.BlockSpec(memory_space=pl.ANY)
    wholes = pl.pallas_call(
        functools.partial(gather_kernel, count, chunks, lines),
        in_specs=[anywhere] * count,
        out_specs=[anywhere] * count,
        out_shape=[jax.ShapeDtypeStruct((4, 2, 2, *shape), jnp.bfloat16) for shape in shapes],
        scratch_shapes=[
            dma((total, 2)), dma((total, 2, 3)), dma((total, 2, 3)), dma((total, 2)), dma((total, 2)),
            dma((total,)), dma((total,)), dma((total, 2)), dma((total, 2)),
        ],
        compiler_params=pltpu.CompilerParams(collective_id=identity, has_side_effects=True, vmem_limit_bytes=4 << 20),
        name="gather_whole",
    )(*shards)
    return [whole.reshape(-1, whole.shape[-1]) for whole in wholes]


SLOTS = 6


def scatter_kernel(count, chunks, lines, *refs):
    grads, small, outs, small_out = refs[:count], refs[count], refs[count + 1 : 2 * count + 1], refs[2 * count + 1]
    (held, core_in, early_in, late_in, mid_in, end_in, done, load_sem, done_sem,
     c_send, c_recv, x_send, x_recv, y_send, y_recv, z_send, z_recv,
     small_held, small_in, small_z, small_send, small_recv, small_z_send, small_z_recv) = refs[2 * count + 2 :]
    me = Place()
    me.greet()
    live = {}
    order = [sum(other[3] == chunk[3] for other in chunks[:t]) for t, chunk in enumerate(chunks)]

    def columns(chunk, j):
        return pl.ds(j * (grads[chunk[0]].shape[-1] // 2) + chunk[2], PIECE)

    def sums(former, latter):
        return (former.astype(jnp.float32) + latter.astype(jnp.float32)).astype(jnp.bfloat16)

    def first(t):
        index, line, column, early = chunks[t]
        grad, rows, slot = grads[index], pl.ds(line, lines), t % SLOTS
        if t >= SLOTS:
            for kind in "zyx":
                for copy in live[t - SLOTS, kind]:
                    copy.wait_send()
        live[t, "c"], live[t, "load"] = [], []
        for j in range(2):
            cols = columns(chunks[t], j)
            live[t, "c"].append(send(grad.at[:, :, 1 - me.c, rows, cols], core_in.at[t, j], c_send.at[t, j], c_recv.at[t, j], me.twin()))
            load = pltpu.make_async_copy(grad.at[:, :, me.c, rows, cols], held.at[slot, j], load_sem.at[t, j])
            load.start()
            live[t, "load"].append(load)

    def second(t):
        early, slot = chunks[t][3], t % SLOTS
        for j in range(2):
            live[t, "load"][j].wait()
            live[t, "c"][j].wait_recv()
            for z in range(4):
                held[slot, j, z] = sums(held[slot, j, z], core_in[t, j, z])
        if early:
            live[t, "x"] = [send(held.at[slot, 1 - me.x], early_in.at[order[t]], x_send.at[t], x_recv.at[t], me.across())]
        else:
            live[t, "y"] = [send(held.at[slot, :, :, 1 - me.y], late_in.at[order[t]], y_send.at[t], y_recv.at[t], me.beside())]

    def third(t):
        early, slot = chunks[t][3], t % SLOTS
        if early:
            live[t, "x"][0].wait_recv()
            for z in range(4):
                held[slot, me.x, z] = sums(held[slot, me.x, z], early_in[order[t], z])
            live[t, "y"] = [send(held.at[slot, me.x, :, 1 - me.y], mid_in.at[t, 0], y_send.at[t], y_recv.at[t], me.beside())]
        else:
            live[t, "y"][0].wait_recv()
            for j in range(2):
                for z in range(4):
                    held[slot, j, z, me.y] = sums(held[slot, j, z, me.y], late_in[order[t], j, z])
            live[t, "z"] = [
                send(held.at[slot, :, lax.rem(me.z + s, 4), me.y], mid_in.at[t, s - 1, 0:2], z_send.at[t, s - 1], z_recv.at[t, s - 1], me.along(s))
                for s in (1, 2, 3)
            ]

    def fourth(t):
        early, slot = chunks[t][3], t % SLOTS
        if early:
            live[t, "y"][0].wait_recv()
            for z in range(4):
                held[slot, me.x, z, me.y] = sums(held[slot, me.x, z, me.y], mid_in[t, 0, z])
            live[t, "z"] = [
                send(held.at[slot, me.x, lax.rem(me.z + s, 4), me.y], end_in.at[t, s - 1], z_send.at[t, s - 1], z_recv.at[t, s - 1], me.along(s))
                for s in (1, 2, 3)
            ]
        else:
            for copy in live[t, "z"]:
                copy.wait_recv()
            for j in range(2):
                value = held[slot, j, me.z, me.y].astype(jnp.float32)
                for s in range(3):
                    value = value + mid_in[t, s, j].astype(jnp.float32)
                held[slot, j, me.z, me.y] = value.astype(jnp.bfloat16)
            live[t, "x"] = [send(held.at[slot, 1 - me.x, me.z, me.y], end_in.at[t, 0], x_send.at[t], x_recv.at[t], me.across())]

    def fifth(t):
        index, line, column, early = chunks[t]
        slot = t % SLOTS
        value = held[slot, me.x, me.z, me.y].astype(jnp.float32)
        if early:
            for copy in live[t, "z"]:
                copy.wait_recv()
            for s in range(3):
                value = value + end_in[t, s].astype(jnp.float32)
        else:
            live[t, "x"][0].wait_recv()
            value = value + end_in[t, 0].astype(jnp.float32)
        done[t] = value
        copy = pltpu.make_async_copy(done.at[t], outs[index].at[pl.ds(line, lines), pl.ds(column, PIECE)], done_sem.at[t])
        copy.start()
        live[t, "done"] = [copy]

    def small_step(stage):
        if stage > 0:
            live["small", stage - 1].wait_recv()
            small_held[stage] = small_held[stage - 1] + small_in[stage - 1]
        if stage < 3:
            peer = (me.twin, me.across, me.beside)[stage]()
            live["small", stage] = send(small_held.at[stage], small_in.at[stage], small_send.at[stage], small_recv.at[stage], peer)
        else:
            small_z[me.z] = small_held[3]
            for s in (1, 2, 3):
                live["small z", s] = send(small_held.at[3], small_z.at[me.z], small_z_send.at[s - 1], small_z_recv.at[s - 1], me.along(s))

    def small_end():
        for s in (1, 2, 3):
            live["small z", s].wait_recv()
            live["small z", s].wait_send()
            live["small", s - 1].wait_send()
        small_out[...] = (small_z[0] + small_z[1]) + (small_z[2] + small_z[3])

    total = len(chunks)
    small_held[0] = small[...]
    for step in range(total + 4):
        if step < 4:
            small_step(step)
        for lag, phase in enumerate((first, second, third, fourth, fifth)):
            if 0 <= step - lag < total:
                phase(step - lag)
    small_end()
    for t in range(total):
        live[t, "done"][0].wait()
        for copy in live[t, "c"]:
            copy.wait_send()
        if t + SLOTS >= total:
            for kind in "zyx":
                for copy in live[t, kind]:
                    copy.wait_send()


def scatter_sums(grads, small, identity):
    shapes = [(grad.shape[0] // 16, grad.shape[1]) for grad in grads]
    lines = min(rows for rows, _ in shapes)
    chunks = chunks_of(shapes, lines)
    count, total = len(grads), len(chunks)
    dma = pltpu.SemaphoreType.DMA
    anywhere = pl.BlockSpec(memory_space=pl.ANY)
    low = jnp.bfloat16
    early_count = sum(chunk[3] for chunk in chunks)
    return pl.pallas_call(
        functools.partial(scatter_kernel, count, chunks, lines),
        in_specs=[anywhere] * count + [pl.BlockSpec(memory_space=pltpu.VMEM)],
        out_specs=[anywhere] * count + [pl.BlockSpec(memory_space=pltpu.VMEM)],
        out_shape=[jax.ShapeDtypeStruct((rows, width // 2), jnp.float32) for rows, width in shapes]
        + [jax.ShapeDtypeStruct(small.shape, jnp.float32)],
        scratch_shapes=[
            pltpu.VMEM((SLOTS, 2, 4, 2, lines, PIECE), low),
            pltpu.VMEM((total, 2, 4, 2, lines, PIECE), low),
            pltpu.VMEM((max(1, early_count), 4, 2, lines, PIECE), low),
            pltpu.VMEM((max(1, total - early_count), 2, 4, lines, PIECE), low),
            pltpu.VMEM((total, 3, 4, lines, PIECE), low),
            pltpu.VMEM((total, 3, lines, PIECE), low),
            pltpu.VMEM((total, lines, PIECE), jnp.float32),
            dma((total, 2)), dma((total,)),
            dma((total, 2)), dma((total, 2)), dma((total,)), dma((total,)),
            dma((total,)), dma((total,)), dma((total, 3)), dma((total, 3)),
            pltpu.VMEM((4, *small.shape), jnp.float32), pltpu.VMEM((3, *small.shape), jnp.float32), pltpu.VMEM((4, *small.shape), jnp.float32),
            dma((3,)), dma((3,)), dma((3,)), dma((3,)),
        ],
        compiler_params=pltpu.CompilerParams(collective_id=identity, has_side_effects=True, vmem_limit_bytes=60 << 20),
        name="scatter_sums",
    )(*[grad.reshape(4, 2, 2, *shape) for grad, shape in zip(grads, shapes)], small)


PAIR = 2
LANES = 128
FWD_ROWS = 256
BACK_ROWS = 256


def nt(former, latter):
    return lax.dot_general(former, latter, (((1,), (1,)), ((), ())), preferred_element_type=jnp.float32)


def nn(former, latter):
    return lax.dot_general(former, latter, (((1,), (0,)), ((), ())), preferred_element_type=jnp.float32)


def window_of(start, rows, length):
    low, high = start - LANES, start + rows + LANES
    return max(low, 0), min(high, length), max(low, 0) - low


def window_buckets(rows):
    width = rows + 2 * LANES
    places = lax.broadcasted_iota(jnp.int32, (rows, width), 1)
    lines = lax.broadcasted_iota(jnp.int32, (rows, width), 0)
    return places - lines - (LANES - LEFT)


def biased_scores(scores, position, start, rows, length):
    width = rows + 2 * LANES
    low, high, skip = window_of(start, rows, length)
    wide = jnp.concatenate([position, jnp.zeros((rows, width - LANES), jnp.float32)], axis=1)
    band = pltpu.roll(wide, LANES - LEFT, 1, stride=1, stride_axis=0)
    first, last = position[:, 0:1], position[:, BUCKETS - 1 : BUCKETS]
    bucket = window_buckets(rows)
    band = jnp.where(bucket <= 0, first, jnp.where(bucket >= BUCKETS - 1, last, band))
    pieces = []
    if low > 0:
        pieces.append(scores[:, :low] + first)
    pieces.append(scores[:, low:high] + band[:, skip : skip + high - low])
    if high < length:
        pieces.append(scores[:, high:] + last)
    return pieces[0] if len(pieces) == 1 else jnp.concatenate(pieces, axis=1)


def bucket_sums(score_grad, mirror, start, rows, length):
    width = rows + 2 * LANES
    low, high, skip = window_of(start, rows, length)
    inner = score_grad[:, low:high]
    pieces = []
    if skip > 0:
        pieces.append(jnp.zeros((rows, skip), jnp.float32))
    pieces.append(inner)
    if skip + high - low < width:
        pieces.append(jnp.zeros((rows, width - skip - high + low), jnp.float32))
    wide = pieces[0] if len(pieces) == 1 else jnp.concatenate(pieces, axis=1)
    bucket = window_buckets(rows)
    first = jnp.sum(jnp.where(bucket <= 0, wide, 0.0), axis=1, keepdims=True)
    last = jnp.sum(jnp.where(bucket >= BUCKETS - 1, wide, 0.0), axis=1, keepdims=True)
    if low > 0:
        first = first + jnp.sum(score_grad[:, :low], axis=1, keepdims=True)
    if high < length:
        last = last + jnp.sum(score_grad[:, high:], axis=1, keepdims=True)
    turned = nn(wide.astype(jnp.bfloat16), mirror)
    band = pltpu.roll(turned, (LANES + LANES - LEFT) % width, 1, stride=1, stride_axis=0)[:, :LANES]
    bucket = LANES - 1 - lax.broadcasted_iota(jnp.int32, (rows, LANES), 1)
    return jnp.where(bucket == 0, first, jnp.where(bucket == BUCKETS - 1, last, jnp.where(bucket < BUCKETS, band, 0.0)))


def mirror_of(width):
    lines = lax.broadcasted_iota(jnp.int32, (width, width), 0)
    places = lax.broadcasted_iota(jnp.int32, (width, width), 1)
    return jnp.where(lines + places == width - 1, 1.0, 0.0).astype(jnp.bfloat16)


def attend_pair(q_ref, k_ref, v_ref, rel_ref, out_ref, log_ref):
    length = q_ref.shape[0]
    rows = min(FWD_ROWS, length)
    scale = HEAD ** (-0.5)
    rel = rel_ref[...]
    for start in range(0, length, rows):
        outs, logs = [], []
        for h in range(PAIR):
            lanes = slice(h * HEAD, (h + 1) * HEAD)
            query = q_ref[start : start + rows, lanes] * scale
            scores = nt(query, k_ref[:, lanes])
            scores = biased_scores(scores, nt(query, rel), start, rows, length)
            highest = jnp.max(scores, axis=1, keepdims=True)
            weights = jnp.exp(scores - highest)
            total = jnp.sum(weights, axis=1, keepdims=True)
            outs.append(nn(weights.astype(jnp.bfloat16), v_ref[:, lanes]) / total)
            logs.append(highest + jnp.log(total))
        out_ref[start : start + rows, :] = jnp.concatenate(outs, axis=1).astype(jnp.bfloat16)
        log_ref[start : start + rows, :] = jnp.concatenate(logs, axis=1)


def attend_back_pair(
    q_ref, k_ref, v_ref, do_ref, log_ref, rel_ref, back_ref, mirror_ref, dq_ref, dk_ref, dv_ref, table_ref, dkt, dvt
):
    length = q_ref.shape[0]
    rows = min(BACK_ROWS, length)
    scale = HEAD ** (-0.5)
    rel, back = rel_ref[...], back_ref[...]
    q_turned = (jnp.transpose(q_ref[...].astype(jnp.float32)) * scale).astype(jnp.bfloat16)
    do_turned = jnp.transpose(do_ref[...].astype(jnp.float32)).astype(jnp.bfloat16)
    table = jnp.zeros((HEAD, LANES), jnp.float32)
    for start in range(0, length, rows):
        span = slice(start, start + rows)
        parts = []
        for h in range(PAIR):
            lanes = slice(h * HEAD, (h + 1) * HEAD)
            query = q_ref[span, lanes] * scale
            scores = nt(query, k_ref[:, lanes])
            scores = biased_scores(scores, nt(query, rel), start, rows, length)
            weights = jnp.exp(scores - log_ref[span, h : h + 1])
            low_weights = weights.astype(jnp.bfloat16)
            grads = nt(do_ref[span, lanes], v_ref[:, lanes])
            both = weights * grads
            delta = jnp.sum(both, axis=1, keepdims=True)
            score_grad = (both - weights * delta).astype(jnp.bfloat16)
            value_part = nn(do_turned[lanes, span], low_weights)
            key_part = nn(q_turned[lanes, span], score_grad)
            if start == 0:
                dvt[lanes, :] = value_part
                dkt[lanes, :] = key_part
            else:
                dvt[lanes, :] += value_part
                dkt[lanes, :] += key_part
            bucket = bucket_sums(score_grad.astype(jnp.float32), mirror_ref[...], start, rows, length)
            high = bucket.astype(jnp.bfloat16)
            rest = (bucket - high.astype(jnp.float32)).astype(jnp.bfloat16)
            parts.append((nn(score_grad, k_ref[:, lanes]) + nn(high, back) + nn(rest, back)) * scale)
            table = table + nn(q_turned[lanes, span], high) + nn(q_turned[lanes, span], rest)
        dq_ref[span, :] = jnp.concatenate(parts, axis=1).astype(jnp.bfloat16)
    dk_ref[...] = jnp.transpose(dkt[...]).astype(jnp.bfloat16)
    dv_ref[...] = jnp.transpose(dvt[...]).astype(jnp.bfloat16)
    table_ref[...] = table


def attend_kernel(q_ref, k_ref, v_ref, rel_ref, out_ref, log_ref):
    attend_pair(q_ref.at[0], k_ref.at[0], v_ref.at[0], rel_ref, out_ref.at[0], log_ref.at[0, 0])


def attend_back_kernel(
    q_ref, k_ref, v_ref, do_ref, log_ref, rel_ref, back_ref, mirror_ref, dq_ref, dk_ref, dv_ref, table_ref, dkt, dvt
):
    attend_back_pair(
        q_ref.at[0], k_ref.at[0], v_ref.at[0], do_ref.at[0], log_ref.at[0, 0], rel_ref, back_ref, mirror_ref,
        dq_ref.at[0], dk_ref.at[0], dv_ref.at[0], table_ref.at[0, 0], dkt, dvt,
    )


def width_of(length):
    return min(BACK_ROWS, length) + 2 * LANES


def head_block(length):
    return pl.BlockSpec((1, length, PAIR * HEAD), lambda i, j: (i, 0, j))


def padded_table(rel_table):
    return jnp.pad(rel_table.astype(jnp.bfloat16), ((0, LANES - BUCKETS), (0, 0)))


def attend(query, key, value, rel_low):
    clips, length, width = query.shape
    pairs = width // (PAIR * HEAD)
    block = head_block(length)
    return pl.pallas_call(
        attend_kernel,
        grid=(clips, pairs),
        in_specs=[block, block, block, pl.BlockSpec((LANES, HEAD), lambda i, j: (0, 0))],
        out_specs=[block, pl.BlockSpec((1, 1, length, PAIR), lambda i, j: (i, j, 0, 0))],
        out_shape=[
            jax.ShapeDtypeStruct(query.shape, jnp.bfloat16),
            jax.ShapeDtypeStruct((clips, pairs, length, PAIR), jnp.float32),
        ],
        compiler_params=pltpu.CompilerParams(vmem_limit_bytes=48 << 20),
        cost_estimate=pl.CostEstimate(flops=4 * clips * width * length * length * 4, bytes_accessed=8 * query.size, transcendentals=clips * pairs * PAIR * length * length),
        name="attend",
    )(query, key, value, rel_low)


def attend_back(query, key, value, out_grad, logs, rel_low):
    clips, length, width = query.shape
    pairs = width // (PAIR * HEAD)
    block = head_block(length)
    shape = jax.ShapeDtypeStruct(query.shape, jnp.bfloat16)
    return pl.pallas_call(
        attend_back_kernel,
        grid=(clips, pairs),
        in_specs=[
            block, block, block, block,
            pl.BlockSpec((1, 1, length, PAIR), lambda i, j: (i, j, 0, 0)),
            pl.BlockSpec((LANES, HEAD), lambda i, j: (0, 0)),
            pl.BlockSpec((LANES, HEAD), lambda i, j: (0, 0)),
            pl.BlockSpec((width_of(length),) * 2, lambda i, j: (0, 0)),
        ],
        out_specs=[block, block, block, pl.BlockSpec((1, 1, HEAD, LANES), lambda i, j: (i, j, 0, 0))],
        out_shape=[shape, shape, shape, jax.ShapeDtypeStruct((clips, pairs, HEAD, LANES), jnp.float32)],
        scratch_shapes=[pltpu.VMEM((PAIR * HEAD, length), jnp.float32)] * 2,
        compiler_params=pltpu.CompilerParams(vmem_limit_bytes=48 << 20),
        cost_estimate=pl.CostEstimate(flops=10 * clips * width * length * length * 4, bytes_accessed=14 * query.size, transcendentals=clips * pairs * PAIR * length * length),
        name="attend_back",
    )(query, key, value, out_grad, logs, rel_low, rel_low[::-1], mirror_of(width_of(length)))


def strip(index):
    return pl.ds(pl.multiple_of(index * LANES, LANES), LANES)


def meet_across(me):
    barrier = pltpu.get_barrier_semaphore()
    pl.semaphore_signal(barrier, inc=1, device_id=me.across(), device_id_type=MESH)
    pl.semaphore_wait(barrier, 1)


def attend_split_kernel(
    pairs, p_ref, rel_ref, out_ref, kept_ref, log_ref, qkv, outs, own_sem, send_sem, recv_sem, kept_sem, out_sem, back_send, back_recv
):
    me = Place()
    step = pl.program_id(0)
    segment = p_ref.shape[0]
    mine, theirs = pl.ds(me.x * segment, segment), pl.ds((1 - me.x) * segment, segment)

    def leaving(i):
        return [
            Sent(p_ref.at[:, strip((2 * part + 1 - me.x) * pairs + i)], qkv.at[i, part, mine, :], send_sem.at[i, part], recv_sem.at[i, part], me.across())
            for part in range(3)
        ]

    def staying(i):
        return [
            pltpu.make_async_copy(p_ref.at[:, strip((2 * part + me.x) * pairs + i)], qkv.at[i, part, mine, :], own_sem.at[i, part])
            for part in range(3)
        ]

    def returns(i):
        there = out_ref.at[:, strip(me.x * pairs + i)]
        return (
            Sent(outs.at[i, theirs, :], there, back_send.at[i], back_recv.at[i], me.across()),
            pltpu.make_async_copy(outs.at[i, mine, :], there, out_sem.at[i]),
            pltpu.make_async_copy(qkv.at[i], kept_ref.at[i], kept_sem.at[i]),
        )

    @pl.when(step == 0)
    def _():
        meet_across(me)
        for i in range(pairs):
            for copy in leaving(i) + staying(i):
                copy.start()

    for copy in leaving(step):
        copy.wait_recv()
    for copy in staying(step):
        copy.wait()
    attend_pair(qkv.at[step, 0], qkv.at[step, 1], qkv.at[step, 2], rel_ref, outs.at[step], log_ref.at[0])
    for copy in returns(step):
        copy.start()

    @pl.when(step == pairs - 1)
    def _():
        for i in range(pairs):
            for copy in leaving(i):
                copy.wait_send()
            sent, kept, own = returns(i)
            sent.wait_send()
            sent.wait_recv()
            kept.wait()
            own.wait()


def attend_split(projected, rel_low, identity):
    segment, width = projected.shape[0], projected.shape[1] // 3
    length, pairs = 2 * segment, width // (2 * PAIR * HEAD)
    dma, anywhere = pltpu.SemaphoreType.DMA, pl.BlockSpec(memory_space=pl.ANY)
    return pl.pallas_call(
        functools.partial(attend_split_kernel, pairs),
        grid=(pairs,),
        in_specs=[anywhere, pl.BlockSpec((LANES, HEAD), lambda i: (0, 0))],
        out_specs=[anywhere, anywhere, pl.BlockSpec((1, length, PAIR), lambda i: (i, 0, 0))],
        out_shape=[
            jax.ShapeDtypeStruct((segment, width), jnp.bfloat16),
            jax.ShapeDtypeStruct((pairs, 3, length, LANES), jnp.bfloat16),
            jax.ShapeDtypeStruct((pairs, length, PAIR), jnp.float32),
        ],
        scratch_shapes=[
            pltpu.VMEM((pairs, 3, length, LANES), jnp.bfloat16),
            pltpu.VMEM((pairs, length, LANES), jnp.bfloat16),
            dma((pairs, 3)), dma((pairs, 3)), dma((pairs, 3)), dma((pairs,)), dma((pairs,)), dma((pairs,)), dma((pairs,)),
        ],
        compiler_params=pltpu.CompilerParams(collective_id=identity, has_side_effects=True, vmem_limit_bytes=48 << 20),
        name="attend_split",
    )(projected, rel_low)


def attend_back_split_kernel(
    pairs, do_ref, kept_ref, log_ref, rel_ref, back_ref, mirror_ref, dp_ref, table_ref,
    grads, qkv, outs, dkt, dvt, own_sem, send_sem, recv_sem, kept_sem, out_sem, back_send, back_recv
):
    me = Place()
    step = pl.program_id(0)
    segment = do_ref.shape[0]
    mine, theirs = pl.ds(me.x * segment, segment), pl.ds((1 - me.x) * segment, segment)

    def leaving(i):
        return Sent(do_ref.at[:, strip((1 - me.x) * pairs + i)], grads.at[i, mine, :], send_sem.at[i], recv_sem.at[i], me.across())

    def staying(i):
        return (
            pltpu.make_async_copy(do_ref.at[:, strip(me.x * pairs + i)], grads.at[i, mine, :], own_sem.at[i]),
            pltpu.make_async_copy(kept_ref.at[i], qkv.at[i], kept_sem.at[i]),
        )

    def returns(i, part):
        there = dp_ref.at[:, strip((2 * part + me.x) * pairs + i)]
        return (
            Sent(outs.at[i, part, theirs, :], there, back_send.at[i, part], back_recv.at[i, part], me.across()),
            pltpu.make_async_copy(outs.at[i, part, mine, :], there, out_sem.at[i, part]),
        )

    @pl.when(step == 0)
    def _():
        meet_across(me)
        for i in range(pairs):
            leaving(i).start()
            for copy in staying(i):
                copy.start()

    leaving(step).wait_recv()
    for copy in staying(step):
        copy.wait()
    attend_back_pair(
        qkv.at[step, 0], qkv.at[step, 1], qkv.at[step, 2], grads.at[step], log_ref.at[0], rel_ref, back_ref, mirror_ref,
        outs.at[step, 0], outs.at[step, 1], outs.at[step, 2], table_ref.at[0], dkt, dvt,
    )
    for part in range(3):
        for copy in returns(step, part):
            copy.start()

    @pl.when(step == pairs - 1)
    def _():
        for i in range(pairs):
            leaving(i).wait_send()
            for part in range(3):
                sent, own = returns(i, part)
                sent.wait_send()
                sent.wait_recv()
                own.wait()


def attend_back_split(out_grad, kept, logs, rel_low, identity):
    segment, width = out_grad.shape
    pairs, _, length, _ = kept.shape
    dma, anywhere = pltpu.SemaphoreType.DMA, pl.BlockSpec(memory_space=pl.ANY)
    table = pl.BlockSpec((LANES, HEAD), lambda i: (0, 0))
    return pl.pallas_call(
        functools.partial(attend_back_split_kernel, pairs),
        grid=(pairs,),
        in_specs=[
            anywhere, anywhere, pl.BlockSpec((1, length, PAIR), lambda i: (i, 0, 0)), table, table,
            pl.BlockSpec((width_of(length),) * 2, lambda i: (0, 0)),
        ],
        out_specs=[anywhere, pl.BlockSpec((1, HEAD, LANES), lambda i: (i, 0, 0))],
        out_shape=[
            jax.ShapeDtypeStruct((segment, 3 * width), jnp.bfloat16),
            jax.ShapeDtypeStruct((pairs, HEAD, LANES), jnp.float32),
        ],
        scratch_shapes=[
            pltpu.VMEM((pairs, length, LANES), jnp.bfloat16),
            pltpu.VMEM((pairs, 3, length, LANES), jnp.bfloat16),
            pltpu.VMEM((pairs, 3, length, LANES), jnp.bfloat16),
            pltpu.VMEM((LANES, length), jnp.float32),
            pltpu.VMEM((LANES, length), jnp.float32),
            dma((pairs,)), dma((pairs,)), dma((pairs,)), dma((pairs,)), dma((pairs, 3)), dma((pairs, 3)), dma((pairs, 3)),
        ],
        compiler_params=pltpu.CompilerParams(collective_id=identity, has_side_effects=True, vmem_limit_bytes=48 << 20),
        name="attend_back_split",
    )(out_grad, kept, logs, rel_low, rel_low[::-1], mirror_of(width_of(length)))


def feed_forward(values, norm_gain, norm_shift, weight_up, bias_up, weight_down, bias_down):
    normed = layer_norm(values, norm_gain, norm_shift).astype(jnp.bfloat16)
    hidden = product(normed, weight_up) + bias_up
    active = jax.nn.silu(hidden).astype(jnp.bfloat16)
    branch = product(active, weight_down) + bias_down
    return (branch, (normed, hidden, active))


def feed_backward(residual_grad, values, kept_parts, norm_gain, norm_shift, weight_up, weight_down):
    normed, hidden, active = kept_parts
    branch_grad = (0.5 * residual_grad).astype(jnp.bfloat16)
    down_grad = contract_rows(active, branch_grad)
    down_bias_grad = jnp.sum(branch_grad.astype(jnp.float32), axis=0)
    active_grad = times_transposed(branch_grad, weight_down)
    silu_pull = jax.vjp(jax.nn.silu, hidden)[1]
    hidden_grad = silu_pull(active_grad)[0].astype(jnp.bfloat16)
    up_grad = contract_rows(normed, hidden_grad)
    up_bias_grad = jnp.sum(hidden_grad.astype(jnp.float32), axis=0)
    normed_grad = times_transposed(hidden_grad, weight_up)
    norm_pull = jax.vjp(layer_norm, values, norm_gain, norm_shift)[1]
    values_grad, gain_grad, shift_grad = norm_pull(normed_grad)
    return (
        residual_grad + values_grad,
        up_grad,
        up_bias_grad,
        down_grad,
        down_bias_grad,
        gain_grad,
        shift_grad,
    )


def heads_of(projected, clip_count, segment, rel_low):
    parts = [
        lax.all_to_all(part.reshape(clip_count, segment, -1), "seq", split_axis=2, concat_axis=1, tiled=True)
        for part in jnp.split(projected, 3, axis=1)
    ]
    merged, log_totals = attend(*parts, rel_low)
    attn_seq = lax.all_to_all(merged, "seq", split_axis=1, concat_axis=2, tiled=True)
    return attn_seq.reshape(clip_count * segment, -1), parts, log_totals


def heads_back(out_grad, parts, log_totals, clip_count, segment, rel_low):
    merged = lax.all_to_all(
        out_grad.reshape(clip_count, segment, -1), "seq", split_axis=2, concat_axis=1, tiled=True
    )
    *grads, table_parts = attend_back(*parts, merged, log_totals, rel_low)
    grads = [
        lax.all_to_all(grad, "seq", split_axis=1, concat_axis=2, tiled=True).reshape(clip_count * segment, -1)
        for grad in grads
    ]
    return jnp.concatenate(grads, axis=1), jnp.sum(table_parts, axis=0)


def spread_sums(grads, small):
    sums = []
    for grad in grads:
        part = lax.psum_scatter(grad, "seq", scatter_dimension=1, tiled=True)
        part = lax.psum_scatter(part, "fsdp", scatter_dimension=0, tiled=True)
        sums.append(part.astype(jnp.float32))
    return (*sums, lax.psum(small, ("seq", "fsdp")))


def stacked(rows):
    lines = jnp.concatenate([row.reshape(-1, rows[0].shape[-1]) for row in rows])
    return jnp.pad(lines, ((0, -lines.shape[0] % 8), (0, 0)))


def body(
    tokens,
    cotangent,
    ffn1_up,
    ffn1_down,
    qkv_weight,
    out_weight,
    conv_in,
    conv_out,
    ffn2_up,
    ffn2_down,
    norm_gains,
    norm_biases,
    hidden_biases,
    model_biases,
    dw_kernel,
    rel_table,
):
    clip_count, segment, model_width = tokens.shape
    row_count = clip_count * segment
    rim_width = KERNEL - 1
    close = lax.axis_size("seq") == 2 and lax.axis_size("fsdp") == 16 and clip_count == 1
    low = jnp.bfloat16
    shards = [
        weight.astype(low)
        for weight in (ffn1_up, ffn1_down, qkv_weight, out_weight, conv_in, conv_out, ffn2_up, ffn2_down)
    ]
    if close:
        weights = gather_whole(shards, 0)
    else:
        weights = [lax.all_gather(shard, "fsdp", axis=0, tiled=True) for shard in shards]
    up_one, down_one, qkv_full, out_full, conv_first, conv_second, up_two, down_two = weights
    input_rows = tokens.reshape(row_count, model_width).astype(jnp.float32)
    branch_one, kept_one = feed_forward(
        input_rows,
        norm_gains[0],
        norm_biases[0],
        up_one,
        hidden_biases[0],
        down_one,
        model_biases[0],
    )
    after_one = input_rows + 0.5 * branch_one
    normed_attn = layer_norm(after_one, norm_gains[1], norm_biases[1]).astype(low)
    project_bias = jnp.concatenate([model_biases[1], jnp.zeros_like(model_biases[1]), model_biases[2]])
    projected = (product(normed_attn, qkv_full) + project_bias).astype(low)
    rel_low = padded_table(rel_table)
    if close:
        attn_rows, kept_heads, log_totals = attend_split(projected, rel_low, 1)
    else:
        attn_rows, kept_heads, log_totals = heads_of(projected, clip_count, segment, rel_low)
    after_two = after_one + product(attn_rows, out_full) + model_biases[3]
    normed_conv = layer_norm(after_two, norm_gains[2], norm_biases[2]).astype(low)
    gate_input = product(normed_conv, conv_first)
    glu_out = glu_function(gate_input).astype(low).reshape(clip_count, segment, model_width)
    glu_before = passed_along(glu_out[:, segment - rim_width :], "seq", 1)
    glu_wide = jnp.concatenate([glu_before, glu_out], axis=1).astype(jnp.float32)
    mixed_rows, kernel_pull = jax.vjp(partial(depthwise, glu_wide), dw_kernel)
    mixed_flat = mixed_rows.reshape(row_count, model_width)
    swished = conv_tail(mixed_flat, norm_gains[3], norm_biases[3]).astype(low)
    after_three = after_two + product(swished, conv_second)
    branch_two, kept_two = feed_forward(
        after_three,
        norm_gains[4],
        norm_biases[4],
        up_two,
        hidden_biases[1],
        down_two,
        model_biases[4],
    )
    after_four = after_three + 0.5 * branch_two
    final_rows, final_pull = jax.vjp(layer_norm, after_four, norm_gains[5], norm_biases[5])
    output = final_rows.astype(low).reshape(clip_count, segment, model_width)
    grad_four, gain_five, shift_five = final_pull(
        cotangent.reshape(row_count, model_width).astype(jnp.float32)
    )
    grad_three, up_two_grad, up_two_bias, down_two_grad, down_two_bias, gain_four, shift_four = (
        feed_backward(
            grad_four, after_three, kept_two, norm_gains[4], norm_biases[4], up_two, down_two
        )
    )
    conv_grad = grad_three.astype(low)
    conv_second_grad = contract_rows(swished, conv_grad)
    swished_grad = times_transposed(conv_grad, conv_second)
    tail_pull = jax.vjp(conv_tail, mixed_flat, norm_gains[3], norm_biases[3])[1]
    mixed_grad, gain_three, shift_three = tail_pull(swished_grad)
    mixed_low = mixed_grad.astype(low).reshape(clip_count, segment, model_width)
    mixed_after = passed_along(mixed_low[:, 0:rim_width], "seq", -1)
    mixed_wide = jnp.concatenate([mixed_low, mixed_after], axis=1).astype(jnp.float32)
    glu_grad = depthwise(mixed_wide, dw_kernel[::-1])
    kernel_grad = kernel_pull(mixed_low.astype(jnp.float32))[0]
    glu_pull = jax.vjp(glu_function, gate_input)[1]
    gate_grad = glu_pull(glu_grad.reshape(row_count, model_width))[0].astype(low)
    conv_first_grad = contract_rows(normed_conv, gate_grad)
    conv_norm_pull = jax.vjp(layer_norm, after_two, norm_gains[2], norm_biases[2])[1]
    values_grad, gain_two, shift_two = conv_norm_pull(times_transposed(gate_grad, conv_first))
    grad_two = grad_three + values_grad
    sums_of = partial(scatter_sums, identity=2) if close else spread_sums
    later_small = stacked(
        [gain_two, gain_three, gain_four, gain_five, shift_two, shift_three, shift_four, shift_five]
        + [up_two_bias, down_two_bias, kernel_grad]
    )
    conv_first_sum, conv_second_sum, up_two_sum, down_two_sum, later_sum = sums_of(
        [grad.astype(low) for grad in (conv_first_grad, conv_second_grad, up_two_grad, down_two_grad)],
        later_small,
    )
    attn_grad = grad_two.astype(low)
    out_grad = contract_rows(attn_rows, attn_grad)
    out_bias_grad = jnp.sum(attn_grad.astype(jnp.float32), axis=0)
    merged_grad = times_transposed(attn_grad, out_full).astype(low)
    if close:
        projected_grad, table_parts = attend_back_split(merged_grad, kept_heads, log_totals, rel_low, 3)
    else:
        projected_grad, table_parts = heads_back(
            merged_grad, kept_heads, log_totals, clip_count, segment, rel_low
        )
    table_grad = jnp.sum(table_parts, axis=0).T[::-1][:BUCKETS]
    qkv_grad = contract_rows(normed_attn, projected_grad)
    query_bias_grad = jnp.sum(projected_grad[:, :model_width].astype(jnp.float32), axis=0)
    value_bias_grad = jnp.sum(projected_grad[:, 2 * model_width :].astype(jnp.float32), axis=0)
    attn_norm_pull = jax.vjp(layer_norm, after_one, norm_gains[1], norm_biases[1])[1]
    values_grad, gain_one, shift_one = attn_norm_pull(times_transposed(projected_grad, qkv_full))
    grad_one = grad_two + values_grad
    grad_zero, up_one_grad, up_one_bias, down_one_grad, down_one_bias, gain_zero, shift_zero = (
        feed_backward(
            grad_one, input_rows, kept_one, norm_gains[0], norm_biases[0], up_one, down_one
        )
    )
    input_grad = grad_zero.astype(low).reshape(clip_count, segment, model_width)
    table_flat = table_grad.reshape(-1)
    table_rows = jnp.pad(table_flat, (0, -table_flat.size % model_width)).reshape(-1, model_width)
    early_small = stacked(
        [gain_zero, gain_one, shift_zero, shift_one, up_one_bias]
        + [down_one_bias, query_bias_grad, value_bias_grad, out_bias_grad, table_rows]
    )
    sums_of = partial(scatter_sums, identity=4) if close else spread_sums
    up_one_sum, down_one_sum, qkv_sum, out_sum, early_sum = sums_of(
        [grad.astype(low) for grad in (up_one_grad, down_one_grad, qkv_grad, out_grad)],
        early_small,
    )
    hidden_rows = up_one_bias.size // model_width
    after_hidden = 4 + hidden_rows
    table_at = after_hidden + 4
    table_sum = early_sum[table_at : table_at + table_rows.shape[0]].reshape(-1)[: table_flat.size]
    later_hidden = 8 + hidden_rows
    return (
        output,
        input_grad,
        up_one_sum,
        down_one_sum,
        qkv_sum,
        out_sum,
        conv_first_sum,
        conv_second_sum,
        up_two_sum,
        down_two_sum,
        jnp.concatenate([early_sum[0:2], later_sum[0:4]]),
        jnp.concatenate([early_sum[2:4], later_sum[4:5]]),
        later_sum[5:8],
        jnp.stack([early_sum[4:after_hidden].reshape(-1), later_sum[8:later_hidden].reshape(-1)]),
        early_sum[after_hidden : after_hidden + 3],
        jnp.concatenate([early_sum[after_hidden + 3 : table_at], later_sum[later_hidden : later_hidden + 1]]),
        later_sum[later_hidden + 1 : later_hidden + 1 + KERNEL],
        table_sum.reshape(table_grad.shape),
    )


def solution(mesh):
    in_specs = (
        P("fsdp", "seq", None),
        P("fsdp", "seq", None),
        P("fsdp", None),
        P("fsdp", None),
        P("fsdp", None),
        P("fsdp", None),
        P("fsdp", None),
        P("fsdp", None),
        P("fsdp", None),
        P("fsdp", None),
        P(),
        P(),
        P(),
        P(),
        P(),
        P(),
    )
    out_specs = (
        P("fsdp", "seq", None),
        P("fsdp", "seq", None),
        P("fsdp", "seq"),
        P("fsdp", "seq"),
        P("fsdp", "seq"),
        P("fsdp", "seq"),
        P("fsdp", "seq"),
        P("fsdp", "seq"),
        P("fsdp", "seq"),
        P("fsdp", "seq"),
        P(),
        P(),
        P(),
        P(),
        P(),
        P(),
        P(),
        P(),
    )
    return jax.shard_map(body, mesh=mesh, in_specs=in_specs, out_specs=out_specs, check_vma=False)
```

```python
import functools
from functools import partial

import jax
import jax.numpy as jnp
from jax import lax
from jax.experimental import pallas as pl
from jax.experimental.pallas import tpu as pltpu
from jax.sharding import PartitionSpec as P

HEAD = 64
KERNEL = 31
LEFT = 64
RIGHT = 8
BUCKETS = 73


EPSILON = 1e-05


def passed_along(value, axis, by):
    length = lax.axis_size(axis)
    pairs = [(i, i + by) for i in range(length) if 0 <= i + by < length]
    return lax.ppermute(value, axis, pairs)


def layer_norm(values, norm_gain, norm_shift):
    center = values - jnp.mean(values, axis=-1, keepdims=True)
    spread = jnp.mean(center * center, axis=-1, keepdims=True)
    return center * lax.rsqrt(spread + EPSILON) * norm_gain + norm_shift


def product(former, latter):
    return jnp.dot(former, latter, preferred_element_type=jnp.float32)


def contract_rows(former, latter):
    return lax.dot_general(
        former, latter, (((0,), (0,)), ((), ())), preferred_element_type=jnp.float32
    )


def times_transposed(former, latter):
    return lax.dot_general(
        former, latter, (((1,), (1,)), ((), ())), preferred_element_type=jnp.float32
    )


def glu_function(gate_input):
    half_width = gate_input.shape[1] // 2
    return gate_input[:, :half_width] * jax.nn.sigmoid(gate_input[:, half_width:])


def conv_tail(mixed_rows, norm_gain, norm_shift):
    return jax.nn.silu(layer_norm(mixed_rows, norm_gain, norm_shift))


MESH = pl.DeviceIdType.MESH
PIECE = 512


class Place:
    def __init__(self):
        self.x = lax.axis_index("seq")
        self.f = lax.axis_index("fsdp")
        self.c = lax.rem(self.f, 2)
        self.y = lax.rem(lax.div(self.f, 2), 2)
        self.z = lax.div(self.f, 4)

    def across(self):
        return (1 - self.x, self.f)

    def twin(self):
        return (self.x, self.f + 1 - 2 * self.c)

    def beside(self):
        return (self.x, self.f + 2 - 4 * self.y)

    def along(self, step):
        return (self.x, lax.rem(self.z + step, 4) * 4 + self.y * 2 + self.c)

    def greet(self):
        barrier = pltpu.get_barrier_semaphore()
        peers = [self.across(), self.twin(), self.beside()] + [self.along(s) for s in (1, 2, 3)]
        for peer in peers:
            pl.semaphore_signal(barrier, inc=1, device_id=peer, device_id_type=MESH)
        pl.semaphore_wait(barrier, len(peers))


def chunks_of(shapes, lines):
    found = []
    for index, (rows, width) in enumerate(shapes):
        for line in range(0, rows, lines):
            for column in range(0, width // 2, PIECE):
                found.append((index, line, column, len(found) % 3 != 2))
    return found


class Sent:
    def __init__(self, source, target, send_sem, recv_sem, device):
        self.parts = dict(src_ref=source, dst_ref=target, send_sem=send_sem, recv_sem=recv_sem, device_id=device, device_id_type=MESH)

    def start(self):
        pltpu.make_async_remote_copy(**self.parts).start()

    def wait_recv(self):
        pltpu.make_async_remote_copy(**self.parts).wait_recv()

    def wait_send(self):
        pltpu.make_async_remote_copy(**self.parts).wait_send()


def send(source, target, send_sem, recv_sem, device):
    copy = Sent(source, target, send_sem, recv_sem, device)
    copy.start()
    return copy


def gather_kernel(count, chunks, lines, *refs):
    shards, wholes = refs[:count], refs[count : 2 * count]
    own_sem, z_send, z_recv, y_send, y_recv, x_send, x_recv, c_send, c_recv = refs[2 * count :]
    me = Place()
    me.greet()
    live = {}

    def halves(chunk):
        index, line, column, early = chunk
        half = shards[index].shape[1] // 2
        if early:
            return [pl.ds(pl.multiple_of(me.x * half + column, PIECE), PIECE)]
        return [pl.ds(column, PIECE), pl.ds(half + column, PIECE)]

    def both(chunk):
        half = shards[chunk[0]].shape[1] // 2
        return [pl.ds(chunk[2], PIECE), pl.ds(half + chunk[2], PIECE)]

    def first(t):
        index, line, column, early = chunks[t]
        shard, whole = shards[index], wholes[index]
        rows = pl.ds(line, lines)
        live[t, "own"] = []
        for j, cols in enumerate(halves(chunks[t])):
            copy = pltpu.make_async_copy(shard.at[rows, cols], whole.at[me.z, me.y, me.c, rows, cols], own_sem.at[t, j])
            copy.start()
            live[t, "own"].append(copy)
        live[t, "z"] = [
            send(shard.at[rows, cols], whole.at[me.z, me.y, me.c, rows, cols], z_send.at[t, j, s - 1], z_recv.at[t, j, s - 1], me.along(s))
            for j, cols in enumerate(halves(chunks[t]))
            for s in (1, 2, 3)
        ]

    def second(t):
        index, line, column, early = chunks[t]
        whole, rows = wholes[index], pl.ds(line, lines)
        for copy in live[t, "own"]:
            copy.wait()
        for copy in live[t, "z"]:
            copy.wait_recv()
        live[t, "y"] = [
            send(whole.at[:, me.y, me.c, rows, cols], whole.at[:, me.y, me.c, rows, cols], y_send.at[t, j], y_recv.at[t, j], me.beside())
            for j, cols in enumerate(halves(chunks[t]))
        ]

    def third(t):
        index, line, column, early = chunks[t]
        whole, rows = wholes[index], pl.ds(line, lines)
        for copy in live[t, "y"]:
            copy.wait_recv()
        if early:
            (cols,) = halves(chunks[t])
            view = whole.at[:, :, me.c, rows, cols]
            live[t, "x"] = [send(view, view, x_send.at[t], x_recv.at[t], me.across())]
        else:
            live[t, "x"] = []

    def fourth(t):
        index, line, column, early = chunks[t]
        whole, rows = wholes[index], pl.ds(line, lines)
        for copy in live[t, "x"]:
            copy.wait_recv()
        live[t, "c"] = [
            send(whole.at[:, :, me.c, rows, cols], whole.at[:, :, me.c, rows, cols], c_send.at[t, j], c_recv.at[t, j], me.twin())
            for j, cols in enumerate(both(chunks[t]))
        ]

    total = len(chunks)
    for step in range(total + 3):
        for lag, phase in enumerate((first, second, third, fourth)):
            if 0 <= step - lag < total:
                phase(step - lag)
    for t in range(total):
        for copy in live[t, "c"]:
            copy.wait_recv()
        for kind in "zyxc":
            for copy in live[t, kind]:
                copy.wait_send()


def gather_whole(shards, identity):
    shapes = [shard.shape for shard in shards]
    lines = min(rows for rows, _ in shapes)
    chunks = chunks_of(shapes, lines)
    count, total = len(shards), len(chunks)
    dma = pltpu.SemaphoreType.DMA
    anywhere = pl.BlockSpec(memory_space=pl.ANY)
    wholes = pl.pallas_call(
        functools.partial(gather_kernel, count, chunks, lines),
        in_specs=[anywhere] * count,
        out_specs=[anywhere] * count,
        out_shape=[jax.ShapeDtypeStruct((4, 2, 2, *shape), jnp.bfloat16) for shape in shapes],
        scratch_shapes=[
            dma((total, 2)), dma((total, 2, 3)), dma((total, 2, 3)), dma((total, 2)), dma((total, 2)),
            dma((total,)), dma((total,)), dma((total, 2)), dma((total, 2)),
        ],
        compiler_params=pltpu.CompilerParams(collective_id=identity, has_side_effects=True, vmem_limit_bytes=4 << 20),
        name="gather_whole",
    )(*shards)
    return [whole.reshape(-1, whole.shape[-1]) for whole in wholes]


SLOTS = 5


def scatter_kernel(count, chunks, lines, *refs):
    lefts, rights, small = refs[:count], refs[count : 2 * count], refs[2 * count]
    outs, small_out = refs[2 * count + 1 : 3 * count + 1], refs[3 * count + 1]
    (turned, held, core_in, early_in, late_in, y_in, z_in, end_in, done, done_sem,
     c_send, c_recv, x_send, x_recv, y_send, y_recv, z_send, z_recv,
     small_held, small_in, small_z, small_send, small_recv, small_z_send, small_z_recv) = refs[3 * count + 2 :]
    me = Place()
    me.greet()
    live = {}
    order = [sum(other[3] == chunk[3] for other in chunks[:t]) for t, chunk in enumerate(chunks)]

    def columns(chunk, j):
        return pl.ds(j * (rights[chunk[0]].shape[1] // 2) + chunk[2], PIECE)

    def sums(former, latter):
        return (former.astype(jnp.float32) + latter.astype(jnp.float32)).astype(jnp.bfloat16)

    def turn(t):
        index, line, column, early = chunks[t]
        left, rows = lefts[index], lefts[index].shape[1] // 16
        if rows > lines:
            if line % (2 * lines) == 0:

                @pl.loop(0, 16)
                def _(i):
                    block = jnp.transpose(left[:, pl.ds(pl.multiple_of(i * rows + line, 2 * lines), 2 * lines)])
                    turned[0, pl.ds(pl.multiple_of(i * lines, lines), lines), :] = block[:lines]
                    turned[1, pl.ds(pl.multiple_of(i * lines, lines), lines), :] = block[lines:]

            return line // lines % 2
        if column == 0:

            @pl.loop(0, 8)
            def _(i):
                span = pl.ds(pl.multiple_of(i * 2 * lines, 2 * lines), 2 * lines)
                turned[0, span, :] = jnp.transpose(left[:, span])

        return 0

    def first(t):
        slot = t % SLOTS
        if t >= SLOTS:
            for kind in "czyx":
                for copy in live[t - SLOTS, kind]:
                    copy.wait_send()
        which = turn(t)
        right = rights[chunks[t][0]]
        live[t, "c"] = []
        for j in range(2):
            cols = columns(chunks[t], j)

            @pl.loop(0, 4)
            def _(z):
                part = nn(turned[which, pl.ds(pl.multiple_of(z * 4 * lines, 4 * lines), 4 * lines), :], right[:, cols]).astype(jnp.bfloat16)
                for y in range(2):
                    for core in range(2):
                        held[slot, core, j, z, y] = part[(2 * y + core) * lines : (2 * y + core + 1) * lines]

            live[t, "c"].append(send(held.at[slot, 1 - me.c, j], core_in.at[t, j], c_send.at[t, j], c_recv.at[t, j], me.twin()))

    def second(t):
        early, slot = chunks[t][3], t % SLOTS
        for j in range(2):
            live[t, "c"][j].wait_recv()
            for z in range(4):
                held[slot, me.c, j, z] = sums(held[slot, me.c, j, z], core_in[t, j, z])
        if early:
            live[t, "x"] = [send(held.at[slot, me.c, 1 - me.x], early_in.at[order[t]], x_send.at[t], x_recv.at[t], me.across())]
        else:
            live[t, "y"] = [send(held.at[slot, me.c, :, :, 1 - me.y], late_in.at[order[t]], y_send.at[t], y_recv.at[t], me.beside())]

    def third(t):
        early, slot = chunks[t][3], t % SLOTS
        if early:
            live[t, "x"][0].wait_recv()
            for z in range(4):
                held[slot, me.c, me.x, z] = sums(held[slot, me.c, me.x, z], early_in[order[t], z])
            live[t, "y"] = [send(held.at[slot, me.c, me.x, :, 1 - me.y], y_in.at[order[t]], y_send.at[t], y_recv.at[t], me.beside())]
        else:
            live[t, "y"][0].wait_recv()
            for j in range(2):
                for z in range(4):
                    held[slot, me.c, j, z, me.y] = sums(held[slot, me.c, j, z, me.y], late_in[order[t], j, z])
            live[t, "z"] = [
                send(held.at[slot, me.c, :, lax.rem(me.z + s, 4), me.y], z_in.at[order[t], s - 1], z_send.at[t, s - 1], z_recv.at[t, s - 1], me.along(s))
                for s in (1, 2, 3)
            ]

    def fourth(t):
        early, slot = chunks[t][3], t % SLOTS
        if early:
            live[t, "y"][0].wait_recv()
            for z in range(4):
                held[slot, me.c, me.x, z, me.y] = sums(held[slot, me.c, me.x, z, me.y], y_in[order[t], z])
            live[t, "z"] = [
                send(held.at[slot, me.c, me.x, lax.rem(me.z + s, 4), me.y], end_in.at[t, s - 1], z_send.at[t, s - 1], z_recv.at[t, s - 1], me.along(s))
                for s in (1, 2, 3)
            ]
        else:
            for copy in live[t, "z"]:
                copy.wait_recv()
            for j in range(2):
                value = held[slot, me.c, j, me.z, me.y].astype(jnp.float32)
                for s in range(3):
                    value = value + z_in[order[t], s, j].astype(jnp.float32)
                held[slot, me.c, j, me.z, me.y] = value.astype(jnp.bfloat16)
            live[t, "x"] = [send(held.at[slot, me.c, 1 - me.x, me.z, me.y], end_in.at[t, 0], x_send.at[t], x_recv.at[t], me.across())]

    def fifth(t):
        index, line, column, early = chunks[t]
        slot = t % SLOTS
        value = held[slot, me.c, me.x, me.z, me.y].astype(jnp.float32)
        if early:
            for copy in live[t, "z"]:
                copy.wait_recv()
            for s in range(3):
                value = value + end_in[t, s].astype(jnp.float32)
        else:
            live[t, "x"][0].wait_recv()
            value = value + end_in[t, 0].astype(jnp.float32)
        done[t] = value
        copy = pltpu.make_async_copy(done.at[t], outs[index].at[pl.ds(line, lines), pl.ds(column, PIECE)], done_sem.at[t])
        copy.start()
        live[t, "done"] = [copy]

    def small_step(stage):
        if stage > 0:
            live["small", stage - 1].wait_recv()
            small_held[stage] = small_held[stage - 1] + small_in[stage - 1]
        if stage < 3:
            peer = (me.twin, me.across, me.beside)[stage]()
            live["small", stage] = send(small_held.at[stage], small_in.at[stage], small_send.at[stage], small_recv.at[stage], peer)
        else:
            small_z[me.z] = small_held[3]
            for s in (1, 2, 3):
                live["small z", s] = send(small_held.at[3], small_z.at[me.z], small_z_send.at[s - 1], small_z_recv.at[s - 1], me.along(s))

    def small_end():
        for s in (1, 2, 3):
            live["small z", s].wait_recv()
            live["small z", s].wait_send()
            live["small", s - 1].wait_send()
        small_out[...] = (small_z[0] + small_z[1]) + (small_z[2] + small_z[3])

    total = len(chunks)
    small_held[0] = small[...]
    for step in range(total + 4):
        if step < 4:
            small_step(step)
        for lag, phase in enumerate((first, second, third, fourth, fifth)):
            if 0 <= step - lag < total:
                phase(step - lag)
    small_end()
    for t in range(total):
        live[t, "done"][0].wait()
        if t + SLOTS >= total:
            for kind in "czyx":
                for copy in live[t, kind]:
                    copy.wait_send()


def scatter_sums(factors, small, identity):
    shapes = [(left.shape[1] // 16, right.shape[1]) for left, right in factors]
    lines = min(rows for rows, _ in shapes)
    chunks = chunks_of(shapes, lines)
    count, total = len(factors), len(chunks)
    tokens = factors[0][0].shape[0]
    dma = pltpu.SemaphoreType.DMA
    anywhere, near = pl.BlockSpec(memory_space=pl.ANY), pl.BlockSpec(memory_space=pltpu.VMEM)
    low = jnp.bfloat16
    early = sum(chunk[3] for chunk in chunks)
    late = total - early
    return pl.pallas_call(
        functools.partial(scatter_kernel, count, chunks, lines),
        in_specs=[near] * (2 * count + 1),
        out_specs=[anywhere] * count + [near],
        out_shape=[jax.ShapeDtypeStruct((rows, width // 2), jnp.float32) for rows, width in shapes]
        + [jax.ShapeDtypeStruct(small.shape, jnp.float32)],
        scratch_shapes=[
            pltpu.VMEM((2, 16 * lines, tokens), low),
            pltpu.VMEM((SLOTS, 2, 2, 4, 2, lines, PIECE), low),
            pltpu.VMEM((total, 2, 4, 2, lines, PIECE), low),
            pltpu.VMEM((early, 4, 2, lines, PIECE), low),
            pltpu.VMEM((late, 2, 4, lines, PIECE), low),
            pltpu.VMEM((early, 4, lines, PIECE), low),
            pltpu.VMEM((late, 3, 2, lines, PIECE), low),
            pltpu.VMEM((total, 3, lines, PIECE), low),
            pltpu.VMEM((total, lines, PIECE), jnp.float32),
            dma((total,)),
            dma((total, 2)), dma((total, 2)), dma((total,)), dma((total,)),
            dma((total,)), dma((total,)), dma((total, 3)), dma((total, 3)),
            pltpu.VMEM((4, *small.shape), jnp.float32),
            pltpu.VMEM((3, *small.shape), jnp.float32),
            pltpu.VMEM((4, *small.shape), jnp.float32),
            dma((3,)), dma((3,)), dma((3,)), dma((3,)),
        ],
        compiler_params=pltpu.CompilerParams(collective_id=identity, has_side_effects=True, vmem_limit_bytes=60 << 20),
        name="scatter_sums",
    )(*[left for left, _ in factors], *[right for _, right in factors], small)


PAIR = 2
LANES = 128
FWD_ROWS = 256
BACK_ROWS = 256


def nt(former, latter):
    return lax.dot_general(former, latter, (((1,), (1,)), ((), ())), preferred_element_type=jnp.float32)


def nn(former, latter):
    return lax.dot_general(former, latter, (((1,), (0,)), ((), ())), preferred_element_type=jnp.float32)


def window_of(start, rows, length):
    low, high = start - LANES, start + rows + LANES
    return max(low, 0), min(high, length), max(low, 0) - low


def window_buckets(rows):
    width = rows + 2 * LANES
    places = lax.broadcasted_iota(jnp.int32, (rows, width), 1)
    lines = lax.broadcasted_iota(jnp.int32, (rows, width), 0)
    return places - lines - (LANES - LEFT)


def biased_scores(scores, position, start, rows, length):
    width = rows + 2 * LANES
    low, high, skip = window_of(start, rows, length)
    wide = jnp.concatenate([position, jnp.zeros((rows, width - LANES), jnp.float32)], axis=1)
    band = pltpu.roll(wide, LANES - LEFT, 1, stride=1, stride_axis=0)
    first, last = position[:, 0:1], position[:, BUCKETS - 1 : BUCKETS]
    bucket = window_buckets(rows)
    band = jnp.where(bucket <= 0, first, jnp.where(bucket >= BUCKETS - 1, last, band))
    pieces = []
    if low > 0:
        pieces.append(scores[:, :low] + first)
    pieces.append(scores[:, low:high] + band[:, skip : skip + high - low])
    if high < length:
        pieces.append(scores[:, high:] + last)
    return pieces[0] if len(pieces) == 1 else jnp.concatenate(pieces, axis=1)


def bucket_sums(score_grad, mirror, start, rows, length):
    width = rows + 2 * LANES
    low, high, skip = window_of(start, rows, length)
    inner = score_grad[:, low:high]
    pieces = []
    if skip > 0:
        pieces.append(jnp.zeros((rows, skip), jnp.float32))
    pieces.append(inner)
    if skip + high - low < width:
        pieces.append(jnp.zeros((rows, width - skip - high + low), jnp.float32))
    wide = pieces[0] if len(pieces) == 1 else jnp.concatenate(pieces, axis=1)
    bucket = window_buckets(rows)
    first = jnp.sum(jnp.where(bucket <= 0, wide, 0.0), axis=1, keepdims=True)
    last = jnp.sum(jnp.where(bucket >= BUCKETS - 1, wide, 0.0), axis=1, keepdims=True)
    if low > 0:
        first = first + jnp.sum(score_grad[:, :low], axis=1, keepdims=True)
    if high < length:
        last = last + jnp.sum(score_grad[:, high:], axis=1, keepdims=True)
    turned = nn(wide.astype(jnp.bfloat16), mirror)
    band = pltpu.roll(turned, (LANES + LANES - LEFT) % width, 1, stride=1, stride_axis=0)[:, :LANES]
    bucket = LANES - 1 - lax.broadcasted_iota(jnp.int32, (rows, LANES), 1)
    return jnp.where(bucket == 0, first, jnp.where(bucket == BUCKETS - 1, last, jnp.where(bucket < BUCKETS, band, 0.0)))


def mirror_of(width):
    lines = lax.broadcasted_iota(jnp.int32, (width, width), 0)
    places = lax.broadcasted_iota(jnp.int32, (width, width), 1)
    return jnp.where(lines + places == width - 1, 1.0, 0.0).astype(jnp.bfloat16)


def attend_pair(q_ref, k_ref, v_ref, rel_ref, out_ref, log_ref):
    length = q_ref.shape[0]
    rows = min(FWD_ROWS, length)
    scale = HEAD ** (-0.5)
    rel = rel_ref[...]
    for start in range(0, length, rows):
        outs, logs = [], []
        for h in range(PAIR):
            lanes = slice(h * HEAD, (h + 1) * HEAD)
            query = q_ref[start : start + rows, lanes] * scale
            scores = nt(query, k_ref[:, lanes])
            scores = biased_scores(scores, nt(query, rel), start, rows, length)
            highest = jnp.max(scores, axis=1, keepdims=True)
            weights = jnp.exp(scores - highest)
            total = jnp.sum(weights, axis=1, keepdims=True)
            outs.append(nn(weights.astype(jnp.bfloat16), v_ref[:, lanes]) / total)
            logs.append(highest + jnp.log(total))
        out_ref[start : start + rows, :] = jnp.concatenate(outs, axis=1).astype(jnp.bfloat16)
        log_ref[start : start + rows, :] = jnp.concatenate(logs, axis=1)


def attend_back_pair(
    q_ref, k_ref, v_ref, do_ref, log_ref, rel_ref, back_ref, mirror_ref, dq_ref, dk_ref, dv_ref, table_ref, dkt, dvt
):
    length = q_ref.shape[0]
    rows = min(BACK_ROWS, length)
    scale = HEAD ** (-0.5)
    rel, back = rel_ref[...], back_ref[...]
    q_turned = (jnp.transpose(q_ref[...].astype(jnp.float32)) * scale).astype(jnp.bfloat16)
    do_turned = jnp.transpose(do_ref[...].astype(jnp.float32)).astype(jnp.bfloat16)
    table = jnp.zeros((HEAD, LANES), jnp.float32)
    for start in range(0, length, rows):
        span = slice(start, start + rows)
        parts = []
        for h in range(PAIR):
            lanes = slice(h * HEAD, (h + 1) * HEAD)
            query = q_ref[span, lanes] * scale
            scores = nt(query, k_ref[:, lanes])
            scores = biased_scores(scores, nt(query, rel), start, rows, length)
            weights = jnp.exp(scores - log_ref[span, h : h + 1])
            low_weights = weights.astype(jnp.bfloat16)
            grads = nt(do_ref[span, lanes], v_ref[:, lanes])
            both = weights * grads
            delta = jnp.sum(both, axis=1, keepdims=True)
            score_grad = (both - weights * delta).astype(jnp.bfloat16)
            value_part = nn(do_turned[lanes, span], low_weights)
            key_part = nn(q_turned[lanes, span], score_grad)
            if start == 0:
                dvt[lanes, :] = value_part
                dkt[lanes, :] = key_part
            else:
                dvt[lanes, :] += value_part
                dkt[lanes, :] += key_part
            bucket = bucket_sums(score_grad.astype(jnp.float32), mirror_ref[...], start, rows, length)
            high = bucket.astype(jnp.bfloat16)
            rest = (bucket - high.astype(jnp.float32)).astype(jnp.bfloat16)
            parts.append((nn(score_grad, k_ref[:, lanes]) + nn(high, back) + nn(rest, back)) * scale)
            table = table + nn(q_turned[lanes, span], high) + nn(q_turned[lanes, span], rest)
        dq_ref[span, :] = jnp.concatenate(parts, axis=1).astype(jnp.bfloat16)
    dk_ref[...] = jnp.transpose(dkt[...]).astype(jnp.bfloat16)
    dv_ref[...] = jnp.transpose(dvt[...]).astype(jnp.bfloat16)
    table_ref[...] = table


def attend_kernel(q_ref, k_ref, v_ref, rel_ref, out_ref, log_ref):
    attend_pair(q_ref.at[0], k_ref.at[0], v_ref.at[0], rel_ref, out_ref.at[0], log_ref.at[0, 0])


def attend_back_kernel(
    q_ref, k_ref, v_ref, do_ref, log_ref, rel_ref, back_ref, mirror_ref, dq_ref, dk_ref, dv_ref, table_ref, dkt, dvt
):
    attend_back_pair(
        q_ref.at[0], k_ref.at[0], v_ref.at[0], do_ref.at[0], log_ref.at[0, 0], rel_ref, back_ref, mirror_ref,
        dq_ref.at[0], dk_ref.at[0], dv_ref.at[0], table_ref.at[0, 0], dkt, dvt,
    )


def width_of(length):
    return min(BACK_ROWS, length) + 2 * LANES


def head_block(length):
    return pl.BlockSpec((1, length, PAIR * HEAD), lambda i, j: (i, 0, j))


def padded_table(rel_table):
    return jnp.pad(rel_table.astype(jnp.bfloat16), ((0, LANES - BUCKETS), (0, 0)))


def attend(query, key, value, rel_low):
    clips, length, width = query.shape
    pairs = width // (PAIR * HEAD)
    block = head_block(length)
    return pl.pallas_call(
        attend_kernel,
        grid=(clips, pairs),
        in_specs=[block, block, block, pl.BlockSpec((LANES, HEAD), lambda i, j: (0, 0))],
        out_specs=[block, pl.BlockSpec((1, 1, length, PAIR), lambda i, j: (i, j, 0, 0))],
        out_shape=[
            jax.ShapeDtypeStruct(query.shape, jnp.bfloat16),
            jax.ShapeDtypeStruct((clips, pairs, length, PAIR), jnp.float32),
        ],
        compiler_params=pltpu.CompilerParams(vmem_limit_bytes=48 << 20),
        cost_estimate=pl.CostEstimate(flops=4 * clips * width * length * length * 4, bytes_accessed=8 * query.size, transcendentals=clips * pairs * PAIR * length * length),
        name="attend",
    )(query, key, value, rel_low)


def attend_back(query, key, value, out_grad, logs, rel_low):
    clips, length, width = query.shape
    pairs = width // (PAIR * HEAD)
    block = head_block(length)
    shape = jax.ShapeDtypeStruct(query.shape, jnp.bfloat16)
    return pl.pallas_call(
        attend_back_kernel,
        grid=(clips, pairs),
        in_specs=[
            block, block, block, block,
            pl.BlockSpec((1, 1, length, PAIR), lambda i, j: (i, j, 0, 0)),
            pl.BlockSpec((LANES, HEAD), lambda i, j: (0, 0)),
            pl.BlockSpec((LANES, HEAD), lambda i, j: (0, 0)),
            pl.BlockSpec((width_of(length),) * 2, lambda i, j: (0, 0)),
        ],
        out_specs=[block, block, block, pl.BlockSpec((1, 1, HEAD, LANES), lambda i, j: (i, j, 0, 0))],
        out_shape=[shape, shape, shape, jax.ShapeDtypeStruct((clips, pairs, HEAD, LANES), jnp.float32)],
        scratch_shapes=[pltpu.VMEM((PAIR * HEAD, length), jnp.float32)] * 2,
        compiler_params=pltpu.CompilerParams(vmem_limit_bytes=48 << 20),
        cost_estimate=pl.CostEstimate(flops=10 * clips * width * length * length * 4, bytes_accessed=14 * query.size, transcendentals=clips * pairs * PAIR * length * length),
        name="attend_back",
    )(query, key, value, out_grad, logs, rel_low, rel_low[::-1], mirror_of(width_of(length)))


def strip(index):
    return pl.ds(pl.multiple_of(index * LANES, LANES), LANES)


def meet_across(me):
    barrier = pltpu.get_barrier_semaphore()
    pl.semaphore_signal(barrier, inc=1, device_id=me.across(), device_id_type=MESH)
    pl.semaphore_wait(barrier, 1)


def attend_split_kernel(
    pairs, p_ref, rel_ref, out_ref, kept_ref, log_ref, qkv, outs, own_sem, send_sem, recv_sem, kept_sem, out_sem, back_send, back_recv
):
    me = Place()
    step = pl.program_id(0)
    segment = p_ref.shape[0]
    mine, theirs = pl.ds(me.x * segment, segment), pl.ds((1 - me.x) * segment, segment)

    def leaving(i):
        return [
            Sent(p_ref.at[:, strip((2 * part + 1 - me.x) * pairs + i)], qkv.at[i, part, mine, :], send_sem.at[i, part], recv_sem.at[i, part], me.across())
            for part in range(3)
        ]

    def staying(i):
        return [
            pltpu.make_async_copy(p_ref.at[:, strip((2 * part + me.x) * pairs + i)], qkv.at[i, part, mine, :], own_sem.at[i, part])
            for part in range(3)
        ]

    def returns(i):
        there = out_ref.at[:, strip(me.x * pairs + i)]
        return (
            Sent(outs.at[i, theirs, :], there, back_send.at[i], back_recv.at[i], me.across()),
            pltpu.make_async_copy(outs.at[i, mine, :], there, out_sem.at[i]),
            pltpu.make_async_copy(qkv.at[i], kept_ref.at[i], kept_sem.at[i]),
        )

    @pl.when(step == 0)
    def _():
        meet_across(me)
        for i in range(pairs):
            for copy in leaving(i) + staying(i):
                copy.start()

    for copy in leaving(step):
        copy.wait_recv()
    for copy in staying(step):
        copy.wait()
    attend_pair(qkv.at[step, 0], qkv.at[step, 1], qkv.at[step, 2], rel_ref, outs.at[step], log_ref.at[0])
    for copy in returns(step):
        copy.start()

    @pl.when(step == pairs - 1)
    def _():
        for i in range(pairs):
            for copy in leaving(i):
                copy.wait_send()
            sent, kept, own = returns(i)
            sent.wait_send()
            sent.wait_recv()
            kept.wait()
            own.wait()


def attend_split(projected, rel_low, identity):
    segment, width = projected.shape[0], projected.shape[1] // 3
    length, pairs = 2 * segment, width // (2 * PAIR * HEAD)
    dma, anywhere = pltpu.SemaphoreType.DMA, pl.BlockSpec(memory_space=pl.ANY)
    return pl.pallas_call(
        functools.partial(attend_split_kernel, pairs),
        grid=(pairs,),
        in_specs=[anywhere, pl.BlockSpec((LANES, HEAD), lambda i: (0, 0))],
        out_specs=[anywhere, anywhere, pl.BlockSpec((1, length, PAIR), lambda i: (i, 0, 0))],
        out_shape=[
            jax.ShapeDtypeStruct((segment, width), jnp.bfloat16),
            jax.ShapeDtypeStruct((pairs, 3, length, LANES), jnp.bfloat16),
            jax.ShapeDtypeStruct((pairs, length, PAIR), jnp.float32),
        ],
        scratch_shapes=[
            pltpu.VMEM((pairs, 3, length, LANES), jnp.bfloat16),
            pltpu.VMEM((pairs, length, LANES), jnp.bfloat16),
            dma((pairs, 3)), dma((pairs, 3)), dma((pairs, 3)), dma((pairs,)), dma((pairs,)), dma((pairs,)), dma((pairs,)),
        ],
        compiler_params=pltpu.CompilerParams(collective_id=identity, has_side_effects=True, vmem_limit_bytes=48 << 20),
        name="attend_split",
    )(projected, rel_low)


def attend_back_split_kernel(
    pairs, do_ref, kept_ref, log_ref, rel_ref, back_ref, mirror_ref, dp_ref, table_ref,
    grads, qkv, outs, dkt, dvt, own_sem, send_sem, recv_sem, kept_sem, out_sem, back_send, back_recv
):
    me = Place()
    step = pl.program_id(0)
    segment = do_ref.shape[0]
    mine, theirs = pl.ds(me.x * segment, segment), pl.ds((1 - me.x) * segment, segment)

    def leaving(i):
        return Sent(do_ref.at[:, strip((1 - me.x) * pairs + i)], grads.at[i, mine, :], send_sem.at[i], recv_sem.at[i], me.across())

    def staying(i):
        return (
            pltpu.make_async_copy(do_ref.at[:, strip(me.x * pairs + i)], grads.at[i, mine, :], own_sem.at[i]),
            pltpu.make_async_copy(kept_ref.at[i], qkv.at[i], kept_sem.at[i]),
        )

    def returns(i, part):
        there = dp_ref.at[:, strip((2 * part + me.x) * pairs + i)]
        return (
            Sent(outs.at[i, part, theirs, :], there, back_send.at[i, part], back_recv.at[i, part], me.across()),
            pltpu.make_async_copy(outs.at[i, part, mine, :], there, out_sem.at[i, part]),
        )

    @pl.when(step == 0)
    def _():
        meet_across(me)
        for i in range(pairs):
            leaving(i).start()
            for copy in staying(i):
                copy.start()

    leaving(step).wait_recv()
    for copy in staying(step):
        copy.wait()
    attend_back_pair(
        qkv.at[step, 0], qkv.at[step, 1], qkv.at[step, 2], grads.at[step], log_ref.at[0], rel_ref, back_ref, mirror_ref,
        outs.at[step, 0], outs.at[step, 1], outs.at[step, 2], table_ref.at[0], dkt, dvt,
    )
    for part in range(3):
        for copy in returns(step, part):
            copy.start()

    @pl.when(step == pairs - 1)
    def _():
        for i in range(pairs):
            leaving(i).wait_send()
            for part in range(3):
                sent, own = returns(i, part)
                sent.wait_send()
                sent.wait_recv()
                own.wait()


def attend_back_split(out_grad, kept, logs, rel_low, identity):
    segment, width = out_grad.shape
    pairs, _, length, _ = kept.shape
    dma, anywhere = pltpu.SemaphoreType.DMA, pl.BlockSpec(memory_space=pl.ANY)
    table = pl.BlockSpec((LANES, HEAD), lambda i: (0, 0))
    return pl.pallas_call(
        functools.partial(attend_back_split_kernel, pairs),
        grid=(pairs,),
        in_specs=[
            anywhere, anywhere, pl.BlockSpec((1, length, PAIR), lambda i: (i, 0, 0)), table, table,
            pl.BlockSpec((width_of(length),) * 2, lambda i: (0, 0)),
        ],
        out_specs=[anywhere, pl.BlockSpec((1, HEAD, LANES), lambda i: (i, 0, 0))],
        out_shape=[
            jax.ShapeDtypeStruct((segment, 3 * width), jnp.bfloat16),
            jax.ShapeDtypeStruct((pairs, HEAD, LANES), jnp.float32),
        ],
        scratch_shapes=[
            pltpu.VMEM((pairs, length, LANES), jnp.bfloat16),
            pltpu.VMEM((pairs, 3, length, LANES), jnp.bfloat16),
            pltpu.VMEM((pairs, 3, length, LANES), jnp.bfloat16),
            pltpu.VMEM((LANES, length), jnp.float32),
            pltpu.VMEM((LANES, length), jnp.float32),
            dma((pairs,)), dma((pairs,)), dma((pairs,)), dma((pairs,)), dma((pairs, 3)), dma((pairs, 3)), dma((pairs, 3)),
        ],
        compiler_params=pltpu.CompilerParams(collective_id=identity, has_side_effects=True, vmem_limit_bytes=48 << 20),
        name="attend_back_split",
    )(out_grad, kept, logs, rel_low, rel_low[::-1], mirror_of(width_of(length)))


TAPS = 32
TILE = 128


def conv_kernel(wide_ref, taps_ref, out_ref, spread):
    length = out_ref.shape[1]
    spread[...] = wide_ref[0].astype(jnp.float32)
    for start in range(0, length, TILE):
        total = jnp.zeros((TILE, LANES), jnp.float32)
        for r in range(KERNEL):
            total = total + taps_ref[r : r + 1, :] * spread[start + r + 2 : start + r + 2 + TILE, :]
        out_ref[0, start : start + TILE, :] = total


def conv_back_kernel(grad_ref, wide_ref, taps_ref, value_ref, gate_ref, dvalue_ref, dgate_ref, kernel_ref, spread, grads, sums):
    length = value_ref.shape[0]
    spread[...] = wide_ref[0].astype(jnp.float32)
    grads[...] = grad_ref[0].astype(jnp.float32)

    @pl.when(pl.program_id(1) == 0)
    def _():
        sums[...] = jnp.zeros_like(sums)

    for start in range(0, length, TILE):
        own = grads[start : start + TILE, :]
        total = jnp.zeros((TILE, LANES), jnp.float32)
        for r in range(KERNEL):
            total = total + taps_ref[r : r + 1, :] * grads[start + KERNEL - 1 - r : start + KERNEL - 1 - r + TILE, :]
            both = own * spread[start + r + 2 : start + r + 2 + TILE, :]
            sums[r] += jnp.sum(both.reshape(TILE // 8, 8, LANES), axis=0)
        span = slice(start, start + TILE)
        opened = jax.nn.sigmoid(gate_ref[span, :])
        dvalue_ref[span, :] = (total * opened).astype(jnp.bfloat16)
        dgate_ref[span, :] = (total * value_ref[span, :] * (opened * (1.0 - opened))).astype(jnp.bfloat16)
    kernel_ref[...] = jnp.sum(sums[...], axis=1)


def padded_taps(dw_kernel):
    return jnp.pad(dw_kernel, ((0, TAPS - KERNEL), (0, 0)))


def depthwise(wide, dw_kernel):
    clips, lines, width = wide.shape
    length = lines - TAPS
    return pl.pallas_call(
        conv_kernel,
        grid=(width // LANES, clips),
        in_specs=[
            pl.BlockSpec((1, lines, LANES), lambda i, j: (j, 0, i)),
            pl.BlockSpec((TAPS, LANES), lambda i, j: (0, i)),
        ],
        out_specs=pl.BlockSpec((1, length, LANES), lambda i, j: (j, 0, i)),
        out_shape=jax.ShapeDtypeStruct((clips, length, width), jnp.float32),
        scratch_shapes=[pltpu.VMEM((lines, LANES), jnp.float32)],
        cost_estimate=pl.CostEstimate(flops=2 * KERNEL * clips * length * width, bytes_accessed=6 * clips * length * width, transcendentals=0),
        name="depthwise",
    )(wide, padded_taps(dw_kernel))


def depthwise_back(grad_wide, wide, dw_kernel, gate_input):
    clips, lines, width = wide.shape
    length, blocks = lines - TAPS, width // LANES
    tall = pl.BlockSpec((1, lines, LANES), lambda i, j: (j, 0, i))
    half = pl.BlockSpec((length, LANES), lambda i, j: (j, i))
    taps = pl.BlockSpec((TAPS, LANES), lambda i, j: (0, i))
    shape = jax.ShapeDtypeStruct((clips * length, width), jnp.bfloat16)
    dvalue, dgate, kernel_grad = pl.pallas_call(
        conv_back_kernel,
        grid=(blocks, clips),
        in_specs=[tall, tall, taps, half, pl.BlockSpec((length, LANES), lambda i, j: (j, blocks + i))],
        out_specs=[half, half, taps],
        out_shape=[shape, shape, jax.ShapeDtypeStruct((TAPS, width), jnp.float32)],
        scratch_shapes=[
            pltpu.VMEM((lines, LANES), jnp.float32),
            pltpu.VMEM((lines, LANES), jnp.float32),
            pltpu.VMEM((TAPS, 8, LANES), jnp.float32),
        ],
        cost_estimate=pl.CostEstimate(flops=4 * KERNEL * clips * length * width, bytes_accessed=16 * clips * length * width, transcendentals=clips * length * width),
        name="depthwise_back",
    )(grad_wide, wide, padded_taps(dw_kernel), gate_input, gate_input)
    return jnp.concatenate([dvalue, dgate], axis=1), kernel_grad[:KERNEL]


def feed_forward(values, norm_gain, norm_shift, weight_up, bias_up, weight_down, bias_down):
    normed = layer_norm(values, norm_gain, norm_shift).astype(jnp.bfloat16)
    hidden = product(normed, weight_up) + bias_up
    active = jax.nn.silu(hidden).astype(jnp.bfloat16)
    branch = product(active, weight_down) + bias_down
    return (branch, (normed, hidden, active))


def feed_backward(residual_grad, values, kept_parts, norm_gain, norm_shift, weight_up, weight_down):
    normed, hidden, active = kept_parts
    branch_grad = (0.5 * residual_grad).astype(jnp.bfloat16)
    down_bias_grad = jnp.sum(branch_grad.astype(jnp.float32), axis=0)
    active_grad = times_transposed(branch_grad, weight_down)
    silu_pull = jax.vjp(jax.nn.silu, hidden)[1]
    hidden_grad = silu_pull(active_grad)[0].astype(jnp.bfloat16)
    up_bias_grad = jnp.sum(hidden_grad.astype(jnp.float32), axis=0)
    normed_grad = times_transposed(hidden_grad, weight_up)
    norm_pull = jax.vjp(layer_norm, values, norm_gain, norm_shift)[1]
    values_grad, gain_grad, shift_grad = norm_pull(normed_grad)
    return (
        residual_grad + values_grad,
        (normed, hidden_grad),
        up_bias_grad,
        (active, branch_grad),
        down_bias_grad,
        gain_grad,
        shift_grad,
    )


def heads_of(projected, clip_count, segment, rel_low):
    parts = [
        lax.all_to_all(part.reshape(clip_count, segment, -1), "seq", split_axis=2, concat_axis=1, tiled=True)
        for part in jnp.split(projected, 3, axis=1)
    ]
    merged, log_totals = attend(*parts, rel_low)
    attn_seq = lax.all_to_all(merged, "seq", split_axis=1, concat_axis=2, tiled=True)
    return attn_seq.reshape(clip_count * segment, -1), parts, log_totals


def heads_back(out_grad, parts, log_totals, clip_count, segment, rel_low):
    merged = lax.all_to_all(
        out_grad.reshape(clip_count, segment, -1), "seq", split_axis=2, concat_axis=1, tiled=True
    )
    *grads, table_parts = attend_back(*parts, merged, log_totals, rel_low)
    grads = [
        lax.all_to_all(grad, "seq", split_axis=1, concat_axis=2, tiled=True).reshape(clip_count * segment, -1)
        for grad in grads
    ]
    return jnp.concatenate(grads, axis=1), jnp.sum(table_parts, axis=0)


def spread_sums(factors, small):
    sums = []
    for left, right in factors:
        part = lax.psum_scatter(contract_rows(left, right).astype(jnp.bfloat16), "seq", scatter_dimension=1, tiled=True)
        part = lax.psum_scatter(part, "fsdp", scatter_dimension=0, tiled=True)
        sums.append(part.astype(jnp.float32))
    return (*sums, lax.psum(small, ("seq", "fsdp")))


def stacked(rows):
    lines = jnp.concatenate([row.reshape(-1, rows[0].shape[-1]) for row in rows])
    return jnp.pad(lines, ((0, -lines.shape[0] % 8), (0, 0)))


def body(
    tokens,
    cotangent,
    ffn1_up,
    ffn1_down,
    qkv_weight,
    out_weight,
    conv_in,
    conv_out,
    ffn2_up,
    ffn2_down,
    norm_gains,
    norm_biases,
    hidden_biases,
    model_biases,
    dw_kernel,
    rel_table,
):
    clip_count, segment, model_width = tokens.shape
    row_count = clip_count * segment
    rim_width = KERNEL - 1
    close = lax.axis_size("seq") == 2 and lax.axis_size("fsdp") == 16 and clip_count == 1
    low = jnp.bfloat16
    shards = [
        weight.astype(low)
        for weight in (ffn1_up, ffn1_down, qkv_weight, out_weight, conv_in, conv_out, ffn2_up, ffn2_down)
    ]
    if close:
        weights = gather_whole(shards, 0)
    else:
        weights = [lax.all_gather(shard, "fsdp", axis=0, tiled=True) for shard in shards]
    up_one, down_one, qkv_full, out_full, conv_first, conv_second, up_two, down_two = weights
    input_rows = tokens.reshape(row_count, model_width).astype(jnp.float32)
    branch_one, kept_one = feed_forward(
        input_rows,
        norm_gains[0],
        norm_biases[0],
        up_one,
        hidden_biases[0],
        down_one,
        model_biases[0],
    )
    after_one = input_rows + 0.5 * branch_one
    normed_attn = layer_norm(after_one, norm_gains[1], norm_biases[1]).astype(low)
    project_bias = jnp.concatenate([model_biases[1], jnp.zeros_like(model_biases[1]), model_biases[2]])
    projected = (product(normed_attn, qkv_full) + project_bias).astype(low)
    rel_low = padded_table(rel_table)
    if close:
        attn_rows, kept_heads, log_totals = attend_split(projected, rel_low, 1)
    else:
        attn_rows, kept_heads, log_totals = heads_of(projected, clip_count, segment, rel_low)
    after_two = after_one + product(attn_rows, out_full) + model_biases[3]
    normed_conv = layer_norm(after_two, norm_gains[2], norm_biases[2]).astype(low)
    gate_input = product(normed_conv, conv_first)
    glu_out = glu_function(gate_input).astype(low).reshape(clip_count, segment, model_width)
    glu_before = passed_along(glu_out[:, segment - rim_width :], "seq", 1)
    margin = jnp.zeros((clip_count, TAPS - rim_width, model_width), low)
    glu_wide = jnp.concatenate([margin, glu_before, glu_out], axis=1)
    mixed_flat = depthwise(glu_wide, dw_kernel).reshape(row_count, model_width)
    swished = conv_tail(mixed_flat, norm_gains[3], norm_biases[3]).astype(low)
    after_three = after_two + product(swished, conv_second)
    branch_two, kept_two = feed_forward(
        after_three,
        norm_gains[4],
        norm_biases[4],
        up_two,
        hidden_biases[1],
        down_two,
        model_biases[4],
    )
    after_four = after_three + 0.5 * branch_two
    final_rows, final_pull = jax.vjp(layer_norm, after_four, norm_gains[5], norm_biases[5])
    output = final_rows.astype(low).reshape(clip_count, segment, model_width)
    grad_four, gain_five, shift_five = final_pull(
        cotangent.reshape(row_count, model_width).astype(jnp.float32)
    )
    grad_three, up_two_factors, up_two_bias, down_two_factors, down_two_bias, gain_four, shift_four = (
        feed_backward(
            grad_four, after_three, kept_two, norm_gains[4], norm_biases[4], up_two, down_two
        )
    )
    conv_grad = grad_three.astype(low)
    swished_grad = times_transposed(conv_grad, conv_second)
    tail_pull = jax.vjp(conv_tail, mixed_flat, norm_gains[3], norm_biases[3])[1]
    mixed_grad, gain_three, shift_three = tail_pull(swished_grad)
    mixed_low = mixed_grad.astype(low).reshape(clip_count, segment, model_width)
    mixed_after = passed_along(mixed_low[:, 0:rim_width], "seq", -1)
    mixed_wide = jnp.concatenate([mixed_low, mixed_after, margin], axis=1)
    gate_grad, kernel_grad = depthwise_back(mixed_wide, glu_wide, dw_kernel, gate_input)
    conv_norm_pull = jax.vjp(layer_norm, after_two, norm_gains[2], norm_biases[2])[1]
    values_grad, gain_two, shift_two = conv_norm_pull(times_transposed(gate_grad, conv_first))
    grad_two = grad_three + values_grad
    sums_of = partial(scatter_sums, identity=2) if close else spread_sums
    later_small = stacked(
        [gain_two, gain_three, gain_four, gain_five, shift_two, shift_three, shift_four, shift_five]
        + [up_two_bias, down_two_bias, kernel_grad]
    )
    conv_first_sum, conv_second_sum, up_two_sum, down_two_sum, later_sum = sums_of(
        [(normed_conv, gate_grad), (swished, conv_grad), up_two_factors, down_two_factors],
        later_small,
    )
    attn_grad = grad_two.astype(low)
    out_bias_grad = jnp.sum(attn_grad.astype(jnp.float32), axis=0)
    merged_grad = times_transposed(attn_grad, out_full).astype(low)
    if close:
        projected_grad, table_parts = attend_back_split(merged_grad, kept_heads, log_totals, rel_low, 3)
    else:
        projected_grad, table_parts = heads_back(
            merged_grad, kept_heads, log_totals, clip_count, segment, rel_low
        )
    table_grad = jnp.sum(table_parts, axis=0).T[::-1][:BUCKETS]
    query_bias_grad = jnp.sum(projected_grad[:, :model_width].astype(jnp.float32), axis=0)
    value_bias_grad = jnp.sum(projected_grad[:, 2 * model_width :].astype(jnp.float32), axis=0)
    attn_norm_pull = jax.vjp(layer_norm, after_one, norm_gains[1], norm_biases[1])[1]
    values_grad, gain_one, shift_one = attn_norm_pull(times_transposed(projected_grad, qkv_full))
    grad_one = grad_two + values_grad
    grad_zero, up_one_factors, up_one_bias, down_one_factors, down_one_bias, gain_zero, shift_zero = (
        feed_backward(
            grad_one, input_rows, kept_one, norm_gains[0], norm_biases[0], up_one, down_one
        )
    )
    input_grad = grad_zero.astype(low).reshape(clip_count, segment, model_width)
    table_flat = table_grad.reshape(-1)
    table_rows = jnp.pad(table_flat, (0, -table_flat.size % model_width)).reshape(-1, model_width)
    early_small = stacked(
        [gain_zero, gain_one, shift_zero, shift_one, up_one_bias]
        + [down_one_bias, query_bias_grad, value_bias_grad, out_bias_grad, table_rows]
    )
    sums_of = partial(scatter_sums, identity=4) if close else spread_sums
    up_one_sum, down_one_sum, qkv_sum, out_sum, early_sum = sums_of(
        [up_one_factors, down_one_factors, (normed_attn, projected_grad), (attn_rows, attn_grad)],
        early_small,
    )
    hidden_rows = up_one_bias.size // model_width
    after_hidden = 4 + hidden_rows
    table_at = after_hidden + 4
    table_sum = early_sum[table_at : table_at + table_rows.shape[0]].reshape(-1)[: table_flat.size]
    later_hidden = 8 + hidden_rows
    return (
        output,
        input_grad,
        up_one_sum,
        down_one_sum,
        qkv_sum,
        out_sum,
        conv_first_sum,
        conv_second_sum,
        up_two_sum,
        down_two_sum,
        jnp.concatenate([early_sum[0:2], later_sum[0:4]]),
        jnp.concatenate([early_sum[2:4], later_sum[4:5]]),
        later_sum[5:8],
        jnp.stack([early_sum[4:after_hidden].reshape(-1), later_sum[8:later_hidden].reshape(-1)]),
        early_sum[after_hidden : after_hidden + 3],
        jnp.concatenate([early_sum[after_hidden + 3 : table_at], later_sum[later_hidden : later_hidden + 1]]),
        later_sum[later_hidden + 1 : later_hidden + 1 + KERNEL],
        table_sum.reshape(table_grad.shape),
    )


def solution(mesh):
    in_specs = (
        P("fsdp", "seq", None),
        P("fsdp", "seq", None),
        P("fsdp", None),
        P("fsdp", None),
        P("fsdp", None),
        P("fsdp", None),
        P("fsdp", None),
        P("fsdp", None),
        P("fsdp", None),
        P("fsdp", None),
        P(),
        P(),
        P(),
        P(),
        P(),
        P(),
    )
    out_specs = (
        P("fsdp", "seq", None),
        P("fsdp", "seq", None),
        P("fsdp", "seq"),
        P("fsdp", "seq"),
        P("fsdp", "seq"),
        P("fsdp", "seq"),
        P("fsdp", "seq"),
        P("fsdp", "seq"),
        P("fsdp", "seq"),
        P("fsdp", "seq"),
        P(),
        P(),
        P(),
        P(),
        P(),
        P(),
        P(),
        P(),
    )
    return jax.shard_map(body, mesh=mesh, in_specs=in_specs, out_specs=out_specs, check_vma=False)
```

```python
import functools
from functools import partial

import jax
import jax.numpy as jnp
from jax import lax
from jax.experimental import pallas as pl
from jax.experimental.pallas import tpu as pltpu
from jax.sharding import PartitionSpec as P

HEAD = 64
KERNEL = 31
LEFT = 64
RIGHT = 8
BUCKETS = 73


EPSILON = 1e-05


def passed_along(value, axis, by):
    length = lax.axis_size(axis)
    pairs = [(i, i + by) for i in range(length) if 0 <= i + by < length]
    return lax.ppermute(value, axis, pairs)


def layer_norm(values, norm_gain, norm_shift):
    center = values - jnp.mean(values, axis=-1, keepdims=True)
    spread = jnp.mean(center * center, axis=-1, keepdims=True)
    return center * lax.rsqrt(spread + EPSILON) * norm_gain + norm_shift


def product(former, latter):
    return jnp.dot(former, latter, preferred_element_type=jnp.float32)


def contract_rows(former, latter):
    return lax.dot_general(
        former, latter, (((0,), (0,)), ((), ())), preferred_element_type=jnp.float32
    )


def times_transposed(former, latter):
    return lax.dot_general(
        former, latter, (((1,), (1,)), ((), ())), preferred_element_type=jnp.float32
    )


def glu_function(gate_input):
    half_width = gate_input.shape[1] // 2
    return gate_input[:, :half_width] * jax.nn.sigmoid(gate_input[:, half_width:])


def conv_tail(mixed_rows, norm_gain, norm_shift):
    return jax.nn.silu(layer_norm(mixed_rows, norm_gain, norm_shift))


MESH = pl.DeviceIdType.MESH
PIECE = 256
LAG = 2
BLOCK = 512
WAIT = 2
OWN_SLOTS = 8
AWAY_SLOTS = 3


class Place:
    def __init__(self):
        self.x = lax.axis_index("seq")
        self.f = lax.axis_index("fsdp")
        self.c = lax.rem(self.f, 2)
        self.y = lax.rem(lax.div(self.f, 2), 2)
        self.z = lax.div(self.f, 4)

    def across(self):
        return (1 - self.x, self.f)

    def twin(self):
        return (self.x, self.f + 1 - 2 * self.c)

    def beside(self):
        return (self.x, self.f + 2 - 4 * self.y)

    def along(self, step):
        return (self.x, lax.rem(self.z + step, 4) * 4 + self.y * 2 + self.c)

    def greet(self):
        barrier = pltpu.get_barrier_semaphore()
        peers = [self.across(), self.twin(), self.beside()] + [self.along(s) for s in (1, 2, 3)]
        for peer in peers:
            pl.semaphore_signal(barrier, inc=1, device_id=peer, device_id_type=MESH)
        pl.semaphore_wait(barrier, len(peers))


def chunks_of(shapes, lines, crossing, piece):
    part, whole = crossing
    found = []
    for index, (rows, width) in enumerate(shapes):
        for line in range(0, rows, lines):
            for column in range(0, width // 2, piece):
                count = len(found)
                found.append((index, line, column, (count + 1) * part // whole > count * part // whole))
    return found


class Sent:
    def __init__(self, source, target, send_sem, recv_sem, device):
        self.parts = dict(src_ref=source, dst_ref=target, send_sem=send_sem, recv_sem=recv_sem, device_id=device, device_id_type=MESH)

    def start(self):
        pltpu.make_async_remote_copy(**self.parts).start()

    def wait_recv(self):
        pltpu.make_async_remote_copy(**self.parts).wait_recv()

    def wait_send(self):
        pltpu.make_async_remote_copy(**self.parts).wait_send()


class Near:
    def __init__(self, source, target, sem):
        self.parts = (source, target, sem)

    def start(self):
        pltpu.make_async_copy(*self.parts).start()

    def wait(self):
        pltpu.make_async_copy(*self.parts).wait()


class Gather:
    def __init__(self, me, shards, wholes, chunks, lines, sems):
        self.me, self.shards, self.wholes, self.chunks, self.lines = me, shards, wholes, chunks, lines
        (self.own_sem, self.z_send, self.z_recv, self.y_send, self.y_recv, self.x_send, self.x_recv, self.c_send, self.c_recv) = sems
        self.steps = len(chunks) + 3 * LAG
        self.number = 0
        self.whole = set()

    @staticmethod
    def scratch(total):
        dma = pltpu.SemaphoreType.DMA
        return [
            dma((total, 2)), dma((total, 2, 3)), dma((total, 2, 3)), dma((total, 2)), dma((total, 2)),
            dma((total,)), dma((total,)), dma((total, 2)), dma((total, 2)),
        ]

    def halves(self, chunk):
        index, line, column, early = chunk
        half = self.shards[index].shape[1] // 2
        if early:
            return [pl.ds(pl.multiple_of(self.me.x * half + column, PIECE), PIECE)]
        return [pl.ds(column, PIECE), pl.ds(half + column, PIECE)]

    def both(self, chunk):
        half = self.shards[chunk[0]].shape[1] // 2
        return [pl.ds(chunk[2], PIECE), pl.ds(half + chunk[2], PIECE)]

    def make(self, t, kind):
        index, line, column, early = self.chunks[t]
        shard, whole, rows, me = self.shards[index], self.wholes[index], pl.ds(line, self.lines), self.me
        halves = self.halves(self.chunks[t])
        if kind == "own":
            return [
                Near(shard.at[rows, cols], whole.at[me.z, me.y, me.c, rows, cols], self.own_sem.at[t, j])
                for j, cols in enumerate(halves)
            ]
        if kind == "z":
            return [
                Sent(shard.at[rows, cols], whole.at[me.z, me.y, me.c, rows, cols], self.z_send.at[t, j, s - 1], self.z_recv.at[t, j, s - 1], me.along(s))
                for j, cols in enumerate(halves)
                for s in (1, 2, 3)
            ]
        if kind == "y":
            views = [whole.at[:, me.y, me.c, rows, cols] for cols in halves]
            return [Sent(view, view, self.y_send.at[t, j], self.y_recv.at[t, j], me.beside()) for j, view in enumerate(views)]
        if kind == "x":
            views = [whole.at[:, :, me.c, rows, halves[0]]] if early else []
            return [Sent(view, view, self.x_send.at[t], self.x_recv.at[t], me.across()) for view in views]
        views = [whole.at[:, :, me.c, rows, cols] for cols in self.both(self.chunks[t])]
        return [Sent(view, view, self.c_send.at[t, j], self.c_recv.at[t, j], me.twin()) for j, view in enumerate(views)]

    def start(self, t, kind):
        for copy in self.make(t, kind):
            copy.start()

    def arrive(self, t, kind):
        for copy in self.make(t, kind):
            copy.wait_recv()

    def first(self, t):
        self.start(t, "own")
        self.start(t, "z")

    def second(self, t):
        for copy in self.make(t, "own"):
            copy.wait()
        self.arrive(t, "z")
        self.start(t, "y")

    def third(self, t):
        self.arrive(t, "y")
        self.start(t, "x")

    def fourth(self, t):
        self.arrive(t, "x")
        self.start(t, "c")

    def step(self, number):
        for stage, phase in reversed(list(enumerate((self.first, self.second, self.third, self.fourth)))):
            if 0 <= number - LAG * stage < len(self.chunks):
                phase(number - LAG * stage)

    def run(self, number):
        while self.number < min(number, self.steps):
            self.step(self.number)
            self.number += 1

    def landed(self, t):
        if t not in self.whole:
            self.arrive(t, "c")
            self.whole.add(t)

    def finish(self):
        for t in range(len(self.chunks)):
            self.landed(t)
            for kind in "zyxc":
                for copy in self.make(t, kind):
                    copy.wait_send()


def gather_plan(shards, crossing):
    shapes = [shard.shape for shard in shards]
    lines = min(rows for rows, _ in shapes)
    wholes = [jax.ShapeDtypeStruct((4, 2, 2, *shape), jnp.bfloat16) for shape in shapes]
    return wholes, chunks_of(shapes, lines, crossing, PIECE), lines


def flat(wholes):
    return [whole.reshape(-1, whole.shape[-1]) for whole in wholes]


class Scatter:
    def __init__(self, me, lefts, rights, small, outs, small_out, chunks, lines, scratch):
        self.me, self.lefts, self.rights, self.small, self.outs, self.small_out = me, lefts, rights, small, outs, small_out
        self.chunks, self.lines = chunks, lines
        (self.strips, self.cols, self.turned, self.own, self.away, self.core_in, self.early_in, self.late_in, self.y_in, self.z_in,
         self.end_in, self.done, self.strip_sem, self.cols_sem, self.done_sem,
         self.c_send, self.c_recv, self.x_send, self.x_recv, self.y_send, self.y_recv, self.z_send, self.z_recv,
         self.small_held, self.small_in, self.small_z, self.small_send, self.small_recv, self.small_z_send, self.small_z_recv) = scratch
        self.order = [sum(other[3] == chunk[3] for other in chunks[:t]) for t, chunk in enumerate(chunks)]
        self.steps = len(chunks) + 1 + 4 * WAIT

    @staticmethod
    def scratch(chunks, lines, tokens, small):
        dma, low, total = pltpu.SemaphoreType.DMA, jnp.bfloat16, len(chunks)
        early = sum(chunk[3] for chunk in chunks)
        late = total - early
        return [
            pltpu.VMEM((tokens, 32 * lines), low),
            pltpu.VMEM((2, 2, tokens, BLOCK), low),
            pltpu.VMEM((2, 16 * lines, tokens), low),
            pltpu.VMEM((OWN_SLOTS, 2, 4, 2, lines, BLOCK), low),
            pltpu.VMEM((AWAY_SLOTS, 2, 4, 2, lines, BLOCK), low),
            pltpu.VMEM((total, 2, 4, 2, lines, BLOCK), low),
            pltpu.VMEM((early, 4, 2, lines, BLOCK), low),
            pltpu.VMEM((late, 2, 4, lines, BLOCK), low),
            pltpu.VMEM((early, 4, lines, BLOCK), low),
            pltpu.VMEM((late, 3, 2, lines, BLOCK), low),
            pltpu.VMEM((total, 3, lines, BLOCK), low),
            pltpu.VMEM((total, lines, BLOCK), jnp.float32),
            dma((16,)), dma((2, 2)), dma((total,)),
            dma((total, 2)), dma((total, 2)), dma((total,)), dma((total,)),
            dma((total,)), dma((total,)), dma((total, 3)), dma((total, 3)),
            pltpu.VMEM((4, *small), jnp.float32), pltpu.VMEM((3, *small), jnp.float32), pltpu.VMEM((4, *small), jnp.float32),
            dma((3,)), dma((3,)), dma((3,)), dma((3,)),
        ]

    def columns(self, t, j):
        index, line, column, early = self.chunks[t]
        return pl.ds(j * (self.rights[index].shape[1] // 2) + column, BLOCK)

    def turns(self, t):
        index, line, column, early = self.chunks[t]
        if self.lefts[index].shape[1] > 16 * self.lines:
            return column == 0 and line % (2 * self.lines) == 0, line // self.lines % 2
        return column == 0, 0

    def loads(self, t):
        index, line, column, early = self.chunks[t]
        left, wide = self.lefts[index], 2 * self.lines
        copies = [Near(self.rights[index].at[:, self.columns(t, j)], self.cols.at[t % 2, j], self.cols_sem.at[t % 2, j]) for j in range(2)]
        if self.turns(t)[0]:
            rows = left.shape[1] // 16
            if rows > self.lines:
                copies += [
                    Near(left.at[:, pl.ds(i * rows + line, wide)], self.strips.at[:, pl.ds(i * wide, wide)], self.strip_sem.at[i])
                    for i in range(16)
                ]
            else:
                copies.append(Near(left, self.strips.at[:, pl.ds(0, 8 * wide)], self.strip_sem.at[0]))
        return copies

    def load(self, t):
        for copy in self.loads(t):
            copy.start()

    def turn(self, t):
        lines, me = self.lines, self.me
        left = self.lefts[self.chunks[t][0]]

        def place(core, block):
            return pl.ds(pl.multiple_of((lax.rem(core + me.c, 2) * 8 + block) * lines, lines), lines)

        if left.shape[1] > 16 * lines:

            @pl.loop(0, 16)
            def _(i):
                block = jnp.transpose(self.strips[:, pl.ds(pl.multiple_of(i * 2 * lines, 2 * lines), 2 * lines)])
                rows = place(lax.rem(i, 2), lax.div(i, 2))
                self.turned[0, rows, :] = block[:lines]
                self.turned[1, rows, :] = block[lines:]

        else:

            @pl.loop(0, 8)
            def _(i):
                block = jnp.transpose(self.strips[:, pl.ds(pl.multiple_of(i * 2 * lines, 2 * lines), 2 * lines)])
                self.turned[0, place(0, i), :] = block[:lines]
                self.turned[0, place(1, i), :] = block[lines:]

    def make(self, t, kind):
        index, line, column, early = self.chunks[t]
        me, own, slot, order = self.me, self.own, t % OWN_SLOTS, self.order[t]
        if kind == "c":
            return [
                Sent(self.away.at[t % AWAY_SLOTS, j], self.core_in.at[t, j], self.c_send.at[t, j], self.c_recv.at[t, j], me.twin())
                for j in range(2)
            ]
        if kind == "x":
            source, target = (
                (own.at[slot, 1 - me.x], self.early_in.at[order]) if early
                else (own.at[slot, 1 - me.x, me.z, me.y], self.end_in.at[t, 0])
            )
            return [Sent(source, target, self.x_send.at[t], self.x_recv.at[t], me.across())]
        if kind == "y":
            source, target = (
                (own.at[slot, me.x, :, 1 - me.y], self.y_in.at[order]) if early
                else (own.at[slot, :, :, 1 - me.y], self.late_in.at[order])
            )
            return [Sent(source, target, self.y_send.at[t], self.y_recv.at[t], me.beside())]
        copies = []
        for s in (1, 2, 3):
            z = lax.rem(me.z + s, 4)
            source, target = (
                (own.at[slot, me.x, z, me.y], self.end_in.at[t, s - 1]) if early
                else (own.at[slot, :, z, me.y], self.z_in.at[order, s - 1])
            )
            copies.append(Sent(source, target, self.z_send.at[t, s - 1], self.z_recv.at[t, s - 1], me.along(s)))
        return copies

    def finished(self, t):
        index, line, column, early = self.chunks[t]
        return Near(self.done.at[t], self.outs[index].at[pl.ds(line, self.lines), pl.ds(column, BLOCK)], self.done_sem.at[t])

    def make_small(self, stage):
        me = self.me
        if stage < 3:
            peer = (me.twin, me.across, me.beside)[stage]()
            return [Sent(self.small_held.at[stage], self.small_in.at[stage], self.small_send.at[stage], self.small_recv.at[stage], peer)]
        return [
            Sent(self.small_held.at[3], self.small_z.at[me.z], self.small_z_send.at[s - 1], self.small_z_recv.at[s - 1], me.along(s))
            for s in (1, 2, 3)
        ]

    def start(self, t, kind):
        for copy in self.make(t, kind):
            copy.start()

    def arrive(self, t, kind):
        for copy in self.make(t, kind):
            copy.wait_recv()

    def leave(self, t, kinds):
        for kind in kinds:
            for copy in self.make(t, kind):
                copy.wait_send()

    def first(self, t):
        lines = self.lines
        for copy in self.loads(t):
            copy.wait()
        fresh, which = self.turns(t)
        if fresh:
            self.turn(t)
        if t >= AWAY_SLOTS:
            self.leave(t - AWAY_SLOTS, "c")
        if t >= OWN_SLOTS:
            self.leave(t - OWN_SLOTS, "zyx")
        for other in (1, 0):
            target, slot = (self.own, t % OWN_SLOTS) if other == 0 else (self.away, t % AWAY_SLOTS)
            for j in range(2):

                @pl.loop(0, 2)
                def _(pair):
                    rows = pl.ds(pl.multiple_of((other * 2 + pair) * 4 * lines, 4 * lines), 4 * lines)
                    part = nn(self.turned[which, rows, :], self.cols[t % 2, j]).astype(jnp.bfloat16)
                    for z in range(2):
                        for y in range(2):
                            target[slot, j, 2 * pair + z, y] = part[(2 * z + y) * lines : (2 * z + y + 1) * lines]

                if other == 1:
                    self.make(t, "c")[j].start()

    def second(self, t):
        early, slot, own = self.chunks[t][3], t % OWN_SLOTS, self.own
        self.arrive(t, "c")
        for j in range(2):
            for z in range(4):
                own[slot, j, z] = sums(own[slot, j, z], self.core_in[t, j, z])
        self.start(t, "x" if early else "y")

    def third(self, t):
        early, slot, me, own, order = self.chunks[t][3], t % OWN_SLOTS, self.me, self.own, self.order[t]
        if early:
            self.arrive(t, "x")
            for z in range(4):
                own[slot, me.x, z] = sums(own[slot, me.x, z], self.early_in[order, z])
            self.start(t, "y")
        else:
            self.arrive(t, "y")
            for j in range(2):
                for z in range(4):
                    own[slot, j, z, me.y] = sums(own[slot, j, z, me.y], self.late_in[order, j, z])
            self.start(t, "z")

    def fourth(self, t):
        early, slot, me, own, order = self.chunks[t][3], t % OWN_SLOTS, self.me, self.own, self.order[t]
        if early:
            self.arrive(t, "y")
            for z in range(4):
                own[slot, me.x, z, me.y] = sums(own[slot, me.x, z, me.y], self.y_in[order, z])
            self.start(t, "z")
        else:
            self.arrive(t, "z")
            for j in range(2):
                value = own[slot, j, me.z, me.y].astype(jnp.float32)
                for s in range(3):
                    value = value + self.z_in[order, s, j].astype(jnp.float32)
                own[slot, j, me.z, me.y] = value.astype(jnp.bfloat16)
            self.start(t, "x")

    def fifth(self, t):
        early, slot, me = self.chunks[t][3], t % OWN_SLOTS, self.me
        self.arrive(t, "z" if early else "x")
        value = self.own[slot, me.x, me.z, me.y].astype(jnp.float32)
        for s in range(3 if early else 1):
            value = value + self.end_in[t, s].astype(jnp.float32)
        self.done[t] = value
        self.finished(t).start()

    def small_step(self, stage):
        if stage == 0:
            self.small_held[0] = self.small[...]
        else:
            self.make_small(stage - 1)[0].wait_recv()
            self.small_held[stage] = self.small_held[stage - 1] + self.small_in[stage - 1]
        if stage == 3:
            self.small_z[self.me.z] = self.small_held[3]
        for copy in self.make_small(stage):
            copy.start()

    def step(self, number):
        phases = ((1, self.first), (1 + WAIT, self.second), (1 + 2 * WAIT, self.third), (1 + 3 * WAIT, self.fourth), (1 + 4 * WAIT, self.fifth))
        for lag, phase in reversed(((0, self.load), *phases)):
            if 0 <= number - lag < len(self.chunks):
                phase(number - lag)
        if number % WAIT == 0 and number // WAIT < 4:
            self.small_step(number // WAIT)

    def finish(self):
        for copy in self.make_small(3):
            copy.wait_recv()
        for stage in range(4):
            for copy in self.make_small(stage):
                copy.wait_send()
        self.small_out[...] = (self.small_z[0] + self.small_z[1]) + (self.small_z[2] + self.small_z[3])
        total = len(self.chunks)
        for t in range(total):
            self.finished(t).wait()
            if t + AWAY_SLOTS >= total:
                self.leave(t, "c")
            if t + OWN_SLOTS >= total:
                self.leave(t, "zyx")


def sums(former, latter):
    return (former.astype(jnp.float32) + latter.astype(jnp.float32)).astype(jnp.bfloat16)


def scatter_kernel(count, chunks, lines, *refs):
    me = Place()
    me.greet()
    scatter = Scatter(
        me, refs[:count], refs[count : 2 * count], refs[2 * count], refs[2 * count + 1 : 3 * count + 1], refs[3 * count + 1],
        chunks, lines, refs[3 * count + 2 :],
    )
    for number in range(scatter.steps):
        scatter.step(number)
    scatter.finish()


def scatter_plan(factors, small, crossing):
    shapes = [(left.shape[1] // 16, right.shape[1]) for left, right in factors]
    lines = min(rows for rows, _ in shapes)
    anywhere, near = pl.BlockSpec(memory_space=pl.ANY), pl.BlockSpec(memory_space=pltpu.VMEM)
    outs = [jax.ShapeDtypeStruct((rows, width // 2), jnp.float32) for rows, width in shapes]
    outs.append(jax.ShapeDtypeStruct(small.shape, jnp.float32))
    chunks = chunks_of(shapes, lines, crossing, BLOCK)
    count = len(factors)
    operands = [left for left, _ in factors] + [right for _, right in factors] + [small]
    in_specs = [anywhere] * (2 * count) + [near]
    scratch = Scatter.scratch(chunks, lines, factors[0][0].shape[0], small.shape)
    return operands, in_specs, outs, [anywhere] * count + [near], scratch, chunks, lines


def scatter_sums(factors, small, identity):
    operands, in_specs, outs, out_specs, scratch, chunks, lines = scatter_plan(factors, small, (2, 3))
    return pl.pallas_call(
        functools.partial(scatter_kernel, len(factors), chunks, lines),
        in_specs=in_specs,
        out_specs=out_specs,
        out_shape=outs,
        scratch_shapes=scratch,
        compiler_params=pltpu.CompilerParams(collective_id=identity, has_side_effects=True, vmem_limit_bytes=60 << 20),
        name="scatter_sums",
    )(*operands)


PAIR = 2
LANES = 128
FWD_ROWS = 256
BACK_ROWS = 256


def nt(former, latter):
    return lax.dot_general(former, latter, (((1,), (1,)), ((), ())), preferred_element_type=jnp.float32)


def nn(former, latter):
    return lax.dot_general(former, latter, (((1,), (0,)), ((), ())), preferred_element_type=jnp.float32)


def window_of(start, rows, length):
    low, high = start - LANES, start + rows + LANES
    return max(low, 0), min(high, length), max(low, 0) - low


def window_buckets(rows):
    width = rows + 2 * LANES
    places = lax.broadcasted_iota(jnp.int32, (rows, width), 1)
    lines = lax.broadcasted_iota(jnp.int32, (rows, width), 0)
    return places - lines - (LANES - LEFT)


def biased_scores(scores, position, start, rows, length):
    width = rows + 2 * LANES
    low, high, skip = window_of(start, rows, length)
    wide = jnp.concatenate([position, jnp.zeros((rows, width - LANES), jnp.float32)], axis=1)
    band = pltpu.roll(wide, LANES - LEFT, 1, stride=1, stride_axis=0)
    first, last = position[:, 0:1], position[:, BUCKETS - 1 : BUCKETS]
    bucket = window_buckets(rows)
    band = jnp.where(bucket <= 0, first, jnp.where(bucket >= BUCKETS - 1, last, band))
    pieces = []
    if low > 0:
        pieces.append(scores[:, :low] + first)
    pieces.append(scores[:, low:high] + band[:, skip : skip + high - low])
    if high < length:
        pieces.append(scores[:, high:] + last)
    return pieces[0] if len(pieces) == 1 else jnp.concatenate(pieces, axis=1)


def bucket_sums(score_grad, mirror, start, rows, length):
    width = rows + 2 * LANES
    low, high, skip = window_of(start, rows, length)
    inner = score_grad[:, low:high]
    pieces = []
    if skip > 0:
        pieces.append(jnp.zeros((rows, skip), jnp.float32))
    pieces.append(inner)
    if skip + high - low < width:
        pieces.append(jnp.zeros((rows, width - skip - high + low), jnp.float32))
    wide = pieces[0] if len(pieces) == 1 else jnp.concatenate(pieces, axis=1)
    bucket = window_buckets(rows)
    first = jnp.sum(jnp.where(bucket <= 0, wide, 0.0), axis=1, keepdims=True)
    last = jnp.sum(jnp.where(bucket >= BUCKETS - 1, wide, 0.0), axis=1, keepdims=True)
    if low > 0:
        first = first + jnp.sum(score_grad[:, :low], axis=1, keepdims=True)
    if high < length:
        last = last + jnp.sum(score_grad[:, high:], axis=1, keepdims=True)
    turned = nn(wide.astype(jnp.bfloat16), mirror)
    band = pltpu.roll(turned, (LANES + LANES - LEFT) % width, 1, stride=1, stride_axis=0)[:, :LANES]
    bucket = LANES - 1 - lax.broadcasted_iota(jnp.int32, (rows, LANES), 1)
    return jnp.where(bucket == 0, first, jnp.where(bucket == BUCKETS - 1, last, jnp.where(bucket < BUCKETS, band, 0.0)))


def mirror_of(width):
    lines = lax.broadcasted_iota(jnp.int32, (width, width), 0)
    places = lax.broadcasted_iota(jnp.int32, (width, width), 1)
    return jnp.where(lines + places == width - 1, 1.0, 0.0).astype(jnp.bfloat16)


def attend_pair(q_ref, k_ref, v_ref, rel_ref, out_ref, log_ref, between=lambda block: None):
    length = q_ref.shape[0]
    rows = min(FWD_ROWS, length)
    scale = HEAD ** (-0.5)
    rel = rel_ref[...]
    for start in range(0, length, rows):
        outs, logs = [], []
        for h in range(PAIR):
            lanes = slice(h * HEAD, (h + 1) * HEAD)
            query = q_ref[start : start + rows, lanes] * scale
            scores = nt(query, k_ref[:, lanes])
            scores = biased_scores(scores, nt(query, rel), start, rows, length)
            highest = jnp.max(scores, axis=1, keepdims=True)
            weights = jnp.exp(scores - highest)
            total = jnp.sum(weights, axis=1, keepdims=True)
            outs.append(nn(weights.astype(jnp.bfloat16), v_ref[:, lanes]) / total)
            logs.append(highest + jnp.log(total))
        out_ref[start : start + rows, :] = jnp.concatenate(outs, axis=1).astype(jnp.bfloat16)
        log_ref[start : start + rows, :] = jnp.concatenate(logs, axis=1)
        between(start // rows)


def attend_back_pair(
    q_ref, k_ref, v_ref, do_ref, log_ref, rel_ref, back_ref, mirror_ref, dq_ref, dk_ref, dv_ref, table_ref, dkt, dvt, q_turned, do_turned,
    between=lambda block: None,
):
    length = q_ref.shape[0]
    rows = min(BACK_ROWS, length)
    scale = HEAD ** (-0.5)
    q_turned[...] = (jnp.transpose(q_ref[...].astype(jnp.float32)) * scale).astype(jnp.bfloat16)
    do_turned[...] = jnp.transpose(do_ref[...].astype(jnp.float32)).astype(jnp.bfloat16)
    table_ref[...] = jnp.zeros((HEAD, LANES), jnp.float32)
    for start in range(0, length, rows):
        span = slice(start, start + rows)
        parts = []
        for h in range(PAIR):
            lanes = slice(h * HEAD, (h + 1) * HEAD)
            query = q_ref[span, lanes] * scale
            scores = nt(query, k_ref[:, lanes])
            scores = biased_scores(scores, nt(query, rel_ref[...]), start, rows, length)
            weights = jnp.exp(scores - log_ref[span, h : h + 1])
            low_weights = weights.astype(jnp.bfloat16)
            grads = nt(do_ref[span, lanes], v_ref[:, lanes])
            both = weights * grads
            delta = jnp.sum(both, axis=1, keepdims=True)
            score_grad = (both - weights * delta).astype(jnp.bfloat16)
            value_part = nn(do_turned[lanes, span], low_weights)
            key_part = nn(q_turned[lanes, span], score_grad)
            if start == 0:
                dvt[lanes, :] = value_part
                dkt[lanes, :] = key_part
            else:
                dvt[lanes, :] += value_part
                dkt[lanes, :] += key_part
            bucket = bucket_sums(score_grad.astype(jnp.float32), mirror_ref[...], start, rows, length)
            high = bucket.astype(jnp.bfloat16)
            rest = (bucket - high.astype(jnp.float32)).astype(jnp.bfloat16)
            parts.append((nn(score_grad, k_ref[:, lanes]) + nn(high, back_ref[...]) + nn(rest, back_ref[...])) * scale)
            table_ref[...] += nn(q_turned[lanes, span], high) + nn(q_turned[lanes, span], rest)
        dq_ref[span, :] = jnp.concatenate(parts, axis=1).astype(jnp.bfloat16)
        between(start // rows)
    dk_ref[...] = jnp.transpose(dkt[...]).astype(jnp.bfloat16)
    dv_ref[...] = jnp.transpose(dvt[...]).astype(jnp.bfloat16)


def attend_kernel(q_ref, k_ref, v_ref, rel_ref, out_ref, log_ref):
    attend_pair(q_ref.at[0], k_ref.at[0], v_ref.at[0], rel_ref, out_ref.at[0], log_ref.at[0, 0])


def attend_back_kernel(
    q_ref, k_ref, v_ref, do_ref, log_ref, rel_ref, back_ref, mirror_ref, dq_ref, dk_ref, dv_ref, table_ref, dkt, dvt, q_turned, do_turned
):
    attend_back_pair(
        q_ref.at[0], k_ref.at[0], v_ref.at[0], do_ref.at[0], log_ref.at[0, 0], rel_ref, back_ref, mirror_ref,
        dq_ref.at[0], dk_ref.at[0], dv_ref.at[0], table_ref.at[0, 0], dkt, dvt, q_turned, do_turned,
    )


def width_of(length):
    return min(BACK_ROWS, length) + 2 * LANES


def head_block(length):
    return pl.BlockSpec((1, length, PAIR * HEAD), lambda i, j: (i, 0, j))


def padded_table(rel_table):
    return jnp.pad(rel_table.astype(jnp.bfloat16), ((0, LANES - BUCKETS), (0, 0)))


def attend(query, key, value, rel_low):
    clips, length, width = query.shape
    pairs = width // (PAIR * HEAD)
    block = head_block(length)
    return pl.pallas_call(
        attend_kernel,
        grid=(clips, pairs),
        in_specs=[block, block, block, pl.BlockSpec((LANES, HEAD), lambda i, j: (0, 0))],
        out_specs=[block, pl.BlockSpec((1, 1, length, PAIR), lambda i, j: (i, j, 0, 0))],
        out_shape=[
            jax.ShapeDtypeStruct(query.shape, jnp.bfloat16),
            jax.ShapeDtypeStruct((clips, pairs, length, PAIR), jnp.float32),
        ],
        compiler_params=pltpu.CompilerParams(vmem_limit_bytes=48 << 20),
        cost_estimate=pl.CostEstimate(flops=4 * clips * width * length * length * 4, bytes_accessed=8 * query.size, transcendentals=clips * pairs * PAIR * length * length),
        name="attend",
    )(query, key, value, rel_low)


def attend_back(query, key, value, out_grad, logs, rel_low):
    clips, length, width = query.shape
    pairs = width // (PAIR * HEAD)
    block = head_block(length)
    shape = jax.ShapeDtypeStruct(query.shape, jnp.bfloat16)
    return pl.pallas_call(
        attend_back_kernel,
        grid=(clips, pairs),
        in_specs=[
            block, block, block, block,
            pl.BlockSpec((1, 1, length, PAIR), lambda i, j: (i, j, 0, 0)),
            pl.BlockSpec((LANES, HEAD), lambda i, j: (0, 0)),
            pl.BlockSpec((LANES, HEAD), lambda i, j: (0, 0)),
            pl.BlockSpec((width_of(length),) * 2, lambda i, j: (0, 0)),
        ],
        out_specs=[block, block, block, pl.BlockSpec((1, 1, HEAD, LANES), lambda i, j: (i, j, 0, 0))],
        out_shape=[shape, shape, shape, jax.ShapeDtypeStruct((clips, pairs, HEAD, LANES), jnp.float32)],
        scratch_shapes=[pltpu.VMEM((PAIR * HEAD, length), jnp.float32)] * 2 + [pltpu.VMEM((PAIR * HEAD, length), jnp.bfloat16)] * 2,
        compiler_params=pltpu.CompilerParams(vmem_limit_bytes=48 << 20),
        cost_estimate=pl.CostEstimate(flops=10 * clips * width * length * length * 4, bytes_accessed=14 * query.size, transcendentals=clips * pairs * PAIR * length * length),
        name="attend_back",
    )(query, key, value, out_grad, logs, rel_low, rel_low[::-1], mirror_of(width_of(length)))


def strip(index):
    return pl.ds(pl.multiple_of(index * LANES, LANES), LANES)


def attend_back_split_kernel(
    pairs, count, chunks, lines, do_ref, kept_ref, log_ref, rel_ref, back_ref, mirror_ref, *refs
):
    lefts, rights, small = refs[:count], refs[count : 2 * count], refs[2 * count]
    dp_ref, table_ref = refs[2 * count + 1 : 2 * count + 3]
    sums_refs, refs = refs[2 * count + 3 : 3 * count + 4], refs[3 * count + 4 :]
    grads, qkv, outs, dkt, dvt, q_turned, do_turned, own_sem, send_sem, recv_sem, kept_sem, out_sem, back_send, back_recv = refs[:14]
    me = Place()
    scatter = Scatter(me, lefts, rights, small, sums_refs[:count], sums_refs[count], chunks, lines, refs[14:])
    blocks = kept_ref.shape[2] // min(BACK_ROWS, kept_ref.shape[2])
    step = pl.program_id(0)
    segment = do_ref.shape[0]
    mine, theirs = pl.ds(me.x * segment, segment), pl.ds((1 - me.x) * segment, segment)

    def leaving(i):
        return Sent(do_ref.at[:, strip((1 - me.x) * pairs + i)], grads.at[i, mine, :], send_sem.at[i], recv_sem.at[i], me.across())

    def staying(i):
        return (
            pltpu.make_async_copy(do_ref.at[:, strip(me.x * pairs + i)], grads.at[i, mine, :], own_sem.at[i]),
            pltpu.make_async_copy(kept_ref.at[i], qkv.at[i], kept_sem.at[i]),
        )

    def returns(i, part):
        there = dp_ref.at[:, strip((2 * part + me.x) * pairs + i)]
        return (
            Sent(outs.at[i, part, theirs, :], there, back_send.at[i, part], back_recv.at[i, part], me.across()),
            pltpu.make_async_copy(outs.at[i, part, mine, :], there, out_sem.at[i, part]),
        )

    @pl.when(step == 0)
    def _():
        me.greet()
        for i in range(pairs):
            leaving(i).start()
            for copy in staying(i):
                copy.start()
        scatter.step(0)
        scatter.step(1)

    def between(block):
        for i in range(pairs):
            if 2 + i * blocks + block < scatter.steps:

                @pl.when(step == i)
                def _():
                    scatter.step(2 + i * blocks + block)

    leaving(step).wait_recv()
    for copy in staying(step):
        copy.wait()
    attend_back_pair(
        qkv.at[step, 0], qkv.at[step, 1], qkv.at[step, 2], grads.at[step], log_ref.at[0], rel_ref, back_ref, mirror_ref,
        outs.at[step, 0], outs.at[step, 1], outs.at[step, 2], table_ref.at[0], dkt, dvt, q_turned, do_turned, between,
    )
    for part in range(3):
        for copy in returns(step, part):
            copy.start()

    @pl.when(step == pairs - 1)
    def _():
        for number in range(2 + pairs * blocks, scatter.steps):
            scatter.step(number)
        scatter.finish()
        for i in range(pairs):
            leaving(i).wait_send()
            for part in range(3):
                sent, own = returns(i, part)
                sent.wait_send()
                sent.wait_recv()
                own.wait()


def attend_back_split(out_grad, kept, logs, rel_low, factors, small, identity):
    segment, width = out_grad.shape
    pairs, _, length, _ = kept.shape
    operands, more_specs, outs, outs_specs, scratch, chunks, lines = scatter_plan(factors, small, (4, 11))
    dma, anywhere = pltpu.SemaphoreType.DMA, pl.BlockSpec(memory_space=pl.ANY)
    table = pl.BlockSpec((LANES, HEAD), lambda i: (0, 0))
    return pl.pallas_call(
        functools.partial(attend_back_split_kernel, pairs, len(factors), chunks, lines),
        grid=(pairs,),
        in_specs=[
            anywhere, anywhere, pl.BlockSpec((1, length, PAIR), lambda i: (i, 0, 0)), table, table,
            pl.BlockSpec((width_of(length),) * 2, lambda i: (0, 0), pipeline_mode=pl.Buffered(1)), *more_specs,
        ],
        out_specs=[anywhere, pl.BlockSpec((1, HEAD, LANES), lambda i: (i, 0, 0)), *outs_specs],
        out_shape=[
            jax.ShapeDtypeStruct((segment, 3 * width), jnp.bfloat16),
            jax.ShapeDtypeStruct((pairs, HEAD, LANES), jnp.float32),
            *outs,
        ],
        scratch_shapes=[
            pltpu.VMEM((pairs, length, LANES), jnp.bfloat16),
            pltpu.VMEM((pairs, 3, length, LANES), jnp.bfloat16),
            pltpu.VMEM((pairs, 3, length, LANES), jnp.bfloat16),
            pltpu.VMEM((LANES, length), jnp.float32),
            pltpu.VMEM((LANES, length), jnp.float32),
            pltpu.VMEM((LANES, length), jnp.bfloat16),
            pltpu.VMEM((LANES, length), jnp.bfloat16),
            dma((pairs,)), dma((pairs,)), dma((pairs,)), dma((pairs,)), dma((pairs, 3)), dma((pairs, 3)), dma((pairs, 3)),
            *scratch,
        ],
        compiler_params=pltpu.CompilerParams(collective_id=identity, has_side_effects=True, vmem_limit_bytes=62 << 20),
        name="attend_back_split",
    )(out_grad, kept, logs, rel_low, rel_low[::-1], mirror_of(width_of(length)), *operands)


def normed_rows(values, gain, shift):
    center = values - jnp.mean(values, axis=1, keepdims=True)
    spread = jnp.mean(center * center, axis=1, keepdims=True)
    return center * lax.rsqrt(spread + EPSILON) * gain + shift


def front_kernel(
    pairs, count, chunks, lines, tokens_ref, rel_ref, gains_ref, shifts_ref, hidden_bias_ref, model_bias_ref, *refs
):
    shards, refs = refs[:count], refs[count:]
    normed_ref, hidden_ref, active_ref, after_ref, attn_ref, out_ref, kept_ref, log_ref = refs[:8]
    wholes, refs = refs[8 : 8 + count], refs[8 + count :]
    (branch, projected, strips, blocks, qkv, outs, strip_sem, block_sem,
     own_sem, send_sem, recv_sem, kept_sem, out_sem, back_send, back_recv) = refs[:15]
    me = Place()
    gather = Gather(me, shards, wholes, chunks, lines, refs[15:])
    me.greet()
    segment, width = tokens_ref.shape
    low = jnp.bfloat16
    ROWS = 128

    def chunks_for(index):
        return [t for t, chunk in enumerate(chunks) if chunk[0] == index]

    def whole_by_now(t):
        gather.run(t + 3 * LAG + 1)
        gather.landed(t)

    def strip_copies(t):
        index, line, column, early = chunks[t]
        half = shards[index].shape[1] // 2
        return [
            Near(wholes[index].at[:, :, :, :, pl.ds(j * half + column, PIECE)], strips.at[t % 2, j], strip_sem.at[t % 2, j])
            for j in range(2)
        ]

    def load_strips(t):
        whole_by_now(t)
        for copy in strip_copies(t):
            copy.start()

    def strip_spans(t):
        index, line, column, early = chunks[t]
        for copy in strip_copies(t):
            copy.wait()
        for j in range(2):
            start = j * (shards[index].shape[1] // 2) + column
            yield slice(start, start + PIECE), strips[t % 2, j].reshape(width, PIECE)

    def widen(t):
        for span, weight in strip_spans(t):
            hidden = nn(normed_ref[...], weight) + hidden_bias_ref[0:1, span]
            hidden_ref[:, span] = hidden.astype(low)
            active_ref[:, span] = (hidden * jax.nn.sigmoid(hidden)).astype(low)

    def project(t):
        for span, weight in strip_spans(t):
            part = span.start // width
            value = nn(attn_ref[...], weight)
            if part != 1:
                value = value + model_bias_ref[part // 2 + 1 : part // 2 + 2, span.start % width : span.start % width + PIECE]
            projected[:, span] = value.astype(low)

    def in_turn(numbers, load, use):
        load(numbers[0])
        for former, latter in zip(numbers, numbers[1:] + [None]):
            if latter is not None:
                load(latter)
            use(former)

    gather.run(LAG)
    for start in range(0, segment, ROWS):
        rows = slice(start, start + ROWS)
        values = tokens_ref[rows, :].astype(jnp.float32)
        normed_ref[rows, :] = normed_rows(values, gains_ref[0:1, :], shifts_ref[0:1, :]).astype(low)
    in_turn(chunks_for(0), load_strips, widen)
    for t in chunks_for(1):
        whole_by_now(t)
    tall = wholes[1].shape[3]

    def block_copy(f):
        return Near(wholes[1].at[f // 4, f // 2 % 2, f % 2], blocks.at[f % 2], block_sem.at[f % 2])

    def narrow(f):
        block_copy(f).wait()
        value = nn(active_ref[:, f * tall : (f + 1) * tall], blocks[f % 2])
        if f == 0:
            branch[...] = value
        else:
            branch[...] += value
        if f % 4 == 3:
            gather.run(gather.number + 1)

    block_copy(0).start()
    for f in range(16):
        if f < 15:
            block_copy(f + 1).start()
        narrow(f)
    for start in range(0, segment, ROWS):
        rows = slice(start, start + ROWS)
        values = tokens_ref[rows, :].astype(jnp.float32) + 0.5 * (branch[rows, :] + model_bias_ref[0:1, :])
        after_ref[rows, :] = values
        attn_ref[rows, :] = normed_rows(values, gains_ref[1:2, :], shifts_ref[1:2, :]).astype(low)
    in_turn(chunks_for(2), load_strips, project)

    mine, theirs = pl.ds(me.x * segment, segment), pl.ds((1 - me.x) * segment, segment)

    def leaving(i):
        return [
            Sent(projected.at[:, strip((2 * part + 1 - me.x) * pairs + i)], qkv.at[i, part, mine, :], send_sem.at[i, part], recv_sem.at[i, part], me.across())
            for part in range(3)
        ]

    def staying(i):
        return [
            Near(projected.at[:, strip((2 * part + me.x) * pairs + i)], qkv.at[i, part, mine, :], own_sem.at[i, part])
            for part in range(3)
        ]

    def returns(i):
        there = out_ref.at[:, strip(me.x * pairs + i)]
        return (
            Sent(outs.at[i, theirs, :], there, back_send.at[i], back_recv.at[i], me.across()),
            Near(outs.at[i, mine, :], there, out_sem.at[i]),
            Near(qkv.at[i], kept_ref.at[i], kept_sem.at[i]),
        )

    for i in range(pairs):
        for copy in leaving(i) + staying(i):
            copy.start()
    gather.run(gather.number + 1)
    for i in range(pairs):
        for copy in leaving(i):
            copy.wait_recv()
        for copy in staying(i):
            copy.wait()

        def between(block):
            if block % 2 == 1:
                gather.run(gather.number + 1)

        attend_pair(qkv.at[i, 0], qkv.at[i, 1], qkv.at[i, 2], rel_ref, outs.at[i], log_ref.at[i], between)
        for copy in returns(i):
            copy.start()
    gather.run(gather.steps)
    gather.finish()
    for i in range(pairs):
        for copy in leaving(i):
            copy.wait_send()
        sent, own, kept = returns(i)
        sent.wait_send()
        sent.wait_recv()
        own.wait()
        kept.wait()


def front(tokens, rel_low, norm_gains, norm_biases, hidden_biases, model_biases, shards, identity):
    segment, width = tokens.shape
    hidden = shards[0].shape[1]
    length, pairs, count = 2 * segment, width // (2 * PAIR * HEAD), len(shards)
    wholes, chunks, lines = gather_plan(shards, (4, 7))
    dma, low = pltpu.SemaphoreType.DMA, jnp.bfloat16
    anywhere, near = pl.BlockSpec(memory_space=pl.ANY), pl.BlockSpec(memory_space=pltpu.VMEM)
    *kept, = pl.pallas_call(
        functools.partial(front_kernel, pairs, count, chunks, lines),
        in_specs=[near] * 6 + [anywhere] * count,
        out_specs=[near] * 5 + [anywhere] * 2 + [near] + [anywhere] * count,
        out_shape=[
            jax.ShapeDtypeStruct((segment, width), low),
            jax.ShapeDtypeStruct((segment, hidden), low),
            jax.ShapeDtypeStruct((segment, hidden), low),
            jax.ShapeDtypeStruct((segment, width), jnp.float32),
            jax.ShapeDtypeStruct((segment, width), low),
            jax.ShapeDtypeStruct((segment, width), low),
            jax.ShapeDtypeStruct((pairs, 3, length, LANES), low),
            jax.ShapeDtypeStruct((pairs, length, PAIR), jnp.float32),
            *wholes,
        ],
        scratch_shapes=[
            pltpu.VMEM((segment, width), jnp.float32),
            pltpu.VMEM((segment, 3 * width), low),
            pltpu.VMEM((2, 2, 4, 2, 2, lines, PIECE), low),
            pltpu.VMEM((2, hidden // 16, width), low),
            pltpu.VMEM((pairs, 3, length, LANES), low),
            pltpu.VMEM((pairs, length, LANES), low),
            dma((2, 2)), dma((2,)),
            dma((pairs, 3)), dma((pairs, 3)), dma((pairs, 3)), dma((pairs,)), dma((pairs,)), dma((pairs,)), dma((pairs,)),
            *Gather.scratch(len(chunks)),
        ],
        compiler_params=pltpu.CompilerParams(collective_id=identity, has_side_effects=True, vmem_limit_bytes=60 << 20),
        name="front",
    )(tokens, rel_low, norm_gains, norm_biases, hidden_biases, model_biases, *shards)
    return kept[:8], flat(kept[8:])


TAPS = 32
TILE = 128


def conv_kernel(wide_ref, taps_ref, out_ref, spread):
    length = out_ref.shape[1]
    spread[...] = wide_ref[0].astype(jnp.float32)
    for start in range(0, length, TILE):
        total = jnp.zeros((TILE, LANES), jnp.float32)
        for r in range(KERNEL):
            total = total + taps_ref[r : r + 1, :] * spread[start + r + 2 : start + r + 2 + TILE, :]
        out_ref[0, start : start + TILE, :] = total


def conv_back_kernel(grad_ref, wide_ref, taps_ref, value_ref, gate_ref, dvalue_ref, dgate_ref, kernel_ref, spread, grads, sums):
    length = value_ref.shape[0]
    spread[...] = wide_ref[0].astype(jnp.float32)
    grads[...] = grad_ref[0].astype(jnp.float32)

    @pl.when(pl.program_id(1) == 0)
    def _():
        sums[...] = jnp.zeros_like(sums)

    for start in range(0, length, TILE):
        own = grads[start : start + TILE, :]
        total = jnp.zeros((TILE, LANES), jnp.float32)
        for r in range(KERNEL):
            total = total + taps_ref[r : r + 1, :] * grads[start + KERNEL - 1 - r : start + KERNEL - 1 - r + TILE, :]
            both = own * spread[start + r + 2 : start + r + 2 + TILE, :]
            sums[r] += jnp.sum(both.reshape(TILE // 8, 8, LANES), axis=0)
        span = slice(start, start + TILE)
        opened = jax.nn.sigmoid(gate_ref[span, :])
        dvalue_ref[span, :] = (total * opened).astype(jnp.bfloat16)
        dgate_ref[span, :] = (total * value_ref[span, :] * (opened * (1.0 - opened))).astype(jnp.bfloat16)
    kernel_ref[...] = jnp.sum(sums[...], axis=1)


def padded_taps(dw_kernel):
    return jnp.pad(dw_kernel, ((0, TAPS - KERNEL), (0, 0)))


def depthwise(wide, dw_kernel):
    clips, lines, width = wide.shape
    length = lines - TAPS
    return pl.pallas_call(
        conv_kernel,
        grid=(width // LANES, clips),
        in_specs=[
            pl.BlockSpec((1, lines, LANES), lambda i, j: (j, 0, i)),
            pl.BlockSpec((TAPS, LANES), lambda i, j: (0, i)),
        ],
        out_specs=pl.BlockSpec((1, length, LANES), lambda i, j: (j, 0, i)),
        out_shape=jax.ShapeDtypeStruct((clips, length, width), jnp.float32),
        scratch_shapes=[pltpu.VMEM((lines, LANES), jnp.float32)],
        cost_estimate=pl.CostEstimate(flops=2 * KERNEL * clips * length * width, bytes_accessed=6 * clips * length * width, transcendentals=0),
        name="depthwise",
    )(wide, padded_taps(dw_kernel))


def depthwise_back(grad_wide, wide, dw_kernel, gate_input):
    clips, lines, width = wide.shape
    length, blocks = lines - TAPS, width // LANES
    tall = pl.BlockSpec((1, lines, LANES), lambda i, j: (j, 0, i))
    half = pl.BlockSpec((length, LANES), lambda i, j: (j, i))
    taps = pl.BlockSpec((TAPS, LANES), lambda i, j: (0, i))
    shape = jax.ShapeDtypeStruct((clips * length, width), jnp.bfloat16)
    dvalue, dgate, kernel_grad = pl.pallas_call(
        conv_back_kernel,
        grid=(blocks, clips),
        in_specs=[tall, tall, taps, half, pl.BlockSpec((length, LANES), lambda i, j: (j, blocks + i))],
        out_specs=[half, half, taps],
        out_shape=[shape, shape, jax.ShapeDtypeStruct((TAPS, width), jnp.float32)],
        scratch_shapes=[
            pltpu.VMEM((lines, LANES), jnp.float32),
            pltpu.VMEM((lines, LANES), jnp.float32),
            pltpu.VMEM((TAPS, 8, LANES), jnp.float32),
        ],
        cost_estimate=pl.CostEstimate(flops=4 * KERNEL * clips * length * width, bytes_accessed=16 * clips * length * width, transcendentals=clips * length * width),
        name="depthwise_back",
    )(grad_wide, wide, padded_taps(dw_kernel), gate_input, gate_input)
    return jnp.concatenate([dvalue, dgate], axis=1), kernel_grad[:KERNEL]


def feed_forward(values, norm_gain, norm_shift, weight_up, bias_up, weight_down, bias_down):
    normed = layer_norm(values, norm_gain, norm_shift).astype(jnp.bfloat16)
    hidden = product(normed, weight_up) + bias_up
    active = jax.nn.silu(hidden).astype(jnp.bfloat16)
    branch = product(active, weight_down) + bias_down
    return (branch, (normed, hidden, active))


def feed_backward(residual_grad, values, kept_parts, norm_gain, norm_shift, weight_up, weight_down):
    normed, hidden, active = kept_parts
    branch_grad = (0.5 * residual_grad).astype(jnp.bfloat16)
    down_bias_grad = jnp.sum(branch_grad.astype(jnp.float32), axis=0)
    active_grad = times_transposed(branch_grad, weight_down)
    silu_pull = jax.vjp(jax.nn.silu, hidden)[1]
    hidden_grad = silu_pull(active_grad)[0].astype(jnp.bfloat16)
    up_bias_grad = jnp.sum(hidden_grad.astype(jnp.float32), axis=0)
    normed_grad = times_transposed(hidden_grad, weight_up)
    norm_pull = jax.vjp(layer_norm, values, norm_gain, norm_shift)[1]
    values_grad, gain_grad, shift_grad = norm_pull(normed_grad)
    return (
        residual_grad + values_grad,
        (normed, hidden_grad),
        up_bias_grad,
        (active, branch_grad),
        down_bias_grad,
        gain_grad,
        shift_grad,
    )


def heads_of(projected, clip_count, segment, rel_low):
    parts = [
        lax.all_to_all(part.reshape(clip_count, segment, -1), "seq", split_axis=2, concat_axis=1, tiled=True)
        for part in jnp.split(projected, 3, axis=1)
    ]
    merged, log_totals = attend(*parts, rel_low)
    attn_seq = lax.all_to_all(merged, "seq", split_axis=1, concat_axis=2, tiled=True)
    return attn_seq.reshape(clip_count * segment, -1), parts, log_totals


def heads_back(out_grad, parts, log_totals, clip_count, segment, rel_low):
    merged = lax.all_to_all(
        out_grad.reshape(clip_count, segment, -1), "seq", split_axis=2, concat_axis=1, tiled=True
    )
    *grads, table_parts = attend_back(*parts, merged, log_totals, rel_low)
    grads = [
        lax.all_to_all(grad, "seq", split_axis=1, concat_axis=2, tiled=True).reshape(clip_count * segment, -1)
        for grad in grads
    ]
    return jnp.concatenate(grads, axis=1), jnp.sum(table_parts, axis=0)


def spread_sums(factors, small):
    sums = []
    for left, right in factors:
        part = lax.psum_scatter(contract_rows(left, right).astype(jnp.bfloat16), "seq", scatter_dimension=1, tiled=True)
        part = lax.psum_scatter(part, "fsdp", scatter_dimension=0, tiled=True)
        sums.append(part.astype(jnp.float32))
    return (*sums, lax.psum(small, ("seq", "fsdp")))


def stacked(rows):
    lines = jnp.concatenate([row.reshape(-1, rows[0].shape[-1]) for row in rows])
    return jnp.pad(lines, ((0, -lines.shape[0] % 8), (0, 0)))


def body(
    tokens,
    cotangent,
    ffn1_up,
    ffn1_down,
    qkv_weight,
    out_weight,
    conv_in,
    conv_out,
    ffn2_up,
    ffn2_down,
    norm_gains,
    norm_biases,
    hidden_biases,
    model_biases,
    dw_kernel,
    rel_table,
):
    clip_count, segment, model_width = tokens.shape
    row_count = clip_count * segment
    rim_width = KERNEL - 1
    close = lax.axis_size("seq") == 2 and lax.axis_size("fsdp") == 16 and clip_count == 1
    low = jnp.bfloat16
    shards = [
        weight.astype(low)
        for weight in (ffn1_up, ffn1_down, qkv_weight, out_weight, conv_in, conv_out, ffn2_up, ffn2_down)
    ]
    rel_low = padded_table(rel_table)
    input_rows = tokens.reshape(row_count, model_width).astype(jnp.float32)
    if close:
        fronts, weights = front(
            tokens.reshape(row_count, model_width), rel_low, norm_gains, norm_biases, hidden_biases, model_biases, shards, 0
        )
        normed_one, hidden_one, active_one, after_one, normed_attn, attn_rows, kept_heads, log_totals = fronts
        kept_one = (normed_one, hidden_one.astype(jnp.float32), active_one)
    else:
        weights = [lax.all_gather(shard, "fsdp", axis=0, tiled=True) for shard in shards]
        branch_one, kept_one = feed_forward(
            input_rows,
            norm_gains[0],
            norm_biases[0],
            weights[0],
            hidden_biases[0],
            weights[1],
            model_biases[0],
        )
        after_one = input_rows + 0.5 * branch_one
        normed_attn = layer_norm(after_one, norm_gains[1], norm_biases[1]).astype(low)
        project_bias = jnp.concatenate([model_biases[1], jnp.zeros_like(model_biases[1]), model_biases[2]])
        projected = (product(normed_attn, weights[2]) + project_bias).astype(low)
        attn_rows, kept_heads, log_totals = heads_of(projected, clip_count, segment, rel_low)
    up_one, down_one, qkv_full, out_full, conv_first, conv_second, up_two, down_two = weights
    after_two = after_one + product(attn_rows, out_full) + model_biases[3]
    normed_conv = layer_norm(after_two, norm_gains[2], norm_biases[2]).astype(low)
    gate_input = product(normed_conv, conv_first)
    glu_out = glu_function(gate_input).astype(low).reshape(clip_count, segment, model_width)
    glu_before = passed_along(glu_out[:, segment - rim_width :], "seq", 1)
    margin = jnp.zeros((clip_count, TAPS - rim_width, model_width), low)
    glu_wide = jnp.concatenate([margin, glu_before, glu_out], axis=1)
    mixed_flat = depthwise(glu_wide, dw_kernel).reshape(row_count, model_width)
    swished = conv_tail(mixed_flat, norm_gains[3], norm_biases[3]).astype(low)
    after_three = after_two + product(swished, conv_second)
    branch_two, kept_two = feed_forward(
        after_three,
        norm_gains[4],
        norm_biases[4],
        up_two,
        hidden_biases[1],
        down_two,
        model_biases[4],
    )
    after_four = after_three + 0.5 * branch_two
    final_rows, final_pull = jax.vjp(layer_norm, after_four, norm_gains[5], norm_biases[5])
    output = final_rows.astype(low).reshape(clip_count, segment, model_width)
    grad_four, gain_five, shift_five = final_pull(
        cotangent.reshape(row_count, model_width).astype(jnp.float32)
    )
    grad_three, up_two_factors, up_two_bias, down_two_factors, down_two_bias, gain_four, shift_four = (
        feed_backward(
            grad_four, after_three, kept_two, norm_gains[4], norm_biases[4], up_two, down_two
        )
    )
    conv_grad = grad_three.astype(low)
    swished_grad = times_transposed(conv_grad, conv_second)
    tail_pull = jax.vjp(conv_tail, mixed_flat, norm_gains[3], norm_biases[3])[1]
    mixed_grad, gain_three, shift_three = tail_pull(swished_grad)
    mixed_low = mixed_grad.astype(low).reshape(clip_count, segment, model_width)
    mixed_after = passed_along(mixed_low[:, 0:rim_width], "seq", -1)
    mixed_wide = jnp.concatenate([mixed_low, mixed_after, margin], axis=1)
    gate_grad, kernel_grad = depthwise_back(mixed_wide, glu_wide, dw_kernel, gate_input)
    conv_norm_pull = jax.vjp(layer_norm, after_two, norm_gains[2], norm_biases[2])[1]
    values_grad, gain_two, shift_two = conv_norm_pull(times_transposed(gate_grad, conv_first))
    grad_two = grad_three + values_grad
    later_small = stacked(
        [gain_two, gain_three, gain_four, gain_five, shift_two, shift_three, shift_four, shift_five]
        + [up_two_bias, down_two_bias, kernel_grad]
    )
    later_factors = [down_two_factors, up_two_factors, (swished, conv_grad), (normed_conv, gate_grad)]
    attn_grad = grad_two.astype(low)
    out_bias_grad = jnp.sum(attn_grad.astype(jnp.float32), axis=0)
    merged_grad = times_transposed(attn_grad, out_full).astype(low)
    if close:
        projected_grad, table_parts, *later_sums = attend_back_split(
            merged_grad, kept_heads, log_totals, rel_low, later_factors, later_small, 3
        )
    else:
        projected_grad, table_parts = heads_back(
            merged_grad, kept_heads, log_totals, clip_count, segment, rel_low
        )
        later_sums = spread_sums(later_factors, later_small)
    down_two_sum, up_two_sum, conv_second_sum, conv_first_sum, later_sum = later_sums
    table_grad = jnp.sum(table_parts, axis=0).T[::-1][:BUCKETS]
    query_bias_grad = jnp.sum(projected_grad[:, :model_width].astype(jnp.float32), axis=0)
    value_bias_grad = jnp.sum(projected_grad[:, 2 * model_width :].astype(jnp.float32), axis=0)
    attn_norm_pull = jax.vjp(layer_norm, after_one, norm_gains[1], norm_biases[1])[1]
    values_grad, gain_one, shift_one = attn_norm_pull(times_transposed(projected_grad, qkv_full))
    grad_one = grad_two + values_grad
    grad_zero, up_one_factors, up_one_bias, down_one_factors, down_one_bias, gain_zero, shift_zero = (
        feed_backward(
            grad_one, input_rows, kept_one, norm_gains[0], norm_biases[0], up_one, down_one
        )
    )
    input_grad = grad_zero.astype(low).reshape(clip_count, segment, model_width)
    table_flat = table_grad.reshape(-1)
    table_rows = jnp.pad(table_flat, (0, -table_flat.size % model_width)).reshape(-1, model_width)
    early_small = stacked(
        [gain_zero, gain_one, shift_zero, shift_one, up_one_bias]
        + [down_one_bias, query_bias_grad, value_bias_grad, out_bias_grad, table_rows]
    )
    sums_of = partial(scatter_sums, identity=4) if close else spread_sums
    up_one_sum, down_one_sum, qkv_sum, out_sum, early_sum = sums_of(
        [up_one_factors, down_one_factors, (normed_attn, projected_grad), (attn_rows, attn_grad)],
        early_small,
    )
    hidden_rows = up_one_bias.size // model_width
    after_hidden = 4 + hidden_rows
    table_at = after_hidden + 4
    table_sum = early_sum[table_at : table_at + table_rows.shape[0]].reshape(-1)[: table_flat.size]
    later_hidden = 8 + hidden_rows
    return (
        output,
        input_grad,
        up_one_sum,
        down_one_sum,
        qkv_sum,
        out_sum,
        conv_first_sum,
        conv_second_sum,
        up_two_sum,
        down_two_sum,
        jnp.concatenate([early_sum[0:2], later_sum[0:4]]),
        jnp.concatenate([early_sum[2:4], later_sum[4:5]]),
        later_sum[5:8],
        jnp.stack([early_sum[4:after_hidden].reshape(-1), later_sum[8:later_hidden].reshape(-1)]),
        early_sum[after_hidden : after_hidden + 3],
        jnp.concatenate([early_sum[after_hidden + 3 : table_at], later_sum[later_hidden : later_hidden + 1]]),
        later_sum[later_hidden + 1 : later_hidden + 1 + KERNEL],
        table_sum.reshape(table_grad.shape),
    )


def solution(mesh):
    in_specs = (
        P("fsdp", "seq", None),
        P("fsdp", "seq", None),
        P("fsdp", None),
        P("fsdp", None),
        P("fsdp", None),
        P("fsdp", None),
        P("fsdp", None),
        P("fsdp", None),
        P("fsdp", None),
        P("fsdp", None),
        P(),
        P(),
        P(),
        P(),
        P(),
        P(),
    )
    out_specs = (
        P("fsdp", "seq", None),
        P("fsdp", "seq", None),
        P("fsdp", "seq"),
        P("fsdp", "seq"),
        P("fsdp", "seq"),
        P("fsdp", "seq"),
        P("fsdp", "seq"),
        P("fsdp", "seq"),
        P("fsdp", "seq"),
        P("fsdp", "seq"),
        P(),
        P(),
        P(),
        P(),
        P(),
        P(),
        P(),
        P(),
    )
    return jax.shard_map(body, mesh=mesh, in_specs=in_specs, out_specs=out_specs, check_vma=False)
```

```python
import functools
from functools import partial

import jax
import jax.numpy as jnp
from jax import lax
from jax.experimental import pallas as pl
from jax.experimental.pallas import tpu as pltpu
from jax.sharding import PartitionSpec as P

HEAD = 64
KERNEL = 31
LEFT = 64
RIGHT = 8
BUCKETS = 73


EPSILON = 1e-05


def passed_along(value, axis, by):
    length = lax.axis_size(axis)
    pairs = [(i, i + by) for i in range(length) if 0 <= i + by < length]
    return lax.ppermute(value, axis, pairs)


def layer_norm(values, norm_gain, norm_shift):
    center = values - jnp.mean(values, axis=-1, keepdims=True)
    spread = jnp.mean(center * center, axis=-1, keepdims=True)
    return center * lax.rsqrt(spread + EPSILON) * norm_gain + norm_shift


def product(former, latter):
    return jnp.dot(former, latter, preferred_element_type=jnp.float32)


def contract_rows(former, latter):
    return lax.dot_general(
        former, latter, (((0,), (0,)), ((), ())), preferred_element_type=jnp.float32
    )


def times_transposed(former, latter):
    return lax.dot_general(
        former, latter, (((1,), (1,)), ((), ())), preferred_element_type=jnp.float32
    )


def glu_function(gate_input):
    half_width = gate_input.shape[1] // 2
    return gate_input[:, :half_width] * jax.nn.sigmoid(gate_input[:, half_width:])


def conv_tail(mixed_rows, norm_gain, norm_shift):
    return jax.nn.silu(layer_norm(mixed_rows, norm_gain, norm_shift))


MESH = pl.DeviceIdType.MESH
PIECE = 256
LAG = 3
BLOCK = 512
WAIT = 2
OWN_SLOTS = 8
AWAY_SLOTS = 3


class Place:
    def __init__(self):
        self.x = lax.axis_index("seq")
        self.f = lax.axis_index("fsdp")
        self.c = lax.rem(self.f, 2)
        self.y = lax.rem(lax.div(self.f, 2), 2)
        self.z = lax.div(self.f, 4)

    def across(self):
        return (1 - self.x, self.f)

    def twin(self):
        return (self.x, self.f + 1 - 2 * self.c)

    def beside(self):
        return (self.x, self.f + 2 - 4 * self.y)

    def along(self, step):
        return (self.x, lax.rem(self.z + step, 4) * 4 + self.y * 2 + self.c)

    def greet(self):
        barrier = pltpu.get_barrier_semaphore()
        peers = [self.across(), self.twin(), self.beside()] + [self.along(s) for s in (1, 2, 3)]
        for peer in peers:
            pl.semaphore_signal(barrier, inc=1, device_id=peer, device_id_type=MESH)
        pl.semaphore_wait(barrier, len(peers))


def chunks_of(shapes, lines, crossing, piece):
    shares = [(part, whole) for blocks, part, whole in crossing for _ in range(blocks)]
    found = []
    for index, (rows, width) in enumerate(shapes):
        for line in range(0, rows, lines):
            for column in range(0, width // 2, piece):
                count = len(found)
                part, whole = shares[min(count, len(shares) - 1)]
                found.append((index, line, column, (count + 1) * part // whole > count * part // whole))
    return found


class Sent:
    def __init__(self, source, target, send_sem, recv_sem, device):
        self.parts = dict(src_ref=source, dst_ref=target, send_sem=send_sem, recv_sem=recv_sem, device_id=device, device_id_type=MESH)

    def start(self):
        pltpu.make_async_remote_copy(**self.parts).start()

    def wait_recv(self):
        pltpu.make_async_remote_copy(**self.parts).wait_recv()

    def wait_send(self):
        pltpu.make_async_remote_copy(**self.parts).wait_send()


class Near:
    def __init__(self, source, target, sem):
        self.parts = (source, target, sem)

    def start(self):
        pltpu.make_async_copy(*self.parts).start()

    def wait(self):
        pltpu.make_async_copy(*self.parts).wait()


class Gather:
    def __init__(self, me, shards, wholes, chunks, lines, sems):
        self.me, self.shards, self.wholes, self.chunks, self.lines = me, shards, wholes, chunks, lines
        (self.own_sem, self.z_send, self.z_recv, self.y_send, self.y_recv, self.x_send, self.x_recv, self.c_send, self.c_recv) = sems
        self.steps = len(chunks) + 3 * LAG
        self.number = 0
        self.whole = set()

    @staticmethod
    def scratch(total):
        dma = pltpu.SemaphoreType.DMA
        return [
            dma((total, 2)), dma((total, 2, 3)), dma((total, 2, 3)), dma((total, 2)), dma((total, 2)),
            dma((total,)), dma((total,)), dma((total, 2)), dma((total, 2)),
        ]

    def halves(self, chunk):
        index, line, column, early = chunk
        half = self.shards[index].shape[1] // 2
        if early:
            return [pl.ds(pl.multiple_of(self.me.x * half + column, PIECE), PIECE)]
        return [pl.ds(column, PIECE), pl.ds(half + column, PIECE)]

    def both(self, chunk):
        half = self.shards[chunk[0]].shape[1] // 2
        return [pl.ds(chunk[2], PIECE), pl.ds(half + chunk[2], PIECE)]

    def make(self, t, kind):
        index, line, column, early = self.chunks[t]
        shard, whole, rows, me = self.shards[index], self.wholes[index], pl.ds(line, self.lines), self.me
        halves = self.halves(self.chunks[t])
        if kind == "own":
            return [
                Near(shard.at[rows, cols], whole.at[me.z, me.y, me.c, rows, cols], self.own_sem.at[t, j])
                for j, cols in enumerate(halves)
            ]
        if kind == "z":
            return [
                Sent(shard.at[rows, cols], whole.at[me.z, me.y, me.c, rows, cols], self.z_send.at[t, j, s - 1], self.z_recv.at[t, j, s - 1], me.along(s))
                for j, cols in enumerate(halves)
                for s in (1, 2, 3)
            ]
        if kind == "y":
            views = [whole.at[:, me.y, me.c, rows, cols] for cols in halves]
            return [Sent(view, view, self.y_send.at[t, j], self.y_recv.at[t, j], me.beside()) for j, view in enumerate(views)]
        if kind == "x":
            views = [whole.at[:, :, me.c, rows, halves[0]]] if early else []
            return [Sent(view, view, self.x_send.at[t], self.x_recv.at[t], me.across()) for view in views]
        views = [whole.at[:, :, me.c, rows, cols] for cols in self.both(self.chunks[t])]
        return [Sent(view, view, self.c_send.at[t, j], self.c_recv.at[t, j], me.twin()) for j, view in enumerate(views)]

    def start(self, t, kind):
        for copy in self.make(t, kind):
            copy.start()

    def arrive(self, t, kind):
        for copy in self.make(t, kind):
            copy.wait_recv()

    def first(self, t):
        self.start(t, "own")
        self.start(t, "z")

    def second(self, t):
        for copy in self.make(t, "own"):
            copy.wait()
        self.arrive(t, "z")
        self.start(t, "y")

    def third(self, t):
        self.arrive(t, "y")
        self.start(t, "x")

    def fourth(self, t):
        self.arrive(t, "x")
        self.start(t, "c")

    def step(self, number):
        for stage, phase in reversed(list(enumerate((self.first, self.second, self.third, self.fourth)))):
            if 0 <= number - LAG * stage < len(self.chunks):
                phase(number - LAG * stage)

    def run(self, number):
        while self.number < min(number, self.steps):
            self.step(self.number)
            self.number += 1

    def landed(self, t):
        if t not in self.whole:
            self.arrive(t, "c")
            self.whole.add(t)

    def finish(self):
        for t in range(len(self.chunks)):
            self.landed(t)
            for kind in "zyxc":
                for copy in self.make(t, kind):
                    copy.wait_send()


def gather_plan(shards, crossing):
    shapes = [shard.shape for shard in shards]
    lines = min(rows for rows, _ in shapes)
    wholes = [jax.ShapeDtypeStruct((4, 2, 2, *shape), jnp.bfloat16) for shape in shapes]
    return wholes, chunks_of(shapes, lines, crossing, PIECE), lines


def flat(wholes):
    return [whole.reshape(-1, whole.shape[-1]) for whole in wholes]


class Scatter:
    def __init__(self, me, lefts, rights, small, outs, small_out, chunks, lines, scratch, small_from=0):
        self.me, self.lefts, self.rights, self.small, self.outs, self.small_out = me, lefts, rights, small, outs, small_out
        self.chunks, self.lines, self.small_from, self.number = chunks, lines, small_from, 0
        (self.strips, self.cols, self.turned, self.own, self.away, self.core_in, self.early_in, self.late_in, self.y_in, self.z_in,
         self.end_in, self.done, self.strip_sem, self.cols_sem, self.done_sem,
         self.c_send, self.c_recv, self.x_send, self.x_recv, self.y_send, self.y_recv, self.z_send, self.z_recv,
         self.small_held, self.small_in, self.small_z, self.small_send, self.small_recv, self.small_z_send, self.small_z_recv) = scratch
        self.order = [sum(other[3] == chunk[3] for other in chunks[:t]) for t, chunk in enumerate(chunks)]
        self.steps = len(chunks) + 1 + 4 * WAIT

    @staticmethod
    def scratch(chunks, lines, tokens, small):
        dma, low, total = pltpu.SemaphoreType.DMA, jnp.bfloat16, len(chunks)
        early = sum(chunk[3] for chunk in chunks)
        late = total - early
        return [
            pltpu.VMEM((tokens, 32 * lines), low),
            pltpu.VMEM((2, 2, tokens, BLOCK), low),
            pltpu.VMEM((2, 16 * lines, tokens), low),
            pltpu.VMEM((OWN_SLOTS, 2, 4, 2, lines, BLOCK), low),
            pltpu.VMEM((AWAY_SLOTS, 2, 4, 2, lines, BLOCK), low),
            pltpu.VMEM((total, 2, 4, 2, lines, BLOCK), low),
            pltpu.VMEM((early, 4, 2, lines, BLOCK), low),
            pltpu.VMEM((late, 2, 4, lines, BLOCK), low),
            pltpu.VMEM((early, 4, lines, BLOCK), low),
            pltpu.VMEM((late, 3, 2, lines, BLOCK), low),
            pltpu.VMEM((total, 3, lines, BLOCK), low),
            pltpu.VMEM((total, lines, BLOCK), jnp.float32),
            dma((16,)), dma((2, 2)), dma((total,)),
            dma((total, 2)), dma((total, 2)), dma((total,)), dma((total,)),
            dma((total,)), dma((total,)), dma((total, 3)), dma((total, 3)),
            pltpu.VMEM((4, *small), jnp.float32), pltpu.VMEM((3, *small), jnp.float32), pltpu.VMEM((4, *small), jnp.float32),
            dma((3,)), dma((3,)), dma((3,)), dma((3,)),
        ]

    def columns(self, t, j):
        index, line, column, early = self.chunks[t]
        return pl.ds(j * (self.rights[index].shape[1] // 2) + column, BLOCK)

    def turns(self, t):
        index, line, column, early = self.chunks[t]
        if self.lefts[index].shape[1] > 16 * self.lines:
            return column == 0 and line % (2 * self.lines) == 0, line // self.lines % 2
        return column == 0, 0

    def loads(self, t):
        index, line, column, early = self.chunks[t]
        left, wide = self.lefts[index], 2 * self.lines
        copies = [Near(self.rights[index].at[:, self.columns(t, j)], self.cols.at[t % 2, j], self.cols_sem.at[t % 2, j]) for j in range(2)]
        if self.turns(t)[0]:
            rows = left.shape[1] // 16
            if rows > self.lines:
                copies += [
                    Near(left.at[:, pl.ds(i * rows + line, wide)], self.strips.at[:, pl.ds(i * wide, wide)], self.strip_sem.at[i])
                    for i in range(16)
                ]
            else:
                copies.append(Near(left, self.strips.at[:, pl.ds(0, 8 * wide)], self.strip_sem.at[0]))
        return copies

    def load(self, t):
        for copy in self.loads(t):
            copy.start()

    def turn(self, t):
        lines, me = self.lines, self.me
        left = self.lefts[self.chunks[t][0]]

        def place(core, block):
            return pl.ds(pl.multiple_of((lax.rem(core + me.c, 2) * 8 + block) * lines, lines), lines)

        if left.shape[1] > 16 * lines:

            @pl.loop(0, 16)
            def _(i):
                block = jnp.transpose(self.strips[:, pl.ds(pl.multiple_of(i * 2 * lines, 2 * lines), 2 * lines)])
                rows = place(lax.rem(i, 2), lax.div(i, 2))
                self.turned[0, rows, :] = block[:lines]
                self.turned[1, rows, :] = block[lines:]

        else:

            @pl.loop(0, 8)
            def _(i):
                block = jnp.transpose(self.strips[:, pl.ds(pl.multiple_of(i * 2 * lines, 2 * lines), 2 * lines)])
                self.turned[0, place(0, i), :] = block[:lines]
                self.turned[0, place(1, i), :] = block[lines:]

    def make(self, t, kind):
        index, line, column, early = self.chunks[t]
        me, own, slot, order = self.me, self.own, t % OWN_SLOTS, self.order[t]
        if kind == "c":
            return [
                Sent(self.away.at[t % AWAY_SLOTS, j], self.core_in.at[t, j], self.c_send.at[t, j], self.c_recv.at[t, j], me.twin())
                for j in range(2)
            ]
        if kind == "x":
            source, target = (
                (own.at[slot, 1 - me.x], self.early_in.at[order]) if early
                else (own.at[slot, 1 - me.x, me.z, me.y], self.end_in.at[t, 0])
            )
            return [Sent(source, target, self.x_send.at[t], self.x_recv.at[t], me.across())]
        if kind == "y":
            source, target = (
                (own.at[slot, me.x, :, 1 - me.y], self.y_in.at[order]) if early
                else (own.at[slot, :, :, 1 - me.y], self.late_in.at[order])
            )
            return [Sent(source, target, self.y_send.at[t], self.y_recv.at[t], me.beside())]
        copies = []
        for s in (1, 2, 3):
            z = lax.rem(me.z + s, 4)
            source, target = (
                (own.at[slot, me.x, z, me.y], self.end_in.at[t, s - 1]) if early
                else (own.at[slot, :, z, me.y], self.z_in.at[order, s - 1])
            )
            copies.append(Sent(source, target, self.z_send.at[t, s - 1], self.z_recv.at[t, s - 1], me.along(s)))
        return copies

    def finished(self, t):
        index, line, column, early = self.chunks[t]
        return Near(self.done.at[t], self.outs[index].at[pl.ds(line, self.lines), pl.ds(column, BLOCK)], self.done_sem.at[t])

    def make_small(self, stage):
        me = self.me
        if stage < 3:
            peer = (me.twin, me.across, me.beside)[stage]()
            return [Sent(self.small_held.at[stage], self.small_in.at[stage], self.small_send.at[stage], self.small_recv.at[stage], peer)]
        return [
            Sent(self.small_held.at[3], self.small_z.at[me.z], self.small_z_send.at[s - 1], self.small_z_recv.at[s - 1], me.along(s))
            for s in (1, 2, 3)
        ]

    def start(self, t, kind):
        for copy in self.make(t, kind):
            copy.start()

    def arrive(self, t, kind):
        for copy in self.make(t, kind):
            copy.wait_recv()

    def leave(self, t, kinds):
        for kind in kinds:
            for copy in self.make(t, kind):
                copy.wait_send()

    def first(self, t):
        lines = self.lines
        for copy in self.loads(t):
            copy.wait()
        fresh, which = self.turns(t)
        if fresh:
            self.turn(t)
        if t >= AWAY_SLOTS:
            self.leave(t - AWAY_SLOTS, "c")
        if t >= OWN_SLOTS:
            self.leave(t - OWN_SLOTS, "zyx")
        for other in (1, 0):
            target, slot = (self.own, t % OWN_SLOTS) if other == 0 else (self.away, t % AWAY_SLOTS)
            for j in range(2):

                @pl.loop(0, 2)
                def _(pair):
                    rows = pl.ds(pl.multiple_of((other * 2 + pair) * 4 * lines, 4 * lines), 4 * lines)
                    part = nn(self.turned[which, rows, :], self.cols[t % 2, j]).astype(jnp.bfloat16)
                    for z in range(2):
                        for y in range(2):
                            target[slot, j, 2 * pair + z, y] = part[(2 * z + y) * lines : (2 * z + y + 1) * lines]

                if other == 1:
                    self.make(t, "c")[j].start()

    def second(self, t):
        early, slot, own = self.chunks[t][3], t % OWN_SLOTS, self.own
        self.arrive(t, "c")
        for j in range(2):
            for z in range(4):
                own[slot, j, z] = sums(own[slot, j, z], self.core_in[t, j, z])
        self.start(t, "x" if early else "y")

    def third(self, t):
        early, slot, me, own, order = self.chunks[t][3], t % OWN_SLOTS, self.me, self.own, self.order[t]
        if early:
            self.arrive(t, "x")
            for z in range(4):
                own[slot, me.x, z] = sums(own[slot, me.x, z], self.early_in[order, z])
            self.start(t, "y")
        else:
            self.arrive(t, "y")
            for j in range(2):
                for z in range(4):
                    own[slot, j, z, me.y] = sums(own[slot, j, z, me.y], self.late_in[order, j, z])
            self.start(t, "z")

    def fourth(self, t):
        early, slot, me, own, order = self.chunks[t][3], t % OWN_SLOTS, self.me, self.own, self.order[t]
        if early:
            self.arrive(t, "y")
            for z in range(4):
                own[slot, me.x, z, me.y] = sums(own[slot, me.x, z, me.y], self.y_in[order, z])
            self.start(t, "z")
        else:
            self.arrive(t, "z")
            for j in range(2):
                value = own[slot, j, me.z, me.y].astype(jnp.float32)
                for s in range(3):
                    value = value + self.z_in[order, s, j].astype(jnp.float32)
                own[slot, j, me.z, me.y] = value.astype(jnp.bfloat16)
            self.start(t, "x")

    def fifth(self, t):
        early, slot, me = self.chunks[t][3], t % OWN_SLOTS, self.me
        self.arrive(t, "z" if early else "x")
        value = self.own[slot, me.x, me.z, me.y].astype(jnp.float32)
        for s in range(3 if early else 1):
            value = value + self.end_in[t, s].astype(jnp.float32)
        self.done[t] = value
        self.finished(t).start()

    def small_step(self, stage):
        if stage == 0:
            self.small_held[0] = self.small[...]
        else:
            self.make_small(stage - 1)[0].wait_recv()
            self.small_held[stage] = self.small_held[stage - 1] + self.small_in[stage - 1]
        if stage == 3:
            self.small_z[self.me.z] = self.small_held[3]
        for copy in self.make_small(stage):
            copy.start()

    def step(self, number):
        phases = ((1, self.first), (1 + WAIT, self.second), (1 + 2 * WAIT, self.third), (1 + 3 * WAIT, self.fourth), (1 + 4 * WAIT, self.fifth))
        for lag, phase in reversed(((0, self.load), *phases)):
            if 0 <= number - lag < len(self.chunks):
                phase(number - lag)
        stage = (number - self.small_from) // WAIT
        if (number - self.small_from) % WAIT == 0 and 0 <= stage < 4:
            self.small_step(stage)

    def run(self, number):
        while self.number < min(number, self.steps):
            self.step(self.number)
            self.number += 1

    def finish(self):
        for copy in self.make_small(3):
            copy.wait_recv()
        for stage in range(4):
            for copy in self.make_small(stage):
                copy.wait_send()
        self.small_out[...] = (self.small_z[0] + self.small_z[1]) + (self.small_z[2] + self.small_z[3])
        total = len(self.chunks)
        for t in range(total):
            self.finished(t).wait()
            if t + AWAY_SLOTS >= total:
                self.leave(t, "c")
            if t + OWN_SLOTS >= total:
                self.leave(t, "zyx")


def sums(former, latter):
    return (former.astype(jnp.float32) + latter.astype(jnp.float32)).astype(jnp.bfloat16)


def scatter_kernel(count, chunks, lines, *refs):
    me = Place()
    me.greet()
    scatter = Scatter(
        me, refs[:count], refs[count : 2 * count], refs[2 * count], refs[2 * count + 1 : 3 * count + 1], refs[3 * count + 1],
        chunks, lines, refs[3 * count + 2 :],
    )
    scatter.run(scatter.steps)
    scatter.finish()


def scatter_plan(factors, small, crossing):
    shapes = [(left.shape[1] // 16, right.shape[1]) for left, right in factors]
    lines = min(rows for rows, _ in shapes)
    anywhere, near = pl.BlockSpec(memory_space=pl.ANY), pl.BlockSpec(memory_space=pltpu.VMEM)
    outs = [jax.ShapeDtypeStruct((rows, width // 2), jnp.float32) for rows, width in shapes]
    outs.append(jax.ShapeDtypeStruct(small.shape, jnp.float32))
    chunks = chunks_of(shapes, lines, crossing, BLOCK)
    count = len(factors)
    operands = [left for left, _ in factors] + [right for _, right in factors] + [small]
    in_specs = [anywhere] * (2 * count) + [near]
    scratch = Scatter.scratch(chunks, lines, factors[0][0].shape[0], small.shape)
    return operands, in_specs, outs, [anywhere] * count + [near], scratch, chunks, lines


def scatter_sums(factors, small, identity):
    operands, in_specs, outs, out_specs, scratch, chunks, lines = scatter_plan(factors, small, [(1, 2, 3)])
    return pl.pallas_call(
        functools.partial(scatter_kernel, len(factors), chunks, lines),
        in_specs=in_specs,
        out_specs=out_specs,
        out_shape=outs,
        scratch_shapes=scratch,
        compiler_params=pltpu.CompilerParams(collective_id=identity, has_side_effects=True, vmem_limit_bytes=60 << 20),
        name="scatter_sums",
    )(*operands)


PAIR = 2
LANES = 128
FWD_ROWS = 256
BACK_ROWS = 256


def nt(former, latter):
    return lax.dot_general(former, latter, (((1,), (1,)), ((), ())), preferred_element_type=jnp.float32)


def nn(former, latter):
    return lax.dot_general(former, latter, (((1,), (0,)), ((), ())), preferred_element_type=jnp.float32)


def window_of(start, rows, length):
    low, high = start - LANES, start + rows + LANES
    return max(low, 0), min(high, length), max(low, 0) - low


def window_buckets(rows):
    width = rows + 2 * LANES
    places = lax.broadcasted_iota(jnp.int32, (rows, width), 1)
    lines = lax.broadcasted_iota(jnp.int32, (rows, width), 0)
    return places - lines - (LANES - LEFT)


def biased_scores(scores, position, start, rows, length):
    width = rows + 2 * LANES
    low, high, skip = window_of(start, rows, length)
    wide = jnp.concatenate([position, jnp.zeros((rows, width - LANES), jnp.float32)], axis=1)
    band = pltpu.roll(wide, LANES - LEFT, 1, stride=1, stride_axis=0)
    first, last = position[:, 0:1], position[:, BUCKETS - 1 : BUCKETS]
    bucket = window_buckets(rows)
    band = jnp.where(bucket <= 0, first, jnp.where(bucket >= BUCKETS - 1, last, band))
    pieces = []
    if low > 0:
        pieces.append(scores[:, :low] + first)
    pieces.append(scores[:, low:high] + band[:, skip : skip + high - low])
    if high < length:
        pieces.append(scores[:, high:] + last)
    return pieces[0] if len(pieces) == 1 else jnp.concatenate(pieces, axis=1)


def bucket_sums(score_grad, mirror, start, rows, length):
    width = rows + 2 * LANES
    low, high, skip = window_of(start, rows, length)
    inner = score_grad[:, low:high]
    pieces = []
    if skip > 0:
        pieces.append(jnp.zeros((rows, skip), jnp.float32))
    pieces.append(inner)
    if skip + high - low < width:
        pieces.append(jnp.zeros((rows, width - skip - high + low), jnp.float32))
    wide = pieces[0] if len(pieces) == 1 else jnp.concatenate(pieces, axis=1)
    bucket = window_buckets(rows)
    first = jnp.sum(jnp.where(bucket <= 0, wide, 0.0), axis=1, keepdims=True)
    last = jnp.sum(jnp.where(bucket >= BUCKETS - 1, wide, 0.0), axis=1, keepdims=True)
    if low > 0:
        first = first + jnp.sum(score_grad[:, :low], axis=1, keepdims=True)
    if high < length:
        last = last + jnp.sum(score_grad[:, high:], axis=1, keepdims=True)
    turned = nn(wide.astype(jnp.bfloat16), mirror)
    band = pltpu.roll(turned, (LANES + LANES - LEFT) % width, 1, stride=1, stride_axis=0)[:, :LANES]
    bucket = LANES - 1 - lax.broadcasted_iota(jnp.int32, (rows, LANES), 1)
    return jnp.where(bucket == 0, first, jnp.where(bucket == BUCKETS - 1, last, jnp.where(bucket < BUCKETS, band, 0.0)))


def mirror_of(width):
    lines = lax.broadcasted_iota(jnp.int32, (width, width), 0)
    places = lax.broadcasted_iota(jnp.int32, (width, width), 1)
    return jnp.where(lines + places == width - 1, 1.0, 0.0).astype(jnp.bfloat16)


def attend_pair(q_ref, k_ref, v_ref, rel_ref, out_ref, log_ref, between=lambda block: None):
    length = q_ref.shape[0]
    rows = min(FWD_ROWS, length)
    scale = HEAD ** (-0.5)
    rel = rel_ref[...]
    for start in range(0, length, rows):
        outs, logs = [], []
        for h in range(PAIR):
            lanes = slice(h * HEAD, (h + 1) * HEAD)
            query = q_ref[start : start + rows, lanes] * scale
            scores = nt(query, k_ref[:, lanes])
            scores = biased_scores(scores, nt(query, rel), start, rows, length)
            highest = jnp.max(scores, axis=1, keepdims=True)
            weights = jnp.exp(scores - highest)
            total = jnp.sum(weights, axis=1, keepdims=True)
            outs.append(nn(weights.astype(jnp.bfloat16), v_ref[:, lanes]) / total)
            logs.append(highest + jnp.log(total))
        out_ref[start : start + rows, :] = jnp.concatenate(outs, axis=1).astype(jnp.bfloat16)
        log_ref[start : start + rows, :] = jnp.concatenate(logs, axis=1)
        between(start // rows)


def attend_back_pair(
    q_ref, k_ref, v_ref, do_ref, log_ref, rel_ref, back_ref, mirror_ref, dq_ref, dk_ref, dv_ref, table_ref, dkt, dvt, q_turned, do_turned,
    between=lambda block: None,
):
    length = q_ref.shape[0]
    rows = min(BACK_ROWS, length)
    scale = HEAD ** (-0.5)
    q_turned[...] = (jnp.transpose(q_ref[...].astype(jnp.float32)) * scale).astype(jnp.bfloat16)
    do_turned[...] = jnp.transpose(do_ref[...].astype(jnp.float32)).astype(jnp.bfloat16)
    table_ref[...] = jnp.zeros((HEAD, LANES), jnp.float32)
    for start in range(0, length, rows):
        span = slice(start, start + rows)
        parts = []
        for h in range(PAIR):
            lanes = slice(h * HEAD, (h + 1) * HEAD)
            query = q_ref[span, lanes] * scale
            scores = nt(query, k_ref[:, lanes])
            scores = biased_scores(scores, nt(query, rel_ref[...]), start, rows, length)
            weights = jnp.exp(scores - log_ref[span, h : h + 1])
            low_weights = weights.astype(jnp.bfloat16)
            grads = nt(do_ref[span, lanes], v_ref[:, lanes])
            both = weights * grads
            delta = jnp.sum(both, axis=1, keepdims=True)
            score_grad = (both - weights * delta).astype(jnp.bfloat16)
            value_part = nn(do_turned[lanes, span], low_weights)
            key_part = nn(q_turned[lanes, span], score_grad)
            if start == 0:
                dvt[lanes, :] = value_part
                dkt[lanes, :] = key_part
            else:
                dvt[lanes, :] += value_part
                dkt[lanes, :] += key_part
            bucket = bucket_sums(score_grad.astype(jnp.float32), mirror_ref[...], start, rows, length)
            high = bucket.astype(jnp.bfloat16)
            rest = (bucket - high.astype(jnp.float32)).astype(jnp.bfloat16)
            parts.append((nn(score_grad, k_ref[:, lanes]) + nn(high, back_ref[...]) + nn(rest, back_ref[...])) * scale)
            table_ref[...] += nn(q_turned[lanes, span], high) + nn(q_turned[lanes, span], rest)
        dq_ref[span, :] = jnp.concatenate(parts, axis=1).astype(jnp.bfloat16)
        between(start // rows)
    dk_ref[...] = jnp.transpose(dkt[...]).astype(jnp.bfloat16)
    dv_ref[...] = jnp.transpose(dvt[...]).astype(jnp.bfloat16)


def attend_kernel(q_ref, k_ref, v_ref, rel_ref, out_ref, log_ref):
    attend_pair(q_ref.at[0], k_ref.at[0], v_ref.at[0], rel_ref, out_ref.at[0], log_ref.at[0, 0])


def attend_back_kernel(
    q_ref, k_ref, v_ref, do_ref, log_ref, rel_ref, back_ref, mirror_ref, dq_ref, dk_ref, dv_ref, table_ref, dkt, dvt, q_turned, do_turned
):
    attend_back_pair(
        q_ref.at[0], k_ref.at[0], v_ref.at[0], do_ref.at[0], log_ref.at[0, 0], rel_ref, back_ref, mirror_ref,
        dq_ref.at[0], dk_ref.at[0], dv_ref.at[0], table_ref.at[0, 0], dkt, dvt, q_turned, do_turned,
    )


def width_of(length):
    return min(BACK_ROWS, length) + 2 * LANES


def head_block(length):
    return pl.BlockSpec((1, length, PAIR * HEAD), lambda i, j: (i, 0, j))


def padded_table(rel_table):
    return jnp.pad(rel_table.astype(jnp.bfloat16), ((0, LANES - BUCKETS), (0, 0)))


def attend(query, key, value, rel_low):
    clips, length, width = query.shape
    pairs = width // (PAIR * HEAD)
    block = head_block(length)
    return pl.pallas_call(
        attend_kernel,
        grid=(clips, pairs),
        in_specs=[block, block, block, pl.BlockSpec((LANES, HEAD), lambda i, j: (0, 0))],
        out_specs=[block, pl.BlockSpec((1, 1, length, PAIR), lambda i, j: (i, j, 0, 0))],
        out_shape=[
            jax.ShapeDtypeStruct(query.shape, jnp.bfloat16),
            jax.ShapeDtypeStruct((clips, pairs, length, PAIR), jnp.float32),
        ],
        compiler_params=pltpu.CompilerParams(vmem_limit_bytes=48 << 20),
        cost_estimate=pl.CostEstimate(flops=4 * clips * width * length * length * 4, bytes_accessed=8 * query.size, transcendentals=clips * pairs * PAIR * length * length),
        name="attend",
    )(query, key, value, rel_low)


def attend_back(query, key, value, out_grad, logs, rel_low):
    clips, length, width = query.shape
    pairs = width // (PAIR * HEAD)
    block = head_block(length)
    shape = jax.ShapeDtypeStruct(query.shape, jnp.bfloat16)
    return pl.pallas_call(
        attend_back_kernel,
        grid=(clips, pairs),
        in_specs=[
            block, block, block, block,
            pl.BlockSpec((1, 1, length, PAIR), lambda i, j: (i, j, 0, 0)),
            pl.BlockSpec((LANES, HEAD), lambda i, j: (0, 0)),
            pl.BlockSpec((LANES, HEAD), lambda i, j: (0, 0)),
            pl.BlockSpec((width_of(length),) * 2, lambda i, j: (0, 0)),
        ],
        out_specs=[block, block, block, pl.BlockSpec((1, 1, HEAD, LANES), lambda i, j: (i, j, 0, 0))],
        out_shape=[shape, shape, shape, jax.ShapeDtypeStruct((clips, pairs, HEAD, LANES), jnp.float32)],
        scratch_shapes=[pltpu.VMEM((PAIR * HEAD, length), jnp.float32)] * 2 + [pltpu.VMEM((PAIR * HEAD, length), jnp.bfloat16)] * 2,
        compiler_params=pltpu.CompilerParams(vmem_limit_bytes=48 << 20),
        cost_estimate=pl.CostEstimate(flops=10 * clips * width * length * length * 4, bytes_accessed=14 * query.size, transcendentals=clips * pairs * PAIR * length * length),
        name="attend_back",
    )(query, key, value, out_grad, logs, rel_low, rel_low[::-1], mirror_of(width_of(length)))


def strip(index):
    return pl.ds(pl.multiple_of(index * LANES, LANES), LANES)


def attend_back_split_kernel(
    pairs, count, chunks, lines, do_ref, kept_ref, log_ref, rel_ref, back_ref, mirror_ref, *refs
):
    lefts, rights, small = refs[:count], refs[count : 2 * count], refs[2 * count]
    dp_ref, table_ref = refs[2 * count + 1 : 2 * count + 3]
    sums_refs, refs = refs[2 * count + 3 : 3 * count + 4], refs[3 * count + 4 :]
    grads, qkv, outs, dkt, dvt, q_turned, do_turned, own_sem, send_sem, recv_sem, kept_sem, out_sem, back_send, back_recv = refs[:14]
    me = Place()
    scatter = Scatter(me, lefts, rights, small, sums_refs[:count], sums_refs[count], chunks, lines, refs[14:])
    blocks = kept_ref.shape[2] // min(BACK_ROWS, kept_ref.shape[2])
    step = pl.program_id(0)
    segment = do_ref.shape[0]
    mine, theirs = pl.ds(me.x * segment, segment), pl.ds((1 - me.x) * segment, segment)

    def leaving(i):
        return Sent(do_ref.at[:, strip((1 - me.x) * pairs + i)], grads.at[i, mine, :], send_sem.at[i], recv_sem.at[i], me.across())

    def staying(i):
        return (
            pltpu.make_async_copy(do_ref.at[:, strip(me.x * pairs + i)], grads.at[i, mine, :], own_sem.at[i]),
            pltpu.make_async_copy(kept_ref.at[i], qkv.at[i], kept_sem.at[i]),
        )

    def returns(i, part):
        there = dp_ref.at[:, strip((2 * part + me.x) * pairs + i)]
        return (
            Sent(outs.at[i, part, theirs, :], there, back_send.at[i, part], back_recv.at[i, part], me.across()),
            pltpu.make_async_copy(outs.at[i, part, mine, :], there, out_sem.at[i, part]),
        )

    @pl.when(step == 0)
    def _():
        me.greet()
        for i in range(pairs):
            leaving(i).start()
            for copy in staying(i):
                copy.start()
        scatter.step(0)
        scatter.step(1)

    def between(block):
        for i in range(pairs):
            if 2 + i * blocks + block < scatter.steps:

                @pl.when(step == i)
                def _():
                    scatter.step(2 + i * blocks + block)

    leaving(step).wait_recv()
    for copy in staying(step):
        copy.wait()
    attend_back_pair(
        qkv.at[step, 0], qkv.at[step, 1], qkv.at[step, 2], grads.at[step], log_ref.at[0], rel_ref, back_ref, mirror_ref,
        outs.at[step, 0], outs.at[step, 1], outs.at[step, 2], table_ref.at[0], dkt, dvt, q_turned, do_turned, between,
    )
    for part in range(3):
        for copy in returns(step, part):
            copy.start()

    @pl.when(step == pairs - 1)
    def _():
        for number in range(2 + pairs * blocks, scatter.steps):
            scatter.step(number)
        scatter.finish()
        for i in range(pairs):
            leaving(i).wait_send()
            for part in range(3):
                sent, own = returns(i, part)
                sent.wait_send()
                sent.wait_recv()
                own.wait()


def attend_back_split(out_grad, kept, logs, rel_low, factors, small, identity):
    segment, width = out_grad.shape
    pairs, _, length, _ = kept.shape
    operands, more_specs, outs, outs_specs, scratch, chunks, lines = scatter_plan(factors, small, [(1, 6, 11)])
    dma, anywhere = pltpu.SemaphoreType.DMA, pl.BlockSpec(memory_space=pl.ANY)
    table = pl.BlockSpec((LANES, HEAD), lambda i: (0, 0))
    return pl.pallas_call(
        functools.partial(attend_back_split_kernel, pairs, len(factors), chunks, lines),
        grid=(pairs,),
        in_specs=[
            anywhere, anywhere, pl.BlockSpec((1, length, PAIR), lambda i: (i, 0, 0)), table, table,
            pl.BlockSpec((width_of(length),) * 2, lambda i: (0, 0), pipeline_mode=pl.Buffered(1)), *more_specs,
        ],
        out_specs=[anywhere, pl.BlockSpec((1, HEAD, LANES), lambda i: (i, 0, 0)), *outs_specs],
        out_shape=[
            jax.ShapeDtypeStruct((segment, 3 * width), jnp.bfloat16),
            jax.ShapeDtypeStruct((pairs, HEAD, LANES), jnp.float32),
            *outs,
        ],
        scratch_shapes=[
            pltpu.VMEM((pairs, length, LANES), jnp.bfloat16),
            pltpu.VMEM((pairs, 3, length, LANES), jnp.bfloat16),
            pltpu.VMEM((pairs, 3, length, LANES), jnp.bfloat16),
            pltpu.VMEM((LANES, length), jnp.float32),
            pltpu.VMEM((LANES, length), jnp.float32),
            pltpu.VMEM((LANES, length), jnp.bfloat16),
            pltpu.VMEM((LANES, length), jnp.bfloat16),
            dma((pairs,)), dma((pairs,)), dma((pairs,)), dma((pairs,)), dma((pairs, 3)), dma((pairs, 3)), dma((pairs, 3)),
            *scratch,
        ],
        compiler_params=pltpu.CompilerParams(collective_id=identity, has_side_effects=True, vmem_limit_bytes=62 << 20),
        name="attend_back_split",
    )(out_grad, kept, logs, rel_low, rel_low[::-1], mirror_of(width_of(length)), *operands)


CROSSING = [(24, 2, 3), (12, 1, 4), (1, 2, 3)]


def normed_rows(values, gain, shift):
    center = values - jnp.mean(values, axis=1, keepdims=True)
    spread = jnp.mean(center * center, axis=1, keepdims=True)
    return center * lax.rsqrt(spread + EPSILON) * gain + shift


def front_kernel(
    pairs, count, chunks, lines, tokens_ref, rel_ref, gains_ref, shifts_ref, hidden_bias_ref, model_bias_ref, *refs
):
    shards, refs = refs[:count], refs[count:]
    normed_ref, hidden_ref, active_ref, after_ref, attn_ref, out_ref, kept_ref, log_ref = refs[:8]
    wholes, refs = refs[8 : 8 + count], refs[8 + count :]
    (branch, projected, strips, blocks, qkv, outs, strip_sem, block_sem,
     own_sem, send_sem, recv_sem, kept_sem, out_sem, back_send, back_recv) = refs[:15]
    me = Place()
    gather = Gather(me, shards, wholes, chunks, lines, refs[15:])
    me.greet()
    segment, width = tokens_ref.shape
    low = jnp.bfloat16
    ROWS = 128

    def chunks_for(index):
        return [t for t, chunk in enumerate(chunks) if chunk[0] == index]

    def whole_by_now(t):
        gather.run(t + 3 * LAG + 1)
        gather.landed(t)

    def strip_copies(t):
        index, line, column, early = chunks[t]
        half = shards[index].shape[1] // 2
        return [
            Near(wholes[index].at[:, :, :, :, pl.ds(j * half + column, PIECE)], strips.at[t % 2, j], strip_sem.at[t % 2, j])
            for j in range(2)
        ]

    def load_strips(t):
        whole_by_now(t)
        for copy in strip_copies(t):
            copy.start()

    def strip_spans(t):
        index, line, column, early = chunks[t]
        for copy in strip_copies(t):
            copy.wait()
        for j in range(2):
            start = j * (shards[index].shape[1] // 2) + column
            yield slice(start, start + PIECE), strips[t % 2, j].reshape(width, PIECE)

    def widen(t):
        for span, weight in strip_spans(t):
            hidden = nn(normed_ref[...], weight) + hidden_bias_ref[0:1, span]
            hidden_ref[:, span] = hidden.astype(low)
            active_ref[:, span] = (hidden * jax.nn.sigmoid(hidden)).astype(low)

    def project(t):
        for span, weight in strip_spans(t):
            part = span.start // width
            value = nn(attn_ref[...], weight)
            if part != 1:
                value = value + model_bias_ref[part // 2 + 1 : part // 2 + 2, span.start % width : span.start % width + PIECE]
            projected[:, span] = value.astype(low)

    def in_turn(numbers, load, use):
        load(numbers[0])
        for former, latter in zip(numbers, numbers[1:] + [None]):
            if latter is not None:
                load(latter)
            use(former)

    gather.run(LAG)
    for start in range(0, segment, ROWS):
        rows = slice(start, start + ROWS)
        values = tokens_ref[rows, :].astype(jnp.float32)
        normed_ref[rows, :] = normed_rows(values, gains_ref[0:1, :], shifts_ref[0:1, :]).astype(low)
    in_turn(chunks_for(0), load_strips, widen)
    for t in chunks_for(1):
        whole_by_now(t)
    tall = wholes[1].shape[3]

    def block_copy(f):
        return Near(wholes[1].at[f // 4, f // 2 % 2, f % 2], blocks.at[f % 2], block_sem.at[f % 2])

    def narrow(f):
        block_copy(f).wait()
        value = nn(active_ref[:, f * tall : (f + 1) * tall], blocks[f % 2])
        if f == 0:
            branch[...] = value
        else:
            branch[...] += value
        if f % 4 == 3:
            gather.run(gather.number + 1)

    block_copy(0).start()
    for f in range(16):
        if f < 15:
            block_copy(f + 1).start()
        narrow(f)
    for start in range(0, segment, ROWS):
        rows = slice(start, start + ROWS)
        values = tokens_ref[rows, :].astype(jnp.float32) + 0.5 * (branch[rows, :] + model_bias_ref[0:1, :])
        after_ref[rows, :] = values
        attn_ref[rows, :] = normed_rows(values, gains_ref[1:2, :], shifts_ref[1:2, :]).astype(low)
    in_turn(chunks_for(2), load_strips, project)

    mine, theirs = pl.ds(me.x * segment, segment), pl.ds((1 - me.x) * segment, segment)

    def leaving(i):
        return [
            Sent(projected.at[:, strip((2 * part + 1 - me.x) * pairs + i)], qkv.at[i, part, mine, :], send_sem.at[i, part], recv_sem.at[i, part], me.across())
            for part in range(3)
        ]

    def staying(i):
        return [
            Near(projected.at[:, strip((2 * part + me.x) * pairs + i)], qkv.at[i, part, mine, :], own_sem.at[i, part])
            for part in range(3)
        ]

    def returns(i):
        there = out_ref.at[:, strip(me.x * pairs + i)]
        return (
            Sent(outs.at[i, theirs, :], there, back_send.at[i], back_recv.at[i], me.across()),
            Near(outs.at[i, mine, :], there, out_sem.at[i]),
            Near(qkv.at[i], kept_ref.at[i], kept_sem.at[i]),
        )

    for i in range(pairs):
        for copy in leaving(i) + staying(i):
            copy.start()
    gather.run(gather.number + 1)
    for i in range(pairs):
        for copy in leaving(i):
            copy.wait_recv()
        for copy in staying(i):
            copy.wait()

        def between(block):
            if block % 2 == 1:
                gather.run(gather.number + 1)

        attend_pair(qkv.at[i, 0], qkv.at[i, 1], qkv.at[i, 2], rel_ref, outs.at[i], log_ref.at[i], between)
        for copy in returns(i):
            copy.start()
    gather.run(gather.steps)
    gather.finish()
    for i in range(pairs):
        for copy in leaving(i):
            copy.wait_send()
        sent, own, kept = returns(i)
        sent.wait_send()
        sent.wait_recv()
        own.wait()
        kept.wait()


def front(tokens, rel_low, norm_gains, norm_biases, hidden_biases, model_biases, shards, identity):
    segment, width = tokens.shape
    hidden = shards[0].shape[1]
    length, pairs, count = 2 * segment, width // (2 * PAIR * HEAD), len(shards)
    wholes, chunks, lines = gather_plan(shards, CROSSING)
    dma, low = pltpu.SemaphoreType.DMA, jnp.bfloat16
    anywhere, near = pl.BlockSpec(memory_space=pl.ANY), pl.BlockSpec(memory_space=pltpu.VMEM)
    *kept, = pl.pallas_call(
        functools.partial(front_kernel, pairs, count, chunks, lines),
        in_specs=[near] * 6 + [anywhere] * count,
        out_specs=[near] * 5 + [anywhere] * 2 + [near] + [anywhere] * count,
        out_shape=[
            jax.ShapeDtypeStruct((segment, width), low),
            jax.ShapeDtypeStruct((segment, hidden), low),
            jax.ShapeDtypeStruct((segment, hidden), low),
            jax.ShapeDtypeStruct((segment, width), jnp.float32),
            jax.ShapeDtypeStruct((segment, width), low),
            jax.ShapeDtypeStruct((segment, width), low),
            jax.ShapeDtypeStruct((pairs, 3, length, LANES), low),
            jax.ShapeDtypeStruct((pairs, length, PAIR), jnp.float32),
            *wholes,
        ],
        scratch_shapes=[
            pltpu.VMEM((segment, width), jnp.float32),
            pltpu.VMEM((segment, 3 * width), low),
            pltpu.VMEM((2, 2, 4, 2, 2, lines, PIECE), low),
            pltpu.VMEM((2, hidden // 16, width), low),
            pltpu.VMEM((pairs, 3, length, LANES), low),
            pltpu.VMEM((pairs, length, LANES), low),
            dma((2, 2)), dma((2,)),
            dma((pairs, 3)), dma((pairs, 3)), dma((pairs, 3)), dma((pairs,)), dma((pairs,)), dma((pairs,)), dma((pairs,)),
            *Gather.scratch(len(chunks)),
        ],
        compiler_params=pltpu.CompilerParams(collective_id=identity, has_side_effects=True, vmem_limit_bytes=60 << 20),
        name="front",
    )(tokens, rel_low, norm_gains, norm_biases, hidden_biases, model_biases, *shards)
    return kept[:8], flat(kept[8:])


TAPS = 32
TILE = 128


def conv_kernel(wide_ref, taps_ref, out_ref, spread):
    length = out_ref.shape[1]
    spread[...] = wide_ref[0].astype(jnp.float32)
    for start in range(0, length, TILE):
        total = jnp.zeros((TILE, LANES), jnp.float32)
        for r in range(KERNEL):
            total = total + taps_ref[r : r + 1, :] * spread[start + r + 2 : start + r + 2 + TILE, :]
        out_ref[0, start : start + TILE, :] = total


def conv_back_kernel(grad_ref, wide_ref, taps_ref, value_ref, gate_ref, dvalue_ref, dgate_ref, kernel_ref, spread, grads, sums):
    length = value_ref.shape[0]
    spread[...] = wide_ref[0].astype(jnp.float32)
    grads[...] = grad_ref[0].astype(jnp.float32)

    @pl.when(pl.program_id(1) == 0)
    def _():
        sums[...] = jnp.zeros_like(sums)

    for start in range(0, length, TILE):
        own = grads[start : start + TILE, :]
        total = jnp.zeros((TILE, LANES), jnp.float32)
        for r in range(KERNEL):
            total = total + taps_ref[r : r + 1, :] * grads[start + KERNEL - 1 - r : start + KERNEL - 1 - r + TILE, :]
            both = own * spread[start + r + 2 : start + r + 2 + TILE, :]
            sums[r] += jnp.sum(both.reshape(TILE // 8, 8, LANES), axis=0)
        span = slice(start, start + TILE)
        opened = jax.nn.sigmoid(gate_ref[span, :])
        dvalue_ref[span, :] = (total * opened).astype(jnp.bfloat16)
        dgate_ref[span, :] = (total * value_ref[span, :] * (opened * (1.0 - opened))).astype(jnp.bfloat16)
    kernel_ref[...] = jnp.sum(sums[...], axis=1)


def padded_taps(dw_kernel):
    return jnp.pad(dw_kernel, ((0, TAPS - KERNEL), (0, 0)))


def depthwise(wide, dw_kernel):
    clips, lines, width = wide.shape
    length = lines - TAPS
    return pl.pallas_call(
        conv_kernel,
        grid=(width // LANES, clips),
        in_specs=[
            pl.BlockSpec((1, lines, LANES), lambda i, j: (j, 0, i)),
            pl.BlockSpec((TAPS, LANES), lambda i, j: (0, i)),
        ],
        out_specs=pl.BlockSpec((1, length, LANES), lambda i, j: (j, 0, i)),
        out_shape=jax.ShapeDtypeStruct((clips, length, width), jnp.float32),
        scratch_shapes=[pltpu.VMEM((lines, LANES), jnp.float32)],
        cost_estimate=pl.CostEstimate(flops=2 * KERNEL * clips * length * width, bytes_accessed=6 * clips * length * width, transcendentals=0),
        name="depthwise",
    )(wide, padded_taps(dw_kernel))


def depthwise_back(grad_wide, wide, dw_kernel, gate_input):
    clips, lines, width = wide.shape
    length, blocks = lines - TAPS, width // LANES
    tall = pl.BlockSpec((1, lines, LANES), lambda i, j: (j, 0, i))
    half = pl.BlockSpec((length, LANES), lambda i, j: (j, i))
    taps = pl.BlockSpec((TAPS, LANES), lambda i, j: (0, i))
    shape = jax.ShapeDtypeStruct((clips * length, width), jnp.bfloat16)
    dvalue, dgate, kernel_grad = pl.pallas_call(
        conv_back_kernel,
        grid=(blocks, clips),
        in_specs=[tall, tall, taps, half, pl.BlockSpec((length, LANES), lambda i, j: (j, blocks + i))],
        out_specs=[half, half, taps],
        out_shape=[shape, shape, jax.ShapeDtypeStruct((TAPS, width), jnp.float32)],
        scratch_shapes=[
            pltpu.VMEM((lines, LANES), jnp.float32),
            pltpu.VMEM((lines, LANES), jnp.float32),
            pltpu.VMEM((TAPS, 8, LANES), jnp.float32),
        ],
        cost_estimate=pl.CostEstimate(flops=4 * KERNEL * clips * length * width, bytes_accessed=16 * clips * length * width, transcendentals=clips * length * width),
        name="depthwise_back",
    )(grad_wide, wide, padded_taps(dw_kernel), gate_input, gate_input)
    return jnp.concatenate([dvalue, dgate], axis=1), kernel_grad[:KERNEL]


def feed_forward(values, norm_gain, norm_shift, weight_up, bias_up, weight_down, bias_down):
    normed = layer_norm(values, norm_gain, norm_shift).astype(jnp.bfloat16)
    hidden = product(normed, weight_up) + bias_up
    active = jax.nn.silu(hidden).astype(jnp.bfloat16)
    branch = product(active, weight_down) + bias_down
    return (branch, (normed, hidden, active))


def feed_backward(residual_grad, values, kept_parts, norm_gain, norm_shift, weight_up, weight_down):
    normed, hidden, active = kept_parts
    branch_grad = (0.5 * residual_grad).astype(jnp.bfloat16)
    down_bias_grad = jnp.sum(branch_grad.astype(jnp.float32), axis=0)
    active_grad = times_transposed(branch_grad, weight_down)
    silu_pull = jax.vjp(jax.nn.silu, hidden)[1]
    hidden_grad = silu_pull(active_grad)[0].astype(jnp.bfloat16)
    up_bias_grad = jnp.sum(hidden_grad.astype(jnp.float32), axis=0)
    normed_grad = times_transposed(hidden_grad, weight_up)
    norm_pull = jax.vjp(layer_norm, values, norm_gain, norm_shift)[1]
    values_grad, gain_grad, shift_grad = norm_pull(normed_grad)
    return (
        residual_grad + values_grad,
        (normed, hidden_grad),
        up_bias_grad,
        (active, branch_grad),
        down_bias_grad,
        gain_grad,
        shift_grad,
    )


def heads_of(projected, clip_count, segment, rel_low):
    parts = [
        lax.all_to_all(part.reshape(clip_count, segment, -1), "seq", split_axis=2, concat_axis=1, tiled=True)
        for part in jnp.split(projected, 3, axis=1)
    ]
    merged, log_totals = attend(*parts, rel_low)
    attn_seq = lax.all_to_all(merged, "seq", split_axis=1, concat_axis=2, tiled=True)
    return attn_seq.reshape(clip_count * segment, -1), parts, log_totals


def heads_back(out_grad, parts, log_totals, clip_count, segment, rel_low):
    merged = lax.all_to_all(
        out_grad.reshape(clip_count, segment, -1), "seq", split_axis=2, concat_axis=1, tiled=True
    )
    *grads, table_parts = attend_back(*parts, merged, log_totals, rel_low)
    grads = [
        lax.all_to_all(grad, "seq", split_axis=1, concat_axis=2, tiled=True).reshape(clip_count * segment, -1)
        for grad in grads
    ]
    return jnp.concatenate(grads, axis=1), jnp.sum(table_parts, axis=0)


def spread_sums(factors, small):
    sums = []
    for left, right in factors:
        part = lax.psum_scatter(contract_rows(left, right).astype(jnp.bfloat16), "seq", scatter_dimension=1, tiled=True)
        part = lax.psum_scatter(part, "fsdp", scatter_dimension=0, tiled=True)
        sums.append(part.astype(jnp.float32))
    return (*sums, lax.psum(small, ("seq", "fsdp")))


def stacked(rows):
    lines = jnp.concatenate([row.reshape(-1, rows[0].shape[-1]) for row in rows])
    return jnp.pad(lines, ((0, -lines.shape[0] % 8), (0, 0)))


def body(
    tokens,
    cotangent,
    ffn1_up,
    ffn1_down,
    qkv_weight,
    out_weight,
    conv_in,
    conv_out,
    ffn2_up,
    ffn2_down,
    norm_gains,
    norm_biases,
    hidden_biases,
    model_biases,
    dw_kernel,
    rel_table,
):
    clip_count, segment, model_width = tokens.shape
    row_count = clip_count * segment
    rim_width = KERNEL - 1
    close = lax.axis_size("seq") == 2 and lax.axis_size("fsdp") == 16 and clip_count == 1
    low = jnp.bfloat16
    shards = [
        weight.astype(low)
        for weight in (ffn1_up, ffn1_down, qkv_weight, out_weight, conv_in, conv_out, ffn2_up, ffn2_down)
    ]
    rel_low = padded_table(rel_table)
    input_rows = tokens.reshape(row_count, model_width).astype(jnp.float32)
    if close:
        fronts, weights = front(
            tokens.reshape(row_count, model_width), rel_low, norm_gains, norm_biases, hidden_biases, model_biases, shards, 0
        )
        normed_one, hidden_one, active_one, after_one, normed_attn, attn_rows, kept_heads, log_totals = fronts
        kept_one = (normed_one, hidden_one.astype(jnp.float32), active_one)
    else:
        weights = [lax.all_gather(shard, "fsdp", axis=0, tiled=True) for shard in shards]
        branch_one, kept_one = feed_forward(
            input_rows,
            norm_gains[0],
            norm_biases[0],
            weights[0],
            hidden_biases[0],
            weights[1],
            model_biases[0],
        )
        after_one = input_rows + 0.5 * branch_one
        normed_attn = layer_norm(after_one, norm_gains[1], norm_biases[1]).astype(low)
        project_bias = jnp.concatenate([model_biases[1], jnp.zeros_like(model_biases[1]), model_biases[2]])
        projected = (product(normed_attn, weights[2]) + project_bias).astype(low)
        attn_rows, kept_heads, log_totals = heads_of(projected, clip_count, segment, rel_low)
    up_one, down_one, qkv_full, out_full, conv_first, conv_second, up_two, down_two = weights
    after_two = after_one + product(attn_rows, out_full) + model_biases[3]
    normed_conv = layer_norm(after_two, norm_gains[2], norm_biases[2]).astype(low)
    gate_input = product(normed_conv, conv_first)
    glu_out = glu_function(gate_input).astype(low).reshape(clip_count, segment, model_width)
    glu_before = passed_along(glu_out[:, segment - rim_width :], "seq", 1)
    margin = jnp.zeros((clip_count, TAPS - rim_width, model_width), low)
    glu_wide = jnp.concatenate([margin, glu_before, glu_out], axis=1)
    mixed_flat = depthwise(glu_wide, dw_kernel).reshape(row_count, model_width)
    swished = conv_tail(mixed_flat, norm_gains[3], norm_biases[3]).astype(low)
    after_three = after_two + product(swished, conv_second)
    branch_two, kept_two = feed_forward(
        after_three,
        norm_gains[4],
        norm_biases[4],
        up_two,
        hidden_biases[1],
        down_two,
        model_biases[4],
    )
    after_four = after_three + 0.5 * branch_two
    final_rows, final_pull = jax.vjp(layer_norm, after_four, norm_gains[5], norm_biases[5])
    output = final_rows.astype(low).reshape(clip_count, segment, model_width)
    grad_four, gain_five, shift_five = final_pull(
        cotangent.reshape(row_count, model_width).astype(jnp.float32)
    )
    grad_three, up_two_factors, up_two_bias, down_two_factors, down_two_bias, gain_four, shift_four = (
        feed_backward(
            grad_four, after_three, kept_two, norm_gains[4], norm_biases[4], up_two, down_two
        )
    )
    conv_grad = grad_three.astype(low)
    swished_grad = times_transposed(conv_grad, conv_second)
    tail_pull = jax.vjp(conv_tail, mixed_flat, norm_gains[3], norm_biases[3])[1]
    mixed_grad, gain_three, shift_three = tail_pull(swished_grad)
    mixed_low = mixed_grad.astype(low).reshape(clip_count, segment, model_width)
    mixed_after = passed_along(mixed_low[:, 0:rim_width], "seq", -1)
    mixed_wide = jnp.concatenate([mixed_low, mixed_after, margin], axis=1)
    gate_grad, kernel_grad = depthwise_back(mixed_wide, glu_wide, dw_kernel, gate_input)
    conv_norm_pull = jax.vjp(layer_norm, after_two, norm_gains[2], norm_biases[2])[1]
    values_grad, gain_two, shift_two = conv_norm_pull(times_transposed(gate_grad, conv_first))
    grad_two = grad_three + values_grad
    later_small = stacked(
        [gain_two, gain_three, gain_four, gain_five, shift_two, shift_three, shift_four, shift_five]
        + [up_two_bias, down_two_bias, kernel_grad]
    )
    later_factors = [down_two_factors, up_two_factors, (swished, conv_grad), (normed_conv, gate_grad)]
    attn_grad = grad_two.astype(low)
    out_bias_grad = jnp.sum(attn_grad.astype(jnp.float32), axis=0)
    merged_grad = times_transposed(attn_grad, out_full).astype(low)
    if close:
        projected_grad, table_parts, *later_sums = attend_back_split(
            merged_grad, kept_heads, log_totals, rel_low, later_factors, later_small, 3
        )
    else:
        projected_grad, table_parts = heads_back(
            merged_grad, kept_heads, log_totals, clip_count, segment, rel_low
        )
        later_sums = spread_sums(later_factors, later_small)
    down_two_sum, up_two_sum, conv_second_sum, conv_first_sum, later_sum = later_sums
    table_grad = jnp.sum(table_parts, axis=0).T[::-1][:BUCKETS]
    query_bias_grad = jnp.sum(projected_grad[:, :model_width].astype(jnp.float32), axis=0)
    value_bias_grad = jnp.sum(projected_grad[:, 2 * model_width :].astype(jnp.float32), axis=0)
    attn_norm_pull = jax.vjp(layer_norm, after_one, norm_gains[1], norm_biases[1])[1]
    values_grad, gain_one, shift_one = attn_norm_pull(times_transposed(projected_grad, qkv_full))
    grad_one = grad_two + values_grad
    grad_zero, up_one_factors, up_one_bias, down_one_factors, down_one_bias, gain_zero, shift_zero = (
        feed_backward(
            grad_one, input_rows, kept_one, norm_gains[0], norm_biases[0], up_one, down_one
        )
    )
    input_grad = grad_zero.astype(low).reshape(clip_count, segment, model_width)
    table_flat = table_grad.reshape(-1)
    table_rows = jnp.pad(table_flat, (0, -table_flat.size % model_width)).reshape(-1, model_width)
    early_small = stacked(
        [gain_zero, gain_one, shift_zero, shift_one, up_one_bias]
        + [down_one_bias, query_bias_grad, value_bias_grad, out_bias_grad, table_rows]
    )
    sums_of = partial(scatter_sums, identity=4) if close else spread_sums
    up_one_sum, down_one_sum, qkv_sum, out_sum, early_sum = sums_of(
        [up_one_factors, down_one_factors, (normed_attn, projected_grad), (attn_rows, attn_grad)],
        early_small,
    )
    hidden_rows = up_one_bias.size // model_width
    after_hidden = 4 + hidden_rows
    table_at = after_hidden + 4
    table_sum = early_sum[table_at : table_at + table_rows.shape[0]].reshape(-1)[: table_flat.size]
    later_hidden = 8 + hidden_rows
    return (
        output,
        input_grad,
        up_one_sum,
        down_one_sum,
        qkv_sum,
        out_sum,
        conv_first_sum,
        conv_second_sum,
        up_two_sum,
        down_two_sum,
        jnp.concatenate([early_sum[0:2], later_sum[0:4]]),
        jnp.concatenate([early_sum[2:4], later_sum[4:5]]),
        later_sum[5:8],
        jnp.stack([early_sum[4:after_hidden].reshape(-1), later_sum[8:later_hidden].reshape(-1)]),
        early_sum[after_hidden : after_hidden + 3],
        jnp.concatenate([early_sum[after_hidden + 3 : table_at], later_sum[later_hidden : later_hidden + 1]]),
        later_sum[later_hidden + 1 : later_hidden + 1 + KERNEL],
        table_sum.reshape(table_grad.shape),
    )


def solution(mesh):
    in_specs = (
        P("fsdp", "seq", None),
        P("fsdp", "seq", None),
        P("fsdp", None),
        P("fsdp", None),
        P("fsdp", None),
        P("fsdp", None),
        P("fsdp", None),
        P("fsdp", None),
        P("fsdp", None),
        P("fsdp", None),
        P(),
        P(),
        P(),
        P(),
        P(),
        P(),
    )
    out_specs = (
        P("fsdp", "seq", None),
        P("fsdp", "seq", None),
        P("fsdp", "seq"),
        P("fsdp", "seq"),
        P("fsdp", "seq"),
        P("fsdp", "seq"),
        P("fsdp", "seq"),
        P("fsdp", "seq"),
        P("fsdp", "seq"),
        P("fsdp", "seq"),
        P(),
        P(),
        P(),
        P(),
        P(),
        P(),
        P(),
        P(),
    )
    return jax.shard_map(body, mesh=mesh, in_specs=in_specs, out_specs=out_specs, check_vma=False)
```

```python
import functools
from functools import partial

import jax
import jax.numpy as jnp
from jax import lax
from jax.experimental import pallas as pl
from jax.experimental.pallas import tpu as pltpu
from jax.sharding import PartitionSpec as P

HEAD = 64
KERNEL = 31
LEFT = 64
RIGHT = 8
BUCKETS = 73


EPSILON = 1e-05


def passed_along(value, axis, by):
    length = lax.axis_size(axis)
    pairs = [(i, i + by) for i in range(length) if 0 <= i + by < length]
    return lax.ppermute(value, axis, pairs)


def layer_norm(values, norm_gain, norm_shift):
    center = values - jnp.mean(values, axis=-1, keepdims=True)
    spread = jnp.mean(center * center, axis=-1, keepdims=True)
    return center * lax.rsqrt(spread + EPSILON) * norm_gain + norm_shift


def product(former, latter):
    return jnp.dot(former, latter, preferred_element_type=jnp.float32)


def contract_rows(former, latter):
    return lax.dot_general(
        former, latter, (((0,), (0,)), ((), ())), preferred_element_type=jnp.float32
    )


def times_transposed(former, latter):
    return lax.dot_general(
        former, latter, (((1,), (1,)), ((), ())), preferred_element_type=jnp.float32
    )


def glu_function(gate_input):
    half_width = gate_input.shape[1] // 2
    return gate_input[:, :half_width] * jax.nn.sigmoid(gate_input[:, half_width:])


def conv_tail(mixed_rows, norm_gain, norm_shift):
    return jax.nn.silu(layer_norm(mixed_rows, norm_gain, norm_shift))


MESH = pl.DeviceIdType.MESH
PIECE = 256
LAG = 3
BLOCK = 512
WAIT = 2
OWN_SLOTS = 8
AWAY_SLOTS = 3


class Place:
    def __init__(self):
        self.x = lax.axis_index("seq")
        self.f = lax.axis_index("fsdp")
        self.c = lax.rem(self.f, 2)
        self.y = lax.rem(lax.div(self.f, 2), 2)
        self.z = lax.div(self.f, 4)

    def across(self):
        return (1 - self.x, self.f)

    def twin(self):
        return (self.x, self.f + 1 - 2 * self.c)

    def beside(self):
        return (self.x, self.f + 2 - 4 * self.y)

    def along(self, step):
        return (self.x, lax.rem(self.z + step, 4) * 4 + self.y * 2 + self.c)

    def greet(self):
        barrier = pltpu.get_barrier_semaphore()
        peers = [self.across(), self.twin(), self.beside()] + [self.along(s) for s in (1, 2, 3)]
        for peer in peers:
            pl.semaphore_signal(barrier, inc=1, device_id=peer, device_id_type=MESH)
        pl.semaphore_wait(barrier, len(peers))


def chunks_of(shapes, lines, crossing, piece):
    shares = [(part, whole) for blocks, part, whole in crossing for _ in range(blocks)]
    found = []
    for index, (rows, width) in enumerate(shapes):
        for line in range(0, rows, lines):
            for column in range(0, width // 2, piece):
                count = len(found)
                part, whole = shares[min(count, len(shares) - 1)]
                found.append((index, line, column, (count + 1) * part // whole > count * part // whole))
    return found


class Sent:
    def __init__(self, source, target, send_sem, recv_sem, device):
        self.parts = dict(src_ref=source, dst_ref=target, send_sem=send_sem, recv_sem=recv_sem, device_id=device, device_id_type=MESH)

    def start(self):
        pltpu.make_async_remote_copy(**self.parts).start()

    def wait_recv(self):
        pltpu.make_async_remote_copy(**self.parts).wait_recv()

    def wait_send(self):
        pltpu.make_async_remote_copy(**self.parts).wait_send()


class Near:
    def __init__(self, source, target, sem):
        self.parts = (source, target, sem)

    def start(self):
        pltpu.make_async_copy(*self.parts).start()

    def wait(self):
        pltpu.make_async_copy(*self.parts).wait()


class Gather:
    def __init__(self, me, shards, wholes, chunks, lines, sems):
        self.me, self.shards, self.wholes, self.chunks, self.lines = me, shards, wholes, chunks, lines
        (self.own_sem, self.z_send, self.z_recv, self.y_send, self.y_recv, self.x_send, self.x_recv, self.c_send, self.c_recv) = sems
        self.steps = len(chunks) + 3 * LAG
        self.number = 0
        self.whole = set()

    @staticmethod
    def scratch(total):
        dma = pltpu.SemaphoreType.DMA
        return [
            dma((total, 2)), dma((total, 2, 3)), dma((total, 2, 3)), dma((total, 2)), dma((total, 2)),
            dma((total,)), dma((total,)), dma((total, 2)), dma((total, 2)),
        ]

    def halves(self, chunk):
        index, line, column, early = chunk
        half = self.shards[index].shape[1] // 2
        if early:
            return [pl.ds(pl.multiple_of(self.me.x * half + column, PIECE), PIECE)]
        return [pl.ds(column, PIECE), pl.ds(half + column, PIECE)]

    def both(self, chunk):
        half = self.shards[chunk[0]].shape[1] // 2
        return [pl.ds(chunk[2], PIECE), pl.ds(half + chunk[2], PIECE)]

    def make(self, t, kind):
        index, line, column, early = self.chunks[t]
        shard, whole, rows, me = self.shards[index], self.wholes[index], pl.ds(line, self.lines), self.me
        halves = self.halves(self.chunks[t])
        if kind == "own":
            return [
                Near(shard.at[rows, cols], whole.at[me.z, me.y, me.c, rows, cols], self.own_sem.at[t, j])
                for j, cols in enumerate(halves)
            ]
        if kind == "z":
            return [
                Sent(shard.at[rows, cols], whole.at[me.z, me.y, me.c, rows, cols], self.z_send.at[t, j, s - 1], self.z_recv.at[t, j, s - 1], me.along(s))
                for j, cols in enumerate(halves)
                for s in (1, 2, 3)
            ]
        if kind == "y":
            views = [whole.at[:, me.y, me.c, rows, cols] for cols in halves]
            return [Sent(view, view, self.y_send.at[t, j], self.y_recv.at[t, j], me.beside()) for j, view in enumerate(views)]
        if kind == "x":
            views = [whole.at[:, :, me.c, rows, halves[0]]] if early else []
            return [Sent(view, view, self.x_send.at[t], self.x_recv.at[t], me.across()) for view in views]
        views = [whole.at[:, :, me.c, rows, cols] for cols in self.both(self.chunks[t])]
        return [Sent(view, view, self.c_send.at[t, j], self.c_recv.at[t, j], me.twin()) for j, view in enumerate(views)]

    def start(self, t, kind):
        for copy in self.make(t, kind):
            copy.start()

    def arrive(self, t, kind):
        for copy in self.make(t, kind):
            copy.wait_recv()

    def first(self, t):
        self.start(t, "own")
        self.start(t, "z")

    def second(self, t):
        for copy in self.make(t, "own"):
            copy.wait()
        self.arrive(t, "z")
        self.start(t, "y")

    def third(self, t):
        self.arrive(t, "y")
        self.start(t, "x")

    def fourth(self, t):
        self.arrive(t, "x")
        self.start(t, "c")

    def step(self, number):
        for stage, phase in reversed(list(enumerate((self.first, self.second, self.third, self.fourth)))):
            if 0 <= number - LAG * stage < len(self.chunks):
                phase(number - LAG * stage)

    def run(self, number):
        while self.number < min(number, self.steps):
            self.step(self.number)
            self.number += 1

    def landed(self, t):
        if t not in self.whole:
            self.arrive(t, "c")
            self.whole.add(t)

    def finish(self):
        for t in range(len(self.chunks)):
            self.landed(t)
            for kind in "zyxc":
                for copy in self.make(t, kind):
                    copy.wait_send()


def gather_plan(shards, crossing):
    shapes = [shard.shape for shard in shards]
    lines = min(rows for rows, _ in shapes)
    wholes = [jax.ShapeDtypeStruct((4, 2, 2, *shape), jnp.bfloat16) for shape in shapes]
    return wholes, chunks_of(shapes, lines, crossing, PIECE), lines


def flat(wholes):
    return [whole.reshape(-1, whole.shape[-1]) for whole in wholes]


class Scatter:
    def __init__(self, me, lefts, rights, small, outs, small_out, chunks, lines, scratch, small_from=0):
        self.me, self.lefts, self.rights, self.small, self.outs, self.small_out = me, lefts, rights, small, outs, small_out
        self.chunks, self.lines, self.small_from, self.number = chunks, lines, small_from, 0
        (self.strips, self.cols, self.turned, self.own, self.away, self.core_in, self.early_in, self.late_in, self.y_in, self.z_in,
         self.end_in, self.done, self.strip_sem, self.cols_sem, self.done_sem,
         self.c_send, self.c_recv, self.x_send, self.x_recv, self.y_send, self.y_recv, self.z_send, self.z_recv,
         self.small_held, self.small_in, self.small_z, self.small_send, self.small_recv, self.small_z_send, self.small_z_recv) = scratch
        self.order = [sum(other[3] == chunk[3] for other in chunks[:t]) for t, chunk in enumerate(chunks)]
        self.steps = len(chunks) + 1 + 4 * WAIT

    @staticmethod
    def scratch(chunks, lines, tokens, small):
        dma, low, total = pltpu.SemaphoreType.DMA, jnp.bfloat16, len(chunks)
        early = sum(chunk[3] for chunk in chunks)
        late = total - early
        return [
            pltpu.VMEM((tokens, 32 * lines), low),
            pltpu.VMEM((2, 2, tokens, BLOCK), low),
            pltpu.VMEM((2, 16 * lines, tokens), low),
            pltpu.VMEM((OWN_SLOTS, 2, 4, 2, lines, BLOCK), low),
            pltpu.VMEM((AWAY_SLOTS, 2, 4, 2, lines, BLOCK), low),
            pltpu.VMEM((total, 2, 4, 2, lines, BLOCK), low),
            pltpu.VMEM((early, 4, 2, lines, BLOCK), low),
            pltpu.VMEM((late, 2, 4, lines, BLOCK), low),
            pltpu.VMEM((early, 4, lines, BLOCK), low),
            pltpu.VMEM((late, 3, 2, lines, BLOCK), low),
            pltpu.VMEM((total, 3, lines, BLOCK), low),
            pltpu.VMEM((total, lines, BLOCK), jnp.float32),
            dma((16,)), dma((2, 2)), dma((total,)),
            dma((total, 2)), dma((total, 2)), dma((total,)), dma((total,)),
            dma((total,)), dma((total,)), dma((total, 3)), dma((total, 3)),
            pltpu.VMEM((4, *small), jnp.float32), pltpu.VMEM((3, *small), jnp.float32), pltpu.VMEM((4, *small), jnp.float32),
            dma((3,)), dma((3,)), dma((3,)), dma((3,)),
        ]

    def columns(self, t, j):
        index, line, column, early = self.chunks[t]
        return pl.ds(j * (self.rights[index].shape[1] // 2) + column, BLOCK)

    def turns(self, t):
        index, line, column, early = self.chunks[t]
        if self.lefts[index].shape[1] > 16 * self.lines:
            return column == 0 and line % (2 * self.lines) == 0, line // self.lines % 2
        return column == 0, 0

    def loads(self, t):
        index, line, column, early = self.chunks[t]
        left, wide = self.lefts[index], 2 * self.lines
        copies = [Near(self.rights[index].at[:, self.columns(t, j)], self.cols.at[t % 2, j], self.cols_sem.at[t % 2, j]) for j in range(2)]
        if self.turns(t)[0]:
            rows = left.shape[1] // 16
            if rows > self.lines:
                copies += [
                    Near(left.at[:, pl.ds(i * rows + line, wide)], self.strips.at[:, pl.ds(i * wide, wide)], self.strip_sem.at[i])
                    for i in range(16)
                ]
            else:
                copies.append(Near(left, self.strips.at[:, pl.ds(0, 8 * wide)], self.strip_sem.at[0]))
        return copies

    def load(self, t):
        for copy in self.loads(t):
            copy.start()

    def turn(self, t):
        lines, me = self.lines, self.me
        left = self.lefts[self.chunks[t][0]]

        def place(core, block):
            return pl.ds(pl.multiple_of((lax.rem(core + me.c, 2) * 8 + block) * lines, lines), lines)

        if left.shape[1] > 16 * lines:

            @pl.loop(0, 16)
            def _(i):
                block = jnp.transpose(self.strips[:, pl.ds(pl.multiple_of(i * 2 * lines, 2 * lines), 2 * lines)])
                rows = place(lax.rem(i, 2), lax.div(i, 2))
                self.turned[0, rows, :] = block[:lines]
                self.turned[1, rows, :] = block[lines:]

        else:

            @pl.loop(0, 8)
            def _(i):
                block = jnp.transpose(self.strips[:, pl.ds(pl.multiple_of(i * 2 * lines, 2 * lines), 2 * lines)])
                self.turned[0, place(0, i), :] = block[:lines]
                self.turned[0, place(1, i), :] = block[lines:]

    def make(self, t, kind):
        index, line, column, early = self.chunks[t]
        me, own, slot, order = self.me, self.own, t % OWN_SLOTS, self.order[t]
        if kind == "c":
            return [
                Sent(self.away.at[t % AWAY_SLOTS, j], self.core_in.at[t, j], self.c_send.at[t, j], self.c_recv.at[t, j], me.twin())
                for j in range(2)
            ]
        if kind == "x":
            source, target = (
                (own.at[slot, 1 - me.x], self.early_in.at[order]) if early
                else (own.at[slot, 1 - me.x, me.z, me.y], self.end_in.at[t, 0])
            )
            return [Sent(source, target, self.x_send.at[t], self.x_recv.at[t], me.across())]
        if kind == "y":
            source, target = (
                (own.at[slot, me.x, :, 1 - me.y], self.y_in.at[order]) if early
                else (own.at[slot, :, :, 1 - me.y], self.late_in.at[order])
            )
            return [Sent(source, target, self.y_send.at[t], self.y_recv.at[t], me.beside())]
        copies = []
        for s in (1, 2, 3):
            z = lax.rem(me.z + s, 4)
            source, target = (
                (own.at[slot, me.x, z, me.y], self.end_in.at[t, s - 1]) if early
                else (own.at[slot, :, z, me.y], self.z_in.at[order, s - 1])
            )
            copies.append(Sent(source, target, self.z_send.at[t, s - 1], self.z_recv.at[t, s - 1], me.along(s)))
        return copies

    def finished(self, t):
        index, line, column, early = self.chunks[t]
        return Near(self.done.at[t], self.outs[index].at[pl.ds(line, self.lines), pl.ds(column, BLOCK)], self.done_sem.at[t])

    def make_small(self, stage):
        me = self.me
        if stage < 3:
            peer = (me.twin, me.across, me.beside)[stage]()
            return [Sent(self.small_held.at[stage], self.small_in.at[stage], self.small_send.at[stage], self.small_recv.at[stage], peer)]
        return [
            Sent(self.small_held.at[3], self.small_z.at[me.z], self.small_z_send.at[s - 1], self.small_z_recv.at[s - 1], me.along(s))
            for s in (1, 2, 3)
        ]

    def start(self, t, kind):
        for copy in self.make(t, kind):
            copy.start()

    def arrive(self, t, kind):
        for copy in self.make(t, kind):
            copy.wait_recv()

    def leave(self, t, kinds):
        for kind in kinds:
            for copy in self.make(t, kind):
                copy.wait_send()

    def first(self, t):
        lines = self.lines
        for copy in self.loads(t):
            copy.wait()
        fresh, which = self.turns(t)
        if fresh:
            self.turn(t)
        if t >= AWAY_SLOTS:
            self.leave(t - AWAY_SLOTS, "c")
        if t >= OWN_SLOTS:
            self.leave(t - OWN_SLOTS, "zyx")
        for other in (1, 0):
            target, slot = (self.own, t % OWN_SLOTS) if other == 0 else (self.away, t % AWAY_SLOTS)
            for j in range(2):

                @pl.loop(0, 2)
                def _(pair):
                    rows = pl.ds(pl.multiple_of((other * 2 + pair) * 4 * lines, 4 * lines), 4 * lines)
                    part = nn(self.turned[which, rows, :], self.cols[t % 2, j]).astype(jnp.bfloat16)
                    for z in range(2):
                        for y in range(2):
                            target[slot, j, 2 * pair + z, y] = part[(2 * z + y) * lines : (2 * z + y + 1) * lines]

                if other == 1:
                    self.make(t, "c")[j].start()

    def second(self, t):
        early, slot, own = self.chunks[t][3], t % OWN_SLOTS, self.own
        self.arrive(t, "c")
        for j in range(2):
            for z in range(4):
                own[slot, j, z] = sums(own[slot, j, z], self.core_in[t, j, z])
        self.start(t, "x" if early else "y")

    def third(self, t):
        early, slot, me, own, order = self.chunks[t][3], t % OWN_SLOTS, self.me, self.own, self.order[t]
        if early:
            self.arrive(t, "x")
            for z in range(4):
                own[slot, me.x, z] = sums(own[slot, me.x, z], self.early_in[order, z])
            self.start(t, "y")
        else:
            self.arrive(t, "y")
            for j in range(2):
                for z in range(4):
                    own[slot, j, z, me.y] = sums(own[slot, j, z, me.y], self.late_in[order, j, z])
            self.start(t, "z")

    def fourth(self, t):
        early, slot, me, own, order = self.chunks[t][3], t % OWN_SLOTS, self.me, self.own, self.order[t]
        if early:
            self.arrive(t, "y")
            for z in range(4):
                own[slot, me.x, z, me.y] = sums(own[slot, me.x, z, me.y], self.y_in[order, z])
            self.start(t, "z")
        else:
            self.arrive(t, "z")
            for j in range(2):
                value = own[slot, j, me.z, me.y].astype(jnp.float32)
                for s in range(3):
                    value = value + self.z_in[order, s, j].astype(jnp.float32)
                own[slot, j, me.z, me.y] = value.astype(jnp.bfloat16)
            self.start(t, "x")

    def fifth(self, t):
        early, slot, me = self.chunks[t][3], t % OWN_SLOTS, self.me
        self.arrive(t, "z" if early else "x")
        value = self.own[slot, me.x, me.z, me.y].astype(jnp.float32)
        for s in range(3 if early else 1):
            value = value + self.end_in[t, s].astype(jnp.float32)
        self.done[t] = value
        self.finished(t).start()

    def small_step(self, stage):
        if stage == 0:
            self.small_held[0] = self.small[...]
        else:
            self.make_small(stage - 1)[0].wait_recv()
            self.small_held[stage] = self.small_held[stage - 1] + self.small_in[stage - 1]
        if stage == 3:
            self.small_z[self.me.z] = self.small_held[3]
        for copy in self.make_small(stage):
            copy.start()

    def step(self, number):
        phases = ((1, self.first), (1 + WAIT, self.second), (1 + 2 * WAIT, self.third), (1 + 3 * WAIT, self.fourth), (1 + 4 * WAIT, self.fifth))
        for lag, phase in reversed(((0, self.load), *phases)):
            if 0 <= number - lag < len(self.chunks):
                phase(number - lag)
        stage = (number - self.small_from) // WAIT
        if (number - self.small_from) % WAIT == 0 and 0 <= stage < 4:
            self.small_step(stage)

    def run(self, number):
        while self.number < min(number, self.steps):
            self.step(self.number)
            self.number += 1

    def finish(self):
        for copy in self.make_small(3):
            copy.wait_recv()
        for stage in range(4):
            for copy in self.make_small(stage):
                copy.wait_send()
        self.small_out[...] = (self.small_z[0] + self.small_z[1]) + (self.small_z[2] + self.small_z[3])
        total = len(self.chunks)
        for t in range(total):
            self.finished(t).wait()
            if t + AWAY_SLOTS >= total:
                self.leave(t, "c")
            if t + OWN_SLOTS >= total:
                self.leave(t, "zyx")


def sums(former, latter):
    return (former.astype(jnp.float32) + latter.astype(jnp.float32)).astype(jnp.bfloat16)


def scatter_kernel(count, chunks, lines, *refs):
    me = Place()
    me.greet()
    scatter = Scatter(
        me, refs[:count], refs[count : 2 * count], refs[2 * count], refs[2 * count + 1 : 3 * count + 1], refs[3 * count + 1],
        chunks, lines, refs[3 * count + 2 :],
    )
    scatter.run(scatter.steps)
    scatter.finish()


def scatter_plan(factors, small, crossing):
    shapes = [(left.shape[1] // 16, right.shape[1]) for left, right in factors]
    lines = min(rows for rows, _ in shapes)
    anywhere, near = pl.BlockSpec(memory_space=pl.ANY), pl.BlockSpec(memory_space=pltpu.VMEM)
    outs = [jax.ShapeDtypeStruct((rows, width // 2), jnp.float32) for rows, width in shapes]
    outs.append(jax.ShapeDtypeStruct(small.shape, jnp.float32))
    chunks = chunks_of(shapes, lines, crossing, BLOCK)
    count = len(factors)
    operands = [left for left, _ in factors] + [right for _, right in factors] + [small]
    in_specs = [anywhere] * (2 * count) + [near]
    scratch = Scatter.scratch(chunks, lines, factors[0][0].shape[0], small.shape)
    return operands, in_specs, outs, [anywhere] * count + [near], scratch, chunks, lines


def scatter_sums(factors, small, identity):
    operands, in_specs, outs, out_specs, scratch, chunks, lines = scatter_plan(factors, small, [(1, 2, 3)])
    return pl.pallas_call(
        functools.partial(scatter_kernel, len(factors), chunks, lines),
        in_specs=in_specs,
        out_specs=out_specs,
        out_shape=outs,
        scratch_shapes=scratch,
        compiler_params=pltpu.CompilerParams(collective_id=identity, has_side_effects=True, vmem_limit_bytes=60 << 20),
        name="scatter_sums",
    )(*operands)


PAIR = 2
LANES = 128
FWD_ROWS = 256
BACK_ROWS = 256


def nt(former, latter):
    return lax.dot_general(former, latter, (((1,), (1,)), ((), ())), preferred_element_type=jnp.float32)


def nn(former, latter):
    return lax.dot_general(former, latter, (((1,), (0,)), ((), ())), preferred_element_type=jnp.float32)


def window_of(start, rows, length):
    low, high = start - LANES, start + rows + LANES
    return max(low, 0), min(high, length), max(low, 0) - low


def window_buckets(rows):
    width = rows + 2 * LANES
    places = lax.broadcasted_iota(jnp.int32, (rows, width), 1)
    lines = lax.broadcasted_iota(jnp.int32, (rows, width), 0)
    return places - lines - (LANES - LEFT)


def biased_scores(scores, position, start, rows, length):
    width = rows + 2 * LANES
    low, high, skip = window_of(start, rows, length)
    wide = jnp.concatenate([position, jnp.zeros((rows, width - LANES), jnp.float32)], axis=1)
    band = pltpu.roll(wide, LANES - LEFT, 1, stride=1, stride_axis=0)
    first, last = position[:, 0:1], position[:, BUCKETS - 1 : BUCKETS]
    bucket = window_buckets(rows)
    band = jnp.where(bucket <= 0, first, jnp.where(bucket >= BUCKETS - 1, last, band))
    pieces = []
    if low > 0:
        pieces.append(scores[:, :low] + first)
    pieces.append(scores[:, low:high] + band[:, skip : skip + high - low])
    if high < length:
        pieces.append(scores[:, high:] + last)
    return pieces[0] if len(pieces) == 1 else jnp.concatenate(pieces, axis=1)


def bucket_sums(score_grad, mirror, start, rows, length):
    width = rows + 2 * LANES
    low, high, skip = window_of(start, rows, length)
    inner = score_grad[:, low:high]
    pieces = []
    if skip > 0:
        pieces.append(jnp.zeros((rows, skip), jnp.float32))
    pieces.append(inner)
    if skip + high - low < width:
        pieces.append(jnp.zeros((rows, width - skip - high + low), jnp.float32))
    wide = pieces[0] if len(pieces) == 1 else jnp.concatenate(pieces, axis=1)
    bucket = window_buckets(rows)
    first = jnp.sum(jnp.where(bucket <= 0, wide, 0.0), axis=1, keepdims=True)
    last = jnp.sum(jnp.where(bucket >= BUCKETS - 1, wide, 0.0), axis=1, keepdims=True)
    if low > 0:
        first = first + jnp.sum(score_grad[:, :low], axis=1, keepdims=True)
    if high < length:
        last = last + jnp.sum(score_grad[:, high:], axis=1, keepdims=True)
    turned = nn(wide.astype(jnp.bfloat16), mirror)
    band = pltpu.roll(turned, (LANES + LANES - LEFT) % width, 1, stride=1, stride_axis=0)[:, :LANES]
    bucket = LANES - 1 - lax.broadcasted_iota(jnp.int32, (rows, LANES), 1)
    return jnp.where(bucket == 0, first, jnp.where(bucket == BUCKETS - 1, last, jnp.where(bucket < BUCKETS, band, 0.0)))


def mirror_of(width):
    lines = lax.broadcasted_iota(jnp.int32, (width, width), 0)
    places = lax.broadcasted_iota(jnp.int32, (width, width), 1)
    return jnp.where(lines + places == width - 1, 1.0, 0.0).astype(jnp.bfloat16)


def attend_pair(q_ref, k_ref, v_ref, rel_ref, out_ref, log_ref, between=lambda block: None):
    length = q_ref.shape[0]
    rows = min(FWD_ROWS, length)
    scale = HEAD ** (-0.5)
    rel = rel_ref[...]
    for start in range(0, length, rows):
        outs, logs = [], []
        for h in range(PAIR):
            lanes = slice(h * HEAD, (h + 1) * HEAD)
            query = q_ref[start : start + rows, lanes] * scale
            scores = nt(query, k_ref[:, lanes])
            scores = biased_scores(scores, nt(query, rel), start, rows, length)
            highest = jnp.max(scores, axis=1, keepdims=True)
            weights = jnp.exp(scores - highest)
            total = jnp.sum(weights, axis=1, keepdims=True)
            outs.append(nn(weights.astype(jnp.bfloat16), v_ref[:, lanes]) / total)
            logs.append(highest + jnp.log(total))
        out_ref[start : start + rows, :] = jnp.concatenate(outs, axis=1).astype(jnp.bfloat16)
        log_ref[start : start + rows, :] = jnp.concatenate(logs, axis=1)
        between(start // rows)


def attend_back_pair(
    q_ref, k_ref, v_ref, do_ref, log_ref, rel_ref, back_ref, mirror_ref, dq_ref, dk_ref, dv_ref, table_ref, dkt, dvt, q_turned, do_turned,
    between=lambda block: None,
):
    length = q_ref.shape[0]
    rows = min(BACK_ROWS, length)
    scale = HEAD ** (-0.5)
    q_turned[...] = (jnp.transpose(q_ref[...].astype(jnp.float32)) * scale).astype(jnp.bfloat16)
    do_turned[...] = jnp.transpose(do_ref[...].astype(jnp.float32)).astype(jnp.bfloat16)
    table_ref[...] = jnp.zeros((HEAD, LANES), jnp.float32)
    for start in range(0, length, rows):
        span = slice(start, start + rows)
        parts = []
        for h in range(PAIR):
            lanes = slice(h * HEAD, (h + 1) * HEAD)
            query = q_ref[span, lanes] * scale
            scores = nt(query, k_ref[:, lanes])
            scores = biased_scores(scores, nt(query, rel_ref[...]), start, rows, length)
            weights = jnp.exp(scores - log_ref[span, h : h + 1])
            low_weights = weights.astype(jnp.bfloat16)
            grads = nt(do_ref[span, lanes], v_ref[:, lanes])
            both = weights * grads
            delta = jnp.sum(both, axis=1, keepdims=True)
            score_grad = (both - weights * delta).astype(jnp.bfloat16)
            value_part = nn(do_turned[lanes, span], low_weights)
            key_part = nn(q_turned[lanes, span], score_grad)
            if start == 0:
                dvt[lanes, :] = value_part
                dkt[lanes, :] = key_part
            else:
                dvt[lanes, :] += value_part
                dkt[lanes, :] += key_part
            bucket = bucket_sums(score_grad.astype(jnp.float32), mirror_ref[...], start, rows, length)
            high = bucket.astype(jnp.bfloat16)
            rest = (bucket - high.astype(jnp.float32)).astype(jnp.bfloat16)
            parts.append((nn(score_grad, k_ref[:, lanes]) + nn(high, back_ref[...]) + nn(rest, back_ref[...])) * scale)
            table_ref[...] += nn(q_turned[lanes, span], high) + nn(q_turned[lanes, span], rest)
        dq_ref[span, :] = jnp.concatenate(parts, axis=1).astype(jnp.bfloat16)
        between(start // rows)
    dk_ref[...] = jnp.transpose(dkt[...]).astype(jnp.bfloat16)
    dv_ref[...] = jnp.transpose(dvt[...]).astype(jnp.bfloat16)


def attend_kernel(q_ref, k_ref, v_ref, rel_ref, out_ref, log_ref):
    attend_pair(q_ref.at[0], k_ref.at[0], v_ref.at[0], rel_ref, out_ref.at[0], log_ref.at[0, 0])


def attend_back_kernel(
    q_ref, k_ref, v_ref, do_ref, log_ref, rel_ref, back_ref, mirror_ref, dq_ref, dk_ref, dv_ref, table_ref, dkt, dvt, q_turned, do_turned
):
    attend_back_pair(
        q_ref.at[0], k_ref.at[0], v_ref.at[0], do_ref.at[0], log_ref.at[0, 0], rel_ref, back_ref, mirror_ref,
        dq_ref.at[0], dk_ref.at[0], dv_ref.at[0], table_ref.at[0, 0], dkt, dvt, q_turned, do_turned,
    )


def width_of(length):
    return min(BACK_ROWS, length) + 2 * LANES


def head_block(length):
    return pl.BlockSpec((1, length, PAIR * HEAD), lambda i, j: (i, 0, j))


def padded_table(rel_table):
    return jnp.pad(rel_table.astype(jnp.bfloat16), ((0, LANES - BUCKETS), (0, 0)))


def attend(query, key, value, rel_low):
    clips, length, width = query.shape
    pairs = width // (PAIR * HEAD)
    block = head_block(length)
    return pl.pallas_call(
        attend_kernel,
        grid=(clips, pairs),
        in_specs=[block, block, block, pl.BlockSpec((LANES, HEAD), lambda i, j: (0, 0))],
        out_specs=[block, pl.BlockSpec((1, 1, length, PAIR), lambda i, j: (i, j, 0, 0))],
        out_shape=[
            jax.ShapeDtypeStruct(query.shape, jnp.bfloat16),
            jax.ShapeDtypeStruct((clips, pairs, length, PAIR), jnp.float32),
        ],
        compiler_params=pltpu.CompilerParams(vmem_limit_bytes=48 << 20),
        cost_estimate=pl.CostEstimate(flops=4 * clips * width * length * length * 4, bytes_accessed=8 * query.size, transcendentals=clips * pairs * PAIR * length * length),
        name="attend",
    )(query, key, value, rel_low)


def attend_back(query, key, value, out_grad, logs, rel_low):
    clips, length, width = query.shape
    pairs = width // (PAIR * HEAD)
    block = head_block(length)
    shape = jax.ShapeDtypeStruct(query.shape, jnp.bfloat16)
    return pl.pallas_call(
        attend_back_kernel,
        grid=(clips, pairs),
        in_specs=[
            block, block, block, block,
            pl.BlockSpec((1, 1, length, PAIR), lambda i, j: (i, j, 0, 0)),
            pl.BlockSpec((LANES, HEAD), lambda i, j: (0, 0)),
            pl.BlockSpec((LANES, HEAD), lambda i, j: (0, 0)),
            pl.BlockSpec((width_of(length),) * 2, lambda i, j: (0, 0)),
        ],
        out_specs=[block, block, block, pl.BlockSpec((1, 1, HEAD, LANES), lambda i, j: (i, j, 0, 0))],
        out_shape=[shape, shape, shape, jax.ShapeDtypeStruct((clips, pairs, HEAD, LANES), jnp.float32)],
        scratch_shapes=[pltpu.VMEM((PAIR * HEAD, length), jnp.float32)] * 2 + [pltpu.VMEM((PAIR * HEAD, length), jnp.bfloat16)] * 2,
        compiler_params=pltpu.CompilerParams(vmem_limit_bytes=48 << 20),
        cost_estimate=pl.CostEstimate(flops=10 * clips * width * length * length * 4, bytes_accessed=14 * query.size, transcendentals=clips * pairs * PAIR * length * length),
        name="attend_back",
    )(query, key, value, out_grad, logs, rel_low, rel_low[::-1], mirror_of(width_of(length)))


def strip(index):
    return pl.ds(pl.multiple_of(index * LANES, LANES), LANES)


def attend_back_split_kernel(
    pairs, count, chunks, lines, do_ref, kept_ref, log_ref, rel_ref, back_ref, mirror_ref, *refs
):
    lefts, rights, small = refs[:count], refs[count : 2 * count], refs[2 * count]
    dp_ref, table_ref = refs[2 * count + 1 : 2 * count + 3]
    sums_refs, refs = refs[2 * count + 3 : 3 * count + 4], refs[3 * count + 4 :]
    grads, qkv, outs, dkt, dvt, q_turned, do_turned, own_sem, send_sem, recv_sem, kept_sem, out_sem, back_send, back_recv = refs[:14]
    me = Place()
    scatter = Scatter(me, lefts, rights, small, sums_refs[:count], sums_refs[count], chunks, lines, refs[14:])
    blocks = kept_ref.shape[2] // min(BACK_ROWS, kept_ref.shape[2])
    step = pl.program_id(0)
    segment = do_ref.shape[0]
    mine, theirs = pl.ds(me.x * segment, segment), pl.ds((1 - me.x) * segment, segment)

    def leaving(i):
        return Sent(do_ref.at[:, strip((1 - me.x) * pairs + i)], grads.at[i, mine, :], send_sem.at[i], recv_sem.at[i], me.across())

    def staying(i):
        return (
            pltpu.make_async_copy(do_ref.at[:, strip(me.x * pairs + i)], grads.at[i, mine, :], own_sem.at[i]),
            pltpu.make_async_copy(kept_ref.at[i], qkv.at[i], kept_sem.at[i]),
        )

    def returns(i, part):
        there = dp_ref.at[:, strip((2 * part + me.x) * pairs + i)]
        return (
            Sent(outs.at[i, part, theirs, :], there, back_send.at[i, part], back_recv.at[i, part], me.across()),
            pltpu.make_async_copy(outs.at[i, part, mine, :], there, out_sem.at[i, part]),
        )

    @pl.when(step == 0)
    def _():
        me.greet()
        for i in range(pairs):
            leaving(i).start()
            for copy in staying(i):
                copy.start()
        scatter.step(0)
        scatter.step(1)

    def between(block):
        for i in range(pairs):
            if 2 + i * blocks + block < scatter.steps:

                @pl.when(step == i)
                def _():
                    scatter.step(2 + i * blocks + block)

    leaving(step).wait_recv()
    for copy in staying(step):
        copy.wait()
    attend_back_pair(
        qkv.at[step, 0], qkv.at[step, 1], qkv.at[step, 2], grads.at[step], log_ref.at[0], rel_ref, back_ref, mirror_ref,
        outs.at[step, 0], outs.at[step, 1], outs.at[step, 2], table_ref.at[0], dkt, dvt, q_turned, do_turned, between,
    )
    for part in range(3):
        for copy in returns(step, part):
            copy.start()

    @pl.when(step == pairs - 1)
    def _():
        for number in range(2 + pairs * blocks, scatter.steps):
            scatter.step(number)
        scatter.finish()
        for i in range(pairs):
            leaving(i).wait_send()
            for part in range(3):
                sent, own = returns(i, part)
                sent.wait_send()
                sent.wait_recv()
                own.wait()


def attend_back_split(out_grad, kept, logs, rel_low, factors, small, identity):
    segment, width = out_grad.shape
    pairs, _, length, _ = kept.shape
    operands, more_specs, outs, outs_specs, scratch, chunks, lines = scatter_plan(factors, small, [(1, 6, 11)])
    dma, anywhere = pltpu.SemaphoreType.DMA, pl.BlockSpec(memory_space=pl.ANY)
    table = pl.BlockSpec((LANES, HEAD), lambda i: (0, 0))
    return pl.pallas_call(
        functools.partial(attend_back_split_kernel, pairs, len(factors), chunks, lines),
        grid=(pairs,),
        in_specs=[
            anywhere, anywhere, pl.BlockSpec((1, length, PAIR), lambda i: (i, 0, 0)), table, table,
            pl.BlockSpec((width_of(length),) * 2, lambda i: (0, 0), pipeline_mode=pl.Buffered(1)), *more_specs,
        ],
        out_specs=[anywhere, pl.BlockSpec((1, HEAD, LANES), lambda i: (i, 0, 0)), *outs_specs],
        out_shape=[
            jax.ShapeDtypeStruct((segment, 3 * width), jnp.bfloat16),
            jax.ShapeDtypeStruct((pairs, HEAD, LANES), jnp.float32),
            *outs,
        ],
        scratch_shapes=[
            pltpu.VMEM((pairs, length, LANES), jnp.bfloat16),
            pltpu.VMEM((pairs, 3, length, LANES), jnp.bfloat16),
            pltpu.VMEM((pairs, 3, length, LANES), jnp.bfloat16),
            pltpu.VMEM((LANES, length), jnp.float32),
            pltpu.VMEM((LANES, length), jnp.float32),
            pltpu.VMEM((LANES, length), jnp.bfloat16),
            pltpu.VMEM((LANES, length), jnp.bfloat16),
            dma((pairs,)), dma((pairs,)), dma((pairs,)), dma((pairs,)), dma((pairs, 3)), dma((pairs, 3)), dma((pairs, 3)),
            *scratch,
        ],
        compiler_params=pltpu.CompilerParams(collective_id=identity, has_side_effects=True, vmem_limit_bytes=62 << 20),
        name="attend_back_split",
    )(out_grad, kept, logs, rel_low, rel_low[::-1], mirror_of(width_of(length)), *operands)


CROSSING = [(24, 2, 3), (12, 1, 4), (1, 2, 3)]


def normed_rows(values, gain, shift):
    center = values - jnp.mean(values, axis=1, keepdims=True)
    spread = jnp.mean(center * center, axis=1, keepdims=True)
    return center * lax.rsqrt(spread + EPSILON) * gain + shift


def front_kernel(
    pairs, count, chunks, lines, tokens_ref, rel_ref, gains_ref, shifts_ref, hidden_bias_ref, model_bias_ref, *refs
):
    shards, refs = refs[:count], refs[count:]
    normed_ref, hidden_ref, active_ref, after_ref, attn_ref, out_ref, kept_ref, log_ref = refs[:8]
    wholes, refs = refs[8 : 8 + count], refs[8 + count :]
    (branch, projected, strips, blocks, qkv, outs, strip_sem, block_sem,
     own_sem, send_sem, recv_sem, kept_sem, out_sem, back_send, back_recv) = refs[:15]
    me = Place()
    gather = Gather(me, shards, wholes, chunks, lines, refs[15:])
    me.greet()
    segment, width = tokens_ref.shape
    low = jnp.bfloat16
    ROWS = 128

    def chunks_for(index):
        return [t for t, chunk in enumerate(chunks) if chunk[0] == index]

    def whole_by_now(t):
        gather.run(t + 3 * LAG + 1)
        gather.landed(t)

    def strip_copies(t):
        index, line, column, early = chunks[t]
        half = shards[index].shape[1] // 2
        return [
            Near(wholes[index].at[:, :, :, :, pl.ds(j * half + column, PIECE)], strips.at[t % 2, j], strip_sem.at[t % 2, j])
            for j in range(2)
        ]

    def load_strips(t):
        whole_by_now(t)
        for copy in strip_copies(t):
            copy.start()

    def strip_spans(t):
        index, line, column, early = chunks[t]
        for copy in strip_copies(t):
            copy.wait()
        for j in range(2):
            start = j * (shards[index].shape[1] // 2) + column
            yield slice(start, start + PIECE), strips[t % 2, j].reshape(width, PIECE)

    def widen(t):
        for span, weight in strip_spans(t):
            hidden = nn(normed_ref[...], weight) + hidden_bias_ref[0:1, span]
            hidden_ref[:, span] = hidden.astype(low)
            active_ref[:, span] = (hidden * jax.nn.sigmoid(hidden)).astype(low)

    def project(t):
        for span, weight in strip_spans(t):
            part = span.start // width
            value = nn(attn_ref[...], weight)
            if part != 1:
                value = value + model_bias_ref[part // 2 + 1 : part // 2 + 2, span.start % width : span.start % width + PIECE]
            projected[:, span] = value.astype(low)

    def in_turn(numbers, load, use):
        load(numbers[0])
        for former, latter in zip(numbers, numbers[1:] + [None]):
            if latter is not None:
                load(latter)
            use(former)

    gather.run(LAG)
    for start in range(0, segment, ROWS):
        rows = slice(start, start + ROWS)
        values = tokens_ref[rows, :].astype(jnp.float32)
        normed_ref[rows, :] = normed_rows(values, gains_ref[0:1, :], shifts_ref[0:1, :]).astype(low)
    in_turn(chunks_for(0), load_strips, widen)
    for t in chunks_for(1):
        whole_by_now(t)
    tall = wholes[1].shape[3]

    def block_copy(f):
        return Near(wholes[1].at[f // 4, f // 2 % 2, f % 2], blocks.at[f % 2], block_sem.at[f % 2])

    def narrow(f):
        block_copy(f).wait()
        value = nn(active_ref[:, f * tall : (f + 1) * tall], blocks[f % 2])
        if f == 0:
            branch[...] = value
        else:
            branch[...] += value
        if f % 4 == 3:
            gather.run(gather.number + 1)

    block_copy(0).start()
    for f in range(16):
        if f < 15:
            block_copy(f + 1).start()
        narrow(f)
    for start in range(0, segment, ROWS):
        rows = slice(start, start + ROWS)
        values = tokens_ref[rows, :].astype(jnp.float32) + 0.5 * (branch[rows, :] + model_bias_ref[0:1, :])
        after_ref[rows, :] = values
        attn_ref[rows, :] = normed_rows(values, gains_ref[1:2, :], shifts_ref[1:2, :]).astype(low)
    in_turn(chunks_for(2), load_strips, project)

    mine, theirs = pl.ds(me.x * segment, segment), pl.ds((1 - me.x) * segment, segment)

    def leaving(i):
        return [
            Sent(projected.at[:, strip((2 * part + 1 - me.x) * pairs + i)], qkv.at[i, part, mine, :], send_sem.at[i, part], recv_sem.at[i, part], me.across())
            for part in range(3)
        ]

    def staying(i):
        return [
            Near(projected.at[:, strip((2 * part + me.x) * pairs + i)], qkv.at[i, part, mine, :], own_sem.at[i, part])
            for part in range(3)
        ]

    def returns(i):
        there = out_ref.at[:, strip(me.x * pairs + i)]
        return (
            Sent(outs.at[i, theirs, :], there, back_send.at[i], back_recv.at[i], me.across()),
            Near(outs.at[i, mine, :], there, out_sem.at[i]),
            Near(qkv.at[i], kept_ref.at[i], kept_sem.at[i]),
        )

    for i in range(pairs):
        for copy in leaving(i) + staying(i):
            copy.start()
    gather.run(gather.number + 1)
    for i in range(pairs):
        for copy in leaving(i):
            copy.wait_recv()
        for copy in staying(i):
            copy.wait()

        def between(block):
            if block % 2 == 1:
                gather.run(gather.number + 1)

        attend_pair(qkv.at[i, 0], qkv.at[i, 1], qkv.at[i, 2], rel_ref, outs.at[i], log_ref.at[i], between)
        for copy in returns(i):
            copy.start()
    gather.run(gather.steps)
    gather.finish()
    for i in range(pairs):
        for copy in leaving(i):
            copy.wait_send()
        sent, own, kept = returns(i)
        sent.wait_send()
        sent.wait_recv()
        own.wait()
        kept.wait()


def front(tokens, rel_low, norm_gains, norm_biases, hidden_biases, model_biases, shards, identity):
    segment, width = tokens.shape
    hidden = shards[0].shape[1]
    length, pairs, count = 2 * segment, width // (2 * PAIR * HEAD), len(shards)
    wholes, chunks, lines = gather_plan(shards, CROSSING)
    dma, low = pltpu.SemaphoreType.DMA, jnp.bfloat16
    anywhere, near = pl.BlockSpec(memory_space=pl.ANY), pl.BlockSpec(memory_space=pltpu.VMEM)
    *kept, = pl.pallas_call(
        functools.partial(front_kernel, pairs, count, chunks, lines),
        in_specs=[near] * 6 + [anywhere] * count,
        out_specs=[near] * 5 + [anywhere] * 2 + [near] + [anywhere] * count,
        out_shape=[
            jax.ShapeDtypeStruct((segment, width), low),
            jax.ShapeDtypeStruct((segment, hidden), low),
            jax.ShapeDtypeStruct((segment, hidden), low),
            jax.ShapeDtypeStruct((segment, width), jnp.float32),
            jax.ShapeDtypeStruct((segment, width), low),
            jax.ShapeDtypeStruct((segment, width), low),
            jax.ShapeDtypeStruct((pairs, 3, length, LANES), low),
            jax.ShapeDtypeStruct((pairs, length, PAIR), jnp.float32),
            *wholes,
        ],
        scratch_shapes=[
            pltpu.VMEM((segment, width), jnp.float32),
            pltpu.VMEM((segment, 3 * width), low),
            pltpu.VMEM((2, 2, 4, 2, 2, lines, PIECE), low),
            pltpu.VMEM((2, hidden // 16, width), low),
            pltpu.VMEM((pairs, 3, length, LANES), low),
            pltpu.VMEM((pairs, length, LANES), low),
            dma((2, 2)), dma((2,)),
            dma((pairs, 3)), dma((pairs, 3)), dma((pairs, 3)), dma((pairs,)), dma((pairs,)), dma((pairs,)), dma((pairs,)),
            *Gather.scratch(len(chunks)),
        ],
        compiler_params=pltpu.CompilerParams(collective_id=identity, has_side_effects=True, vmem_limit_bytes=60 << 20),
        name="front",
    )(tokens, rel_low, norm_gains, norm_biases, hidden_biases, model_biases, *shards)
    return kept[:8], flat(kept[8:])


TAPS = 32
TILE = 128


def conv_kernel(wide_ref, taps_ref, out_ref, spread):
    length = out_ref.shape[1]
    spread[...] = wide_ref[0].astype(jnp.float32)
    for start in range(0, length, TILE):
        total = jnp.zeros((TILE, LANES), jnp.float32)
        for r in range(KERNEL):
            total = total + taps_ref[r : r + 1, :] * spread[start + r + 2 : start + r + 2 + TILE, :]
        out_ref[0, start : start + TILE, :] = total


def conv_back_kernel(grad_ref, wide_ref, taps_ref, value_ref, gate_ref, dvalue_ref, dgate_ref, kernel_ref, spread, grads, sums):
    length = value_ref.shape[0]
    spread[...] = wide_ref[0].astype(jnp.float32)
    grads[...] = grad_ref[0].astype(jnp.float32)

    @pl.when(pl.program_id(1) == 0)
    def _():
        sums[...] = jnp.zeros_like(sums)

    for start in range(0, length, TILE):
        own = grads[start : start + TILE, :]
        total = jnp.zeros((TILE, LANES), jnp.float32)
        for r in range(KERNEL):
            total = total + taps_ref[r : r + 1, :] * grads[start + KERNEL - 1 - r : start + KERNEL - 1 - r + TILE, :]
            both = own * spread[start + r + 2 : start + r + 2 + TILE, :]
            sums[r] += jnp.sum(both.reshape(TILE // 8, 8, LANES), axis=0)
        span = slice(start, start + TILE)
        opened = jax.nn.sigmoid(gate_ref[span, :])
        dvalue_ref[span, :] = (total * opened).astype(jnp.bfloat16)
        dgate_ref[span, :] = (total * value_ref[span, :] * (opened * (1.0 - opened))).astype(jnp.bfloat16)
    kernel_ref[...] = jnp.sum(sums[...], axis=1)


def padded_taps(dw_kernel):
    return jnp.pad(dw_kernel, ((0, TAPS - KERNEL), (0, 0)))


def depthwise(wide, dw_kernel):
    clips, lines, width = wide.shape
    length = lines - TAPS
    return pl.pallas_call(
        conv_kernel,
        grid=(width // LANES, clips),
        in_specs=[
            pl.BlockSpec((1, lines, LANES), lambda i, j: (j, 0, i)),
            pl.BlockSpec((TAPS, LANES), lambda i, j: (0, i)),
        ],
        out_specs=pl.BlockSpec((1, length, LANES), lambda i, j: (j, 0, i)),
        out_shape=jax.ShapeDtypeStruct((clips, length, width), jnp.float32),
        scratch_shapes=[pltpu.VMEM((lines, LANES), jnp.float32)],
        cost_estimate=pl.CostEstimate(flops=2 * KERNEL * clips * length * width, bytes_accessed=6 * clips * length * width, transcendentals=0),
        name="depthwise",
    )(wide, padded_taps(dw_kernel))


def depthwise_back(grad_wide, wide, dw_kernel, gate_input):
    clips, lines, width = wide.shape
    length, blocks = lines - TAPS, width // LANES
    tall = pl.BlockSpec((1, lines, LANES), lambda i, j: (j, 0, i))
    half = pl.BlockSpec((length, LANES), lambda i, j: (j, i))
    taps = pl.BlockSpec((TAPS, LANES), lambda i, j: (0, i))
    shape = jax.ShapeDtypeStruct((clips * length, width), jnp.bfloat16)
    dvalue, dgate, kernel_grad = pl.pallas_call(
        conv_back_kernel,
        grid=(blocks, clips),
        in_specs=[tall, tall, taps, half, pl.BlockSpec((length, LANES), lambda i, j: (j, blocks + i))],
        out_specs=[half, half, taps],
        out_shape=[shape, shape, jax.ShapeDtypeStruct((TAPS, width), jnp.float32)],
        scratch_shapes=[
            pltpu.VMEM((lines, LANES), jnp.float32),
            pltpu.VMEM((lines, LANES), jnp.float32),
            pltpu.VMEM((TAPS, 8, LANES), jnp.float32),
        ],
        cost_estimate=pl.CostEstimate(flops=4 * KERNEL * clips * length * width, bytes_accessed=16 * clips * length * width, transcendentals=clips * length * width),
        name="depthwise_back",
    )(grad_wide, wide, padded_taps(dw_kernel), gate_input, gate_input)
    return jnp.concatenate([dvalue, dgate], axis=1), kernel_grad[:KERNEL]


def feed_forward(values, norm_gain, norm_shift, weight_up, bias_up, weight_down, bias_down):
    normed = layer_norm(values, norm_gain, norm_shift).astype(jnp.bfloat16)
    hidden = product(normed, weight_up) + bias_up
    active = jax.nn.silu(hidden).astype(jnp.bfloat16)
    branch = product(active, weight_down) + bias_down
    return (branch, (normed, hidden, active))


def feed_backward(residual_grad, values, kept_parts, norm_gain, norm_shift, weight_up, weight_down):
    normed, hidden, active = kept_parts
    branch_grad = (0.5 * residual_grad).astype(jnp.bfloat16)
    down_bias_grad = jnp.sum(branch_grad.astype(jnp.float32), axis=0)
    active_grad = times_transposed(branch_grad, weight_down)
    silu_pull = jax.vjp(jax.nn.silu, hidden)[1]
    hidden_grad = silu_pull(active_grad)[0].astype(jnp.bfloat16)
    up_bias_grad = jnp.sum(hidden_grad.astype(jnp.float32), axis=0)
    normed_grad = times_transposed(hidden_grad, weight_up)
    norm_pull = jax.vjp(layer_norm, values, norm_gain, norm_shift)[1]
    values_grad, gain_grad, shift_grad = norm_pull(normed_grad)
    return (
        residual_grad + values_grad,
        (normed, hidden_grad),
        up_bias_grad,
        (active, branch_grad),
        down_bias_grad,
        gain_grad,
        shift_grad,
    )


def heads_of(projected, clip_count, segment, rel_low):
    parts = [
        lax.all_to_all(part.reshape(clip_count, segment, -1), "seq", split_axis=2, concat_axis=1, tiled=True)
        for part in jnp.split(projected, 3, axis=1)
    ]
    merged, log_totals = attend(*parts, rel_low)
    attn_seq = lax.all_to_all(merged, "seq", split_axis=1, concat_axis=2, tiled=True)
    return attn_seq.reshape(clip_count * segment, -1), parts, log_totals


def heads_back(out_grad, parts, log_totals, clip_count, segment, rel_low):
    merged = lax.all_to_all(
        out_grad.reshape(clip_count, segment, -1), "seq", split_axis=2, concat_axis=1, tiled=True
    )
    *grads, table_parts = attend_back(*parts, merged, log_totals, rel_low)
    grads = [
        lax.all_to_all(grad, "seq", split_axis=1, concat_axis=2, tiled=True).reshape(clip_count * segment, -1)
        for grad in grads
    ]
    return jnp.concatenate(grads, axis=1), jnp.sum(table_parts, axis=0)


def spread_sums(factors, small):
    sums = []
    for left, right in factors:
        part = lax.psum_scatter(contract_rows(left, right).astype(jnp.bfloat16), "seq", scatter_dimension=1, tiled=True)
        part = lax.psum_scatter(part, "fsdp", scatter_dimension=0, tiled=True)
        sums.append(part.astype(jnp.float32))
    return (*sums, lax.psum(small, ("seq", "fsdp")))


def stacked(rows):
    lines = jnp.concatenate([row.reshape(-1, rows[0].shape[-1]) for row in rows])
    return jnp.pad(lines, ((0, -lines.shape[0] % 8), (0, 0)))


def split_small_kernel(early, later, gains, firsts, lasts, hidden, model, others, taps, table):
    width = early.shape[1]
    rows = hidden.shape[1] // width
    gains[0:2, :], gains[2:6, :] = early[0:2, :], later[0:4, :]
    firsts[0:2, :], firsts[2:3, :] = early[2:4, :], later[4:5, :]
    lasts[...] = later[5:8, :]
    for k in range(rows):
        span = slice(k * width, (k + 1) * width)
        hidden[0:1, span], hidden[1:2, span] = early[4 + k : 5 + k, :], later[8 + k : 9 + k, :]
    at, then = 4 + rows, 8 + rows
    model[...] = early[at : at + 3, :]
    others[0:1, :], others[1:2, :] = early[at + 3 : at + 4, :], later[then : then + 1, :]
    taps[...] = later[then + 1 : then + 1 + KERNEL, :]
    for b in range(BUCKETS):
        row, lane = at + 4 + b * HEAD // width, b * HEAD % width
        table[b : b + 1, :] = early[row : row + 1, lane : lane + HEAD]


def split_small(early, later, hidden_width):
    width = early.shape[1]
    shapes = [(6, width), (3, width), (3, width), (2, hidden_width), (3, width), (2, width), (KERNEL, width), (BUCKETS, HEAD)]
    return pl.pallas_call(
        split_small_kernel,
        out_shape=[jax.ShapeDtypeStruct(shape, jnp.float32) for shape in shapes],
        name="split_small",
    )(early, later)


def body(
    tokens,
    cotangent,
    ffn1_up,
    ffn1_down,
    qkv_weight,
    out_weight,
    conv_in,
    conv_out,
    ffn2_up,
    ffn2_down,
    norm_gains,
    norm_biases,
    hidden_biases,
    model_biases,
    dw_kernel,
    rel_table,
):
    clip_count, segment, model_width = tokens.shape
    row_count = clip_count * segment
    rim_width = KERNEL - 1
    close = lax.axis_size("seq") == 2 and lax.axis_size("fsdp") == 16 and clip_count == 1
    low = jnp.bfloat16
    shards = [
        weight.astype(low)
        for weight in (ffn1_up, ffn1_down, qkv_weight, out_weight, conv_in, conv_out, ffn2_up, ffn2_down)
    ]
    rel_low = padded_table(rel_table)
    input_rows = tokens.reshape(row_count, model_width).astype(jnp.float32)
    if close:
        fronts, weights = front(
            tokens.reshape(row_count, model_width), rel_low, norm_gains, norm_biases, hidden_biases, model_biases, shards, 0
        )
        normed_one, hidden_one, active_one, after_one, normed_attn, attn_rows, kept_heads, log_totals = fronts
        kept_one = (normed_one, hidden_one.astype(jnp.float32), active_one)
    else:
        weights = [lax.all_gather(shard, "fsdp", axis=0, tiled=True) for shard in shards]
        branch_one, kept_one = feed_forward(
            input_rows,
            norm_gains[0],
            norm_biases[0],
            weights[0],
            hidden_biases[0],
            weights[1],
            model_biases[0],
        )
        after_one = input_rows + 0.5 * branch_one
        normed_attn = layer_norm(after_one, norm_gains[1], norm_biases[1]).astype(low)
        project_bias = jnp.concatenate([model_biases[1], jnp.zeros_like(model_biases[1]), model_biases[2]])
        projected = (product(normed_attn, weights[2]) + project_bias).astype(low)
        attn_rows, kept_heads, log_totals = heads_of(projected, clip_count, segment, rel_low)
    up_one, down_one, qkv_full, out_full, conv_first, conv_second, up_two, down_two = weights
    after_two = after_one + product(attn_rows, out_full) + model_biases[3]
    normed_conv = layer_norm(after_two, norm_gains[2], norm_biases[2]).astype(low)
    gate_input = product(normed_conv, conv_first)
    glu_out = glu_function(gate_input).astype(low).reshape(clip_count, segment, model_width)
    glu_before = passed_along(glu_out[:, segment - rim_width :], "seq", 1)
    margin = jnp.zeros((clip_count, TAPS - rim_width, model_width), low)
    glu_wide = jnp.concatenate([margin, glu_before, glu_out], axis=1)
    mixed_flat = depthwise(glu_wide, dw_kernel).reshape(row_count, model_width)
    swished = conv_tail(mixed_flat, norm_gains[3], norm_biases[3]).astype(low)
    after_three = after_two + product(swished, conv_second)
    branch_two, kept_two = feed_forward(
        after_three,
        norm_gains[4],
        norm_biases[4],
        up_two,
        hidden_biases[1],
        down_two,
        model_biases[4],
    )
    after_four = after_three + 0.5 * branch_two
    final_rows, final_pull = jax.vjp(layer_norm, after_four, norm_gains[5], norm_biases[5])
    output = final_rows.astype(low).reshape(clip_count, segment, model_width)
    grad_four, gain_five, shift_five = final_pull(
        cotangent.reshape(row_count, model_width).astype(jnp.float32)
    )
    grad_three, up_two_factors, up_two_bias, down_two_factors, down_two_bias, gain_four, shift_four = (
        feed_backward(
            grad_four, after_three, kept_two, norm_gains[4], norm_biases[4], up_two, down_two
        )
    )
    conv_grad = grad_three.astype(low)
    swished_grad = times_transposed(conv_grad, conv_second)
    tail_pull = jax.vjp(conv_tail, mixed_flat, norm_gains[3], norm_biases[3])[1]
    mixed_grad, gain_three, shift_three = tail_pull(swished_grad)
    mixed_low = mixed_grad.astype(low).reshape(clip_count, segment, model_width)
    mixed_after = passed_along(mixed_low[:, 0:rim_width], "seq", -1)
    mixed_wide = jnp.concatenate([mixed_low, mixed_after, margin], axis=1)
    gate_grad, kernel_grad = depthwise_back(mixed_wide, glu_wide, dw_kernel, gate_input)
    conv_norm_pull = jax.vjp(layer_norm, after_two, norm_gains[2], norm_biases[2])[1]
    values_grad, gain_two, shift_two = conv_norm_pull(times_transposed(gate_grad, conv_first))
    grad_two = grad_three + values_grad
    later_small = stacked(
        [gain_two, gain_three, gain_four, gain_five, shift_two, shift_three, shift_four, shift_five]
        + [up_two_bias, down_two_bias, kernel_grad]
    )
    later_factors = [down_two_factors, up_two_factors, (swished, conv_grad), (normed_conv, gate_grad)]
    attn_grad = grad_two.astype(low)
    out_bias_grad = jnp.sum(attn_grad.astype(jnp.float32), axis=0)
    merged_grad = times_transposed(attn_grad, out_full).astype(low)
    if close:
        projected_grad, table_parts, *later_sums = attend_back_split(
            merged_grad, kept_heads, log_totals, rel_low, later_factors, later_small, 3
        )
    else:
        projected_grad, table_parts = heads_back(
            merged_grad, kept_heads, log_totals, clip_count, segment, rel_low
        )
        later_sums = spread_sums(later_factors, later_small)
    down_two_sum, up_two_sum, conv_second_sum, conv_first_sum, later_sum = later_sums
    table_grad = jnp.sum(table_parts, axis=0).T[::-1][:BUCKETS]
    query_bias_grad = jnp.sum(projected_grad[:, :model_width].astype(jnp.float32), axis=0)
    value_bias_grad = jnp.sum(projected_grad[:, 2 * model_width :].astype(jnp.float32), axis=0)
    attn_norm_pull = jax.vjp(layer_norm, after_one, norm_gains[1], norm_biases[1])[1]
    values_grad, gain_one, shift_one = attn_norm_pull(times_transposed(projected_grad, qkv_full))
    grad_one = grad_two + values_grad
    grad_zero, up_one_factors, up_one_bias, down_one_factors, down_one_bias, gain_zero, shift_zero = (
        feed_backward(
            grad_one, input_rows, kept_one, norm_gains[0], norm_biases[0], up_one, down_one
        )
    )
    input_grad = grad_zero.astype(low).reshape(clip_count, segment, model_width)
    table_flat = table_grad.reshape(-1)
    table_rows = jnp.pad(table_flat, (0, -table_flat.size % model_width)).reshape(-1, model_width)
    early_small = stacked(
        [gain_zero, gain_one, shift_zero, shift_one, up_one_bias]
        + [down_one_bias, query_bias_grad, value_bias_grad, out_bias_grad, table_rows]
    )
    sums_of = partial(scatter_sums, identity=4) if close else spread_sums
    up_one_sum, down_one_sum, qkv_sum, out_sum, early_sum = sums_of(
        [up_one_factors, down_one_factors, (normed_attn, projected_grad), (attn_rows, attn_grad)],
        early_small,
    )
    return (
        output,
        input_grad,
        up_one_sum,
        down_one_sum,
        qkv_sum,
        out_sum,
        conv_first_sum,
        conv_second_sum,
        up_two_sum,
        down_two_sum,
        *split_small(early_sum, later_sum, up_one_bias.size),
    )


def solution(mesh):
    in_specs = (
        P("fsdp", "seq", None),
        P("fsdp", "seq", None),
        P("fsdp", None),
        P("fsdp", None),
        P("fsdp", None),
        P("fsdp", None),
        P("fsdp", None),
        P("fsdp", None),
        P("fsdp", None),
        P("fsdp", None),
        P(),
        P(),
        P(),
        P(),
        P(),
        P(),
    )
    out_specs = (
        P("fsdp", "seq", None),
        P("fsdp", "seq", None),
        P("fsdp", "seq"),
        P("fsdp", "seq"),
        P("fsdp", "seq"),
        P("fsdp", "seq"),
        P("fsdp", "seq"),
        P("fsdp", "seq"),
        P("fsdp", "seq"),
        P("fsdp", "seq"),
        P(),
        P(),
        P(),
        P(),
        P(),
        P(),
        P(),
        P(),
    )
    return jax.shard_map(body, mesh=mesh, in_specs=in_specs, out_specs=out_specs, check_vma=False)
```
